256 devices in a mesh: shot: 32 (over y_hi, z, core), rcv: 8 (over x, y_lo).
Axes of the slice: x: 4, y: 4 (y_hi: 2, y_lo: 2; y = y_hi * 2 + y_lo), z: 8, core: 2. Of those that a mesh axis runs over, the one named last changes fastest.
Arguments:
- record: bfloat16 [768, 262144], P('rcv', 'shot'), may hold values from -6 to 6
- shot_fire_samples: int32 [1024], P('shot'), may hold values from 0 to 262143, as said below
Outputs:
- psf_gram: float32 [2, 4, 768, 768], P(None, None, 'rcv', 'shot')
The draws below stay inside these ranges and needn't reach their ends.
Inputs may be any that keep to these rules, and one draw needn't show every extreme that they name: `shot_fire_samples`: shot s fires at a sample from s * 256 to s * 256 + 255.
All inputs are finite; a program needn't handle non-finite values.
Results may differ from the reference program's by a relative error of at most 0.0025.
Values may be sent and summed in bfloat16 or wider, within the bound.
No kernel may reach another device: no remote copies, remote signals or barrier semaphores. Data moves between devices by JAX's collectives and lax.ppermute only.
A program may use at most 64 MiB of HBM per device.

```python
import math
import jax
import jax.numpy as jnp
from jax import lax

R = 768
WIN = 2048
F = 4
SPACING = 256
SHOTS_PER_UNIT = 32
SHOTS = 1024
NT = 262144
N_SHOT = 32


def draw_shot_fire_samples(key, part):
    jitter = jax.random.randint(jax.random.fold_in(key, 7), (SHOTS,), 0, SPACING)
    return (jnp.arange(SHOTS, dtype=jnp.int32) * SPACING + jitter).astype(jnp.int32)


def shard_levels(key, shape, split, least, top_value):
    level, own = 1.0, jax.random.fold_in(key, 6)
    for dim, blocks in split:
        steps = jnp.exp(jax.random.uniform(jax.random.fold_in(own, dim), (blocks,), jnp.float32, least / len(split), top_value / len(split)))
        level = level * jnp.repeat(steps, shape[dim] // blocks).reshape([-1 if axis == dim else 1 for axis in range(len(shape))])
    return level


def normal_values(stream_key, shape, deviation, limit, split=(), kind=jnp.bfloat16):
    drawn = jax.random.normal(stream_key, shape, jnp.float32) * deviation
    if len(split) > 0:
        drawn = shard_levels(stream_key, shape, split, -0.22, 0.18) * drawn
    return jnp.clip(drawn, min=-limit, max=limit).astype(kind)


def setup_inputs(seed: int = 0) -> dict:
    arg_keys = jax.random.split(jax.random.key(seed), 3)
    record = normal_values(arg_keys[0], (R, NT), 1.0, 6.0, ((0, 8), (1, 32)))
    shot_fire_samples = draw_shot_fire_samples(jax.random.fold_in(arg_keys[2], 71), 0)
    return {"record": record, "shot_fire_samples": shot_fire_samples}


freq_bins = (24, 40, 56, 80)

def dft_table(window_len):
    lag_index = jnp.arange(window_len, dtype=jnp.int32)
    bin_list = jnp.array(freq_bins, dtype=jnp.int32)
    turn_count = lag_index[:, None] * bin_list[None, :] % window_len
    phase_angle = 2.0 * math.pi / window_len * turn_count.astype(jnp.float32)
    dft_rows = jnp.concatenate([jnp.cos(phase_angle), -jnp.sin(phase_angle)], axis=1) / math.sqrt(window_len)
    return dft_rows.astype(jnp.bfloat16)

def gram_terms(left, right):
    nfreq = len(freq_bins)
    left_re = left[:, :nfreq, :].astype(jnp.float32)
    left_im = left[:, nfreq:, :].astype(jnp.float32)
    right_re = right[:, :nfreq, :].astype(jnp.float32)
    right_im = right[:, nfreq:, :].astype(jnp.float32)
    gram_real = jnp.einsum('sfr,sfq->frq', left_re, right_re) + jnp.einsum('sfr,sfq->frq', left_im, right_im)
    gram_imag = jnp.einsum('sfr,sfq->frq', left_re, right_im) - jnp.einsum('sfr,sfq->frq', left_im, right_re)
    return jnp.stack([gram_real, gram_imag], axis=0)

def reference(record, shot_fire_samples):
    padded = jnp.concatenate([record, jnp.zeros((R, WIN), record.dtype)], axis=1)
    dft_rows = dft_table(WIN)

    def spectra_block(block_times):

        def cut_window(begin_at):
            return lax.dynamic_slice_in_dim(padded, begin_at.astype(jnp.int32), WIN, 1)
        windows = jax.vmap(cut_window)(block_times)
        flat = jnp.dot(windows.reshape(-1, WIN), dft_rows, preferred_element_type=jnp.float32)
        return flat.reshape(SHOTS_PER_UNIT, R, 2 * F).transpose(0, 2, 1).astype(jnp.bfloat16)
    trace_spectra = lax.map(spectra_block, shot_fire_samples.reshape(N_SHOT, SHOTS_PER_UNIT))
    trace_spectra = trace_spectra.reshape(SHOTS, 2 * F, R)
    return gram_terms(trace_spectra, trace_spectra) / SHOTS
```

```python
import math

import jax
import jax.numpy as jnp
import numpy as np
from jax import lax
from jax.experimental import pallas as pl
from jax.experimental.pallas import tpu as pltpu
from jax.sharding import PartitionSpec as P

import ml_dtypes

WIN = 2048
SPACING = 256
PAIR = 2 * SPACING
SPAN = WIN + PAIR
FREQ_BINS = (24, 40, 56, 80)
NF = len(FREQ_BINS)
ROWS = 2 * NF

SHOT_DEVICES = 32
RCV_DEVICES = 8
QUARTERS = 4


def dft_master():
    turns = np.arange(WIN)[None, :] * np.array(FREQ_BINS)[:, None] % WIN
    angle = 2.0 * math.pi / WIN * turns
    rows = np.concatenate([np.cos(angle), -np.sin(angle)], axis=0) / math.sqrt(WIN)
    rows = rows.astype(np.float32).astype(ml_dtypes.bfloat16).astype(np.float32)
    return np.concatenate([rows, np.zeros((ROWS, SPAN - WIN), np.float32)], axis=1)


def send(block, to):
    route = []
    for shot in range(SHOT_DEVICES):
        for rcv in range(RCV_DEVICES):
            target = to(shot >> 3, (shot >> 2) & 1, shot & 3, rcv >> 1, rcv & 1)
            if target is not None:
                e, z1, k, x, yl = target
                route.append((shot * RCV_DEVICES + rcv, (e << 3 | z1 << 2 | k) * RCV_DEVICES + (x << 1 | yl)))
    return lax.ppermute(block, ("shot", "rcv"), route)


def shot_index():
    return lax.axis_index("shot")


def vmem(count):
    return [pl.BlockSpec(memory_space=pltpu.VMEM)] * count


def own_kernel(fire, table, record, total, tables, scratch):
    pairs = total.shape[0] // (2 * ROWS)
    reach = SPAN // PAIR
    master = table[...]
    for p in range(pairs):
        first = pltpu.roll(master, fire[2 * p] & (SPACING - 1), 1)
        second = pltpu.roll(master, (fire[2 * p + 1] & (SPACING - 1)) + SPACING, 1)
        scratch[p] = jnp.concatenate([first, second], axis=0).astype(jnp.bfloat16)
    total[...] = jnp.zeros_like(total)
    for u in range(pairs):
        low = max(0, u - reach + 1)
        left = jnp.concatenate(
            [scratch[p, :, PAIR * (u - p) : PAIR * (u - p + 1)] for p in range(low, u + 1)], axis=0
        )
        part = lax.dot_general(
            left, record[:, PAIR * u : PAIR * (u + 1)], (((1,), (1,)), ((), ())), preferred_element_type=jnp.float32
        )
        rows = slice(2 * ROWS * low, 2 * ROWS * (u + 1))
        total[rows, :] += part
    for p in range(reach - 1):
        tables[p] = scratch[pairs - reach + 1 + p]


def rim_kernel(total, tables, rim, out, scratch):
    pairs = total.shape[0] // (2 * ROWS)
    reach = SPAN // PAIR
    scratch[...] = total[...]
    for v in range(reach - 1):
        u = pairs + v
        low = u - reach + 1
        left = jnp.concatenate(
            [tables[p - (pairs - reach + 1), :, PAIR * (u - p) : PAIR * (u - p + 1)] for p in range(low, pairs)], axis=0
        )
        part = lax.dot_general(
            left, rim[:, PAIR * v : PAIR * (v + 1)], (((1,), (1,)), ((), ())), preferred_element_type=jnp.float32
        )
        scratch[2 * ROWS * low :, :] += part
    shots = 2 * pairs
    ordered = jnp.concatenate([scratch[pl.ds(c, shots, stride=ROWS), :] for c in range(ROWS)], axis=0)
    turned = ordered.T
    count = out.shape[1]
    for k in range(QUARTERS):
        out[k] = turned[count * k : count * (k + 1), :].astype(out.dtype)


def collect_kernel(y0, y1, y2, y3, gathered, quarter):
    k = shot_index() & 3
    for m, y in enumerate((y0, y1, y2, y3)):
        gathered[k ^ m] = y[...]
        quarter[k ^ m] = y[k]


def choose_kernel(own, ring, cross, out):
    straight = ((shot_index() >> 2) & 1) == (lax.axis_index("rcv") & 1)

    @pl.when(straight)
    def _():
        out[0] = own[...]

    @pl.when(jnp.logical_not(straight))
    def _():
        out[0] = cross[...]

    out[1] = ring[...]


def gram_kernel(scale, here, there, q0, q1, q2, q3, p0, p1, p2, p3, right, total):
    shot, rcv = shot_index(), lax.axis_index("rcv")
    e, x = shot >> 3, rcv >> 1
    swapped = ((shot >> 2) & 1) ^ (rcv & 1)
    count = q0.shape[2]
    lanes = q0.shape[3]
    half = lanes // 2
    span = QUARTERS * count
    for slot, block in ((swapped, here), (1 - swapped, there)):
        for k in range(QUARTERS):
            z = block[k].astype(jnp.float32).reshape(span, lanes)
            w = jnp.concatenate([-z[:, half:], z[:, :half]], axis=1)
            right[slot, k] = jnp.concatenate([z, w], axis=0).astype(jnp.bfloat16)
    per = half // NF
    lane = lax.broadcasted_iota(jnp.int32, (count, lanes), 1) % half // per
    for t, q in enumerate((q0, q1, q2, q3)):
        acc = jnp.zeros((NF * count, 2 * span), jnp.float32)
        for slot in range(2):
            for k in range(QUARTERS):
                rows = q[slot, k].astype(jnp.float32)
                left = jnp.concatenate([jnp.where(lane == f, rows, 0.0) for f in range(NF)], axis=0)
                acc = acc + lax.dot_general(
                    left.astype(jnp.bfloat16),
                    right[slot, k],
                    (((1,), (1,)), ((), ())),
                    preferred_element_type=jnp.float32,
                )
        m = (x + t - e) & 3
        total[m, : NF * count, :] = acc[:, :span] * scale
        total[m, NF * count :, :] = acc[:, span:] * scale
    for m, out in enumerate((p0, p1, p2, p3)):
        out[...] = total[m].astype(out.dtype)


def per_device(record, shot_fire_samples):
    receivers, samples = record.shape
    shots = shot_fire_samples.shape[0]
    pairs = shots // 2
    reach = SPAN // PAIR
    lanes = ROWS * shots
    count = receivers // QUARTERS
    bf16, f32 = jnp.bfloat16, jnp.float32
    shape = jax.ShapeDtypeStruct

    def before(e, z1, k, x, yl):
        shot = (e << 3 | z1 << 2 | k) - 1
        return None if shot < 0 else (shot >> 3, (shot >> 2) & 1, shot & 3, x, yl)

    rim = send(record[:, :WIN], before)
    total, tables = pl.pallas_call(
        own_kernel,
        out_shape=(shape((lanes, receivers), f32), shape((reach - 1, 2 * ROWS, SPAN), bf16)),
        in_specs=[pl.BlockSpec(memory_space=pltpu.SMEM)] + vmem(2),
        out_specs=tuple(vmem(2)),
        scratch_shapes=[pltpu.VMEM((pairs, 2 * ROWS, SPAN), bf16)],
        cost_estimate=pl.CostEstimate(
            flops=2 * lanes * receivers * SPAN, bytes_accessed=2 * receivers * samples, transcendentals=0
        ),
        name="own_spectra",
    )(shot_fire_samples, jnp.asarray(dft_master()), record)
    y0 = pl.pallas_call(
        rim_kernel,
        out_shape=shape((QUARTERS, count, lanes), bf16),
        in_specs=vmem(3),
        out_specs=vmem(1)[0],
        scratch_shapes=[pltpu.VMEM((lanes, receivers), f32)],
        name="rim_spectra",
    )(total, tables, rim)

    ys = [send(y0, lambda e, z1, k, x, yl, m=m: (e, z1, k ^ m, x, yl)) for m in (1, 2, 3)]
    here, own = pl.pallas_call(
        collect_kernel,
        out_shape=(shape((QUARTERS, QUARTERS, count, lanes), bf16), shape((QUARTERS, count, lanes), bf16)),
        in_specs=vmem(4),
        out_specs=tuple(vmem(2)),
        name="collect",
    )(y0, *ys)

    turn = {(1, 0): (0, 0), (0, 0): (0, 1), (0, 1): (1, 1), (1, 1): (1, 0)}
    ring = send(own, lambda e, z1, k, x, yl: (e, turn[z1, yl][0], k, x, turn[z1, yl][1]))
    cross = send(own, lambda e, z1, k, x, yl: (e, yl, k, x, z1) if z1 != yl else None)
    there = send(here, lambda e, z1, k, x, yl: (e, 1 - z1, k, x, yl))
    q0 = pl.pallas_call(
        choose_kernel,
        out_shape=shape((2, QUARTERS, count, lanes), bf16),
        in_specs=vmem(3),
        out_specs=vmem(1)[0],
        name="choose",
    )(own, ring, cross)
    qs = [send(q0, lambda e, z1, k, x, yl, t=t: (e, z1, k, (x - t) & 3, yl)) for t in (1, 3, 2)]
    q1, q3, q2 = qs

    total_shots = shots * lax.axis_size("shot")
    rows = 2 * NF * count
    p0, p1, p2, p3 = pl.pallas_call(
        lambda *refs: gram_kernel(1.0 / total_shots, *refs),
        out_shape=(shape((rows, receivers), f32),) + (shape((rows, receivers), bf16),) * 3,
        in_specs=vmem(6),
        out_specs=tuple(vmem(4)),
        scratch_shapes=[
            pltpu.VMEM((2, QUARTERS, 2 * receivers, lanes), bf16),
            pltpu.VMEM((QUARTERS, rows, receivers), f32),
        ],
        name="gram",
    )(here, there, q0, q1, q2, q3)
    sums = p0
    for m, p in ((1, p1), (2, p2), (3, p3)):
        sums = sums + send(p, lambda e, z1, k, x, yl, m=m: ((e + m) & 3, z1, k, x, yl)).astype(f32)
    return sums.reshape(2, NF, count, receivers).transpose(0, 1, 3, 2)


def solution(mesh):
    return jax.shard_map(
        per_device,
        mesh=mesh,
        in_specs=(P("rcv", "shot"), P("shot")),
        out_specs=P(None, None, "rcv", "shot"),
        check_vma=False,
    )
```

```python
import math

import jax
import jax.numpy as jnp
import numpy as np
from jax import lax
from jax.experimental import pallas as pl
from jax.experimental.pallas import tpu as pltpu
from jax.sharding import PartitionSpec as P

import ml_dtypes

WIN = 2048
SPACING = 256
PAIR = 2 * SPACING
SPAN = WIN + PAIR
FREQ_BINS = (24, 40, 56, 80)
NF = len(FREQ_BINS)
ROWS = 2 * NF

SHOT_DEVICES = 32
RCV_DEVICES = 8
QUARTERS = 4


def dft_master():
    turns = np.arange(WIN)[None, :] * np.array(FREQ_BINS)[:, None] % WIN
    angle = 2.0 * math.pi / WIN * turns
    rows = np.concatenate([np.cos(angle), -np.sin(angle)], axis=0) / math.sqrt(WIN)
    rows = rows.astype(np.float32).astype(ml_dtypes.bfloat16).astype(np.float32)
    return np.concatenate([rows, np.zeros((ROWS, SPAN - WIN), np.float32)], axis=1)


def send(block, to):
    route = []
    for shot in range(SHOT_DEVICES):
        for rcv in range(RCV_DEVICES):
            target = to(shot >> 3, (shot >> 2) & 1, shot & 3, rcv >> 1, rcv & 1)
            if target is not None:
                e, z1, k, x, yl = target
                route.append((shot * RCV_DEVICES + rcv, (e << 3 | z1 << 2 | k) * RCV_DEVICES + (x << 1 | yl)))
    return lax.ppermute(block, ("shot", "rcv"), route)


def shot_index():
    return lax.axis_index("shot")


def vmem(count):
    return [pl.BlockSpec(memory_space=pltpu.VMEM)] * count


def pair_tables(fire, table, p):
    first = pltpu.roll(table, fire[2 * p] & (SPACING - 1), 1)
    second = pltpu.roll(table, (fire[2 * p + 1] & (SPACING - 1)) + SPACING, 1)
    return jnp.concatenate([first, second], axis=0).astype(jnp.bfloat16)


def add_products(total, tables, record, blocks, pairs, first_row):
    reach = SPAN // PAIR
    for column, u in blocks:
        low, high = max(0, u - reach + 1), min(u, pairs - 1)
        left = jnp.concatenate(
            [tables[p - first_row, :, PAIR * (u - p) : PAIR * (u - p + 1)] for p in range(low, high + 1)], axis=0
        )
        part = lax.dot_general(
            left,
            record[:, PAIR * column : PAIR * (column + 1)],
            (((1,), (1,)), ((), ())),
            preferred_element_type=jnp.float32,
        )
        total[2 * ROWS * (low - first_row) : 2 * ROWS * (high + 1 - first_row), :] += part


def own_kernel(fire, table, record, total, tables):
    pairs = total.shape[0] // (2 * ROWS)
    master = table[...]
    for p in range(pairs):
        tables[p] = pair_tables(fire, master, p)
    total[...] = jnp.zeros_like(total)
    add_products(total, tables, record, [(u, u) for u in range(pairs)], pairs, 0)


def next_kernel(fire, table, record, total, tables):
    pairs = fire.shape[0] // 2
    reach = SPAN // PAIR
    first_row = pairs - reach + 1
    master = table[...]
    for p in range(first_row, pairs):
        tables[p - first_row] = pair_tables(fire, master, p)
    total[...] = jnp.zeros_like(total)
    add_products(total, tables, record, [(v, pairs + v) for v in range(reach - 1)], pairs, first_row)


def finish_kernel(total, late, out, scratch):
    lanes = total.shape[0]
    split = lanes - late.shape[0]
    scratch[:split, :] = total[:split, :]
    scratch[split:, :] = total[split:, :] + late[...]
    ordered = jnp.concatenate([scratch[pl.ds(c, lanes // ROWS, stride=ROWS), :] for c in range(ROWS)], axis=0)
    turned = ordered.T
    count = out.shape[1]
    for k in range(QUARTERS):
        out[k] = turned[count * k : count * (k + 1), :].astype(out.dtype)


def collect_kernel(y0, y1, y2, y3, gathered, quarter):
    k = shot_index() & 3
    for m, y in enumerate((y0, y1, y2, y3)):
        gathered[k ^ m] = y[...]
        quarter[k ^ m] = y[k]


def choose_kernel(own, ring, cross, out):
    straight = ((shot_index() >> 2) & 1) == (lax.axis_index("rcv") & 1)

    @pl.when(straight)
    def _():
        out[0] = own[...]

    @pl.when(jnp.logical_not(straight))
    def _():
        out[0] = cross[...]

    out[1] = ring[...]


def gram_kernel(scale, here, there, q0, q1, q2, q3, p0, p1, p2, p3, right, total):
    shot, rcv = shot_index(), lax.axis_index("rcv")
    e, x = shot >> 3, rcv >> 1
    swapped = ((shot >> 2) & 1) ^ (rcv & 1)
    count = q0.shape[2]
    lanes = q0.shape[3]
    half = lanes // 2
    span = QUARTERS * count
    for slot, block in ((swapped, here), (1 - swapped, there)):
        for k in range(QUARTERS):
            z = block[k].astype(jnp.float32).reshape(span, lanes)
            w = jnp.concatenate([-z[:, half:], z[:, :half]], axis=1)
            right[slot, k] = jnp.concatenate([z, w], axis=0).astype(jnp.bfloat16)
    per = half // NF
    lane = lax.broadcasted_iota(jnp.int32, (count, lanes), 1) % half // per
    for t, q in enumerate((q0, q1, q2, q3)):
        acc = jnp.zeros((NF * count, 2 * span), jnp.float32)
        for slot in range(2):
            for k in range(QUARTERS):
                rows = q[slot, k].astype(jnp.float32)
                left = jnp.concatenate([jnp.where(lane == f, rows, 0.0) for f in range(NF)], axis=0)
                acc = acc + lax.dot_general(
                    left.astype(jnp.bfloat16),
                    right[slot, k],
                    (((1,), (1,)), ((), ())),
                    preferred_element_type=jnp.float32,
                )
        m = (x + t - e) & 3
        total[m, : NF * count, :] = acc[:, :span] * scale
        total[m, NF * count :, :] = acc[:, span:] * scale
    for m, out in enumerate((p0, p1, p2, p3)):
        out[...] = total[m].astype(out.dtype)


def per_device(record, shot_fire_samples):
    receivers, samples = record.shape
    shots = shot_fire_samples.shape[0]
    pairs = shots // 2
    reach = SPAN // PAIR
    lanes = ROWS * shots
    count = receivers // QUARTERS
    bf16, f32 = jnp.bfloat16, jnp.float32
    shape = jax.ShapeDtypeStruct

    def neighbour(step):
        def to(e, z1, k, x, yl):
            shot = (e << 3 | z1 << 2 | k) + step
            return (shot >> 3, (shot >> 2) & 1, shot & 3, x, yl) if 0 <= shot < SHOT_DEVICES else None

        return to

    table = jnp.asarray(dft_master())
    smem = pl.BlockSpec(memory_space=pltpu.SMEM)
    fire_before = send(shot_fire_samples, neighbour(1))
    total = pl.pallas_call(
        own_kernel,
        out_shape=shape((lanes, receivers), f32),
        in_specs=[smem] + vmem(2),
        out_specs=vmem(1)[0],
        scratch_shapes=[pltpu.VMEM((pairs, 2 * ROWS, SPAN), bf16)],
        cost_estimate=pl.CostEstimate(
            flops=2 * lanes * receivers * SPAN, bytes_accessed=2 * receivers * samples, transcendentals=0
        ),
        compiler_params=pltpu.CompilerParams(vmem_limit_bytes=12 << 20),
        name="own_spectra",
    )(shot_fire_samples, table, record)
    late = pl.pallas_call(
        next_kernel,
        grid=(1,),
        out_shape=shape((2 * ROWS * (reach - 1), receivers), f32),
        in_specs=[
            smem,
            pl.BlockSpec(table.shape, lambda i: (0, 0)),
            pl.BlockSpec((receivers, WIN), lambda i: (0, 0)),
        ],
        out_specs=pl.BlockSpec((2 * ROWS * (reach - 1), receivers), lambda i: (0, 0)),
        scratch_shapes=[pltpu.VMEM((reach - 1, 2 * ROWS, SPAN), bf16)],
        compiler_params=pltpu.CompilerParams(vmem_limit_bytes=6 << 20),
        name="next_spectra",
    )(fire_before, table, record)
    late = send(late, neighbour(-1))
    y0 = pl.pallas_call(
        finish_kernel,
        out_shape=shape((QUARTERS, count, lanes), bf16),
        in_specs=vmem(2),
        out_specs=vmem(1)[0],
        scratch_shapes=[pltpu.VMEM((lanes, receivers), f32)],
        compiler_params=pltpu.CompilerParams(vmem_limit_bytes=4 << 20),
        name="finish_spectra",
    )(total, late)

    ys = [send(y0, lambda e, z1, k, x, yl, m=m: (e, z1, k ^ m, x, yl)) for m in (1, 2, 3)]
    here, own = pl.pallas_call(
        collect_kernel,
        out_shape=(shape((QUARTERS, QUARTERS, count, lanes), bf16), shape((QUARTERS, count, lanes), bf16)),
        in_specs=vmem(4),
        out_specs=tuple(vmem(2)),
        compiler_params=pltpu.CompilerParams(vmem_limit_bytes=4 << 20),
        name="collect",
    )(y0, *ys)

    turn = {(1, 0): (0, 0), (0, 0): (0, 1), (0, 1): (1, 1), (1, 1): (1, 0)}
    ring = send(own, lambda e, z1, k, x, yl: (e, turn[z1, yl][0], k, x, turn[z1, yl][1]))
    cross = send(own, lambda e, z1, k, x, yl: (e, yl, k, x, z1) if z1 != yl else None)
    q0 = pl.pallas_call(
        choose_kernel,
        out_shape=shape((2, QUARTERS, count, lanes), bf16),
        in_specs=vmem(3),
        out_specs=vmem(1)[0],
        compiler_params=pltpu.CompilerParams(vmem_limit_bytes=4 << 20),
        name="choose",
    )(own, ring, cross)
    here, q0 = lax.optimization_barrier((here, q0))
    qs = [send(q0, lambda e, z1, k, x, yl, t=t: (e, z1, k, (x - t) & 3, yl)) for t in (1, 3, 2)]
    q1, q3, q2 = qs
    there = send(here, lambda e, z1, k, x, yl: (e, 1 - z1, k, x, yl))

    total_shots = shots * lax.axis_size("shot")
    rows = 2 * NF * count
    p0, p1, p2, p3 = pl.pallas_call(
        lambda *refs: gram_kernel(1.0 / total_shots, *refs),
        out_shape=(shape((rows, receivers), f32),) + (shape((rows, receivers), bf16),) * 3,
        in_specs=vmem(6),
        out_specs=tuple(vmem(4)),
        scratch_shapes=[
            pltpu.VMEM((2, QUARTERS, 2 * receivers, lanes), bf16),
            pltpu.VMEM((QUARTERS, rows, receivers), f32),
        ],
        compiler_params=pltpu.CompilerParams(vmem_limit_bytes=12 << 20),
        name="gram",
    )(here, there, q0, q1, q2, q3)
    sums = p0
    for m, p in ((1, p1), (2, p2), (3, p3)):
        sums = sums + send(p, lambda e, z1, k, x, yl, m=m: ((e + m) & 3, z1, k, x, yl)).astype(f32)
    return sums.reshape(2, NF, count, receivers).transpose(0, 1, 3, 2)


def solution(mesh):
    return jax.shard_map(
        per_device,
        mesh=mesh,
        in_specs=(P("rcv", "shot"), P("shot")),
        out_specs=P(None, None, "rcv", "shot"),
        check_vma=False,
    )
```

```python
import math

import jax
import jax.numpy as jnp
import numpy as np
from jax import lax
from jax.experimental import pallas as pl
from jax.experimental.pallas import tpu as pltpu
from jax.sharding import PartitionSpec as P

import ml_dtypes

WIN = 2048
SPACING = 256
PAIR = 2 * SPACING
SPAN = WIN + PAIR
FREQ_BINS = (24, 40, 56, 80)
NF = len(FREQ_BINS)
ROWS = 2 * NF

SHOT_DEVICES = 32
RCV_DEVICES = 8
QUARTERS = 4
LATE = WIN // SPACING


def dft_master():
    turns = np.arange(WIN)[None, :] * np.array(FREQ_BINS)[:, None] % WIN
    angle = 2.0 * math.pi / WIN * turns
    rows = np.concatenate([np.cos(angle), -np.sin(angle)], axis=0) / math.sqrt(WIN)
    rows = rows.astype(np.float32).astype(ml_dtypes.bfloat16).astype(np.float32)
    return np.concatenate([rows, np.zeros((ROWS, SPAN - WIN), np.float32)], axis=1)


def send(block, to):
    route = []
    for shot in range(SHOT_DEVICES):
        for rcv in range(RCV_DEVICES):
            target = to(shot >> 4, (shot >> 2) & 3, shot & 3, rcv >> 2, rcv & 3)
            if target is not None:
                yh, u, k, xh, v = target
                route.append((shot * RCV_DEVICES + rcv, (yh << 4 | u << 2 | k) * RCV_DEVICES + (xh << 2 | v)))
    return lax.ppermute(block, ("shot", "rcv"), route)


def shot_index():
    return lax.axis_index("shot")


def vmem(count):
    return [pl.BlockSpec(memory_space=pltpu.VMEM)] * count


def pair_tables(table, first, second):
    rows = [pltpu.roll(table, first, 1), pltpu.roll(table, second + SPACING, 1)]
    return jnp.concatenate(rows, axis=0).astype(jnp.bfloat16)


def delay(fire, shot):
    return fire[shot] & (SPACING - 1)


def add_products(total, tables, first_pair, blocks):
    reach = SPAN // PAIR
    last_pair = first_pair + tables.shape[0] - 1
    for u, samples in blocks:
        low, high = max(first_pair, u - reach + 1), min(u, last_pair)
        left = jnp.concatenate(
            [tables[p - first_pair, :, PAIR * (u - p) : PAIR * (u - p + 1)] for p in range(low, high + 1)], axis=0
        )
        part = lax.dot_general(left, samples, (((1,), (1,)), ((), ())), preferred_element_type=jnp.float32)
        total[2 * ROWS * (low - first_pair) : 2 * ROWS * (high + 1 - first_pair), :] += part


def tail_kernel(fire, table, record, message, tables, samples, sem):
    pairs = fire.shape[0] // 2
    late = LATE // 2
    start = record.shape[1] - samples.shape[1]
    copy = pltpu.make_async_copy(record.at[:, start:], samples, sem)
    copy.start()
    master = table[...]
    for p in range(late):
        shot = 2 * (pairs - late + p)
        tables[p] = pair_tables(master, delay(fire, shot), delay(fire, shot + 1))
    message[...] = jnp.zeros_like(message)
    row = lax.broadcasted_iota(jnp.int32, (LATE, message.shape[1]), 0)
    delays = jnp.zeros(row.shape, jnp.int32)
    for i in range(LATE):
        delays = jnp.where(row == i, delay(fire, 2 * (pairs - late) + i), delays)
    message[ROWS * LATE :, :] = delays.astype(jnp.float32)
    copy.wait()
    blocks = [(pairs - late + v, samples[:, PAIR * v : PAIR * (v + 1)]) for v in range(late)]
    add_products(message, tables, pairs - late, blocks)


def own_kernel(fire, table, record, total, head, tables, samples, sems):
    parts = sems.shape[0]
    width = record.shape[1] // parts
    copies = [
        pltpu.make_async_copy(
            record.at[:, width * i : width * (i + 1)], samples.at[:, width * i : width * (i + 1)], sems.at[i]
        )
        for i in range(parts)
    ]
    for copy in copies:
        copy.start()
    master = table[...]
    for p in range(tables.shape[0]):
        tables[p] = pair_tables(master, delay(fire, 2 * p), delay(fire, 2 * p + 1))
    total[...] = jnp.zeros_like(total)
    per = width // PAIR
    for i, copy in enumerate(copies):
        copy.wait()
        blocks = [(per * i + v, samples[:, PAIR * (per * i + v) : PAIR * (per * i + v + 1)]) for v in range(per)]
        add_products(total, tables, 0, blocks)
    head[...] = samples[:, : head.shape[1]]


def finish_kernel(total, head, table, message, out, scratch, tables):
    own_rows = total.shape[0]
    lanes = scratch.shape[0]
    late = LATE // 2
    follows = (shot_index() > 0).astype(jnp.float32)
    master = table[...]
    for p in range(late):
        rows = [message[ROWS * LATE + 2 * p + i : ROWS * LATE + 2 * p + i + 1, :] for i in range(2)]
        first, second = [jnp.max(r).astype(jnp.int32) for r in rows]
        tables[p] = pair_tables(master, first, second)
    scratch[:own_rows, :] = jnp.zeros_like(total)
    scratch[own_rows:, :] = jnp.zeros((lanes - own_rows, total.shape[1]), jnp.float32)
    blocks = [(late + v, head[:, PAIR * v : PAIR * (v + 1)]) for v in range(late)]
    add_products(scratch.at[own_rows:, :], tables, 0, blocks)
    scratch[own_rows:, :] = message[: ROWS * LATE, :] + follows * scratch[own_rows:, :]
    scratch[:own_rows, :] = total[...]
    ordered = jnp.concatenate([scratch[pl.ds(c, lanes // ROWS, stride=ROWS), :] for c in range(ROWS)], axis=0)
    turned = ordered.T
    count = out.shape[1]
    for k in range(QUARTERS):
        out[k] = turned[count * k : count * (k + 1), :].astype(out.dtype)


def pair_kernel(own, other, out):
    yh = shot_index() >> 4
    out[yh] = own[...]
    out[1 - yh] = other[...]


def collect_kernel(y0, y1, y2, y3, gathered, quarter):
    k = shot_index() & 3
    for m, y in enumerate((y0, y1, y2, y3)):
        gathered[k ^ m] = y[...]
        quarter[k ^ m] = y[:, k]


def choose_kernel(own, cross, out):
    straight = (shot_index() >> 4) == (lax.axis_index("rcv") >> 2)

    @pl.when(straight)
    def _():
        out[...] = own[...]

    @pl.when(jnp.logical_not(straight))
    def _():
        out[...] = cross[...]


def right_kernel(gathered, right):
    half = right.shape[2] // 2
    for k in range(QUARTERS):
        for yh in range(2):
            z = gathered[k, yh].astype(jnp.float32).reshape(right.shape[1] // 2, 2 * half)
            w = jnp.concatenate([-z[:, half:], z[:, :half]], axis=1)
            right[2 * k + yh] = jnp.concatenate([z, w], axis=0).astype(jnp.bfloat16)


def gram_kernel(scale, right, q0, q1, q2, q3, p0, p1, p2, p3, total):
    turn = ((shot_index() >> 2) ^ lax.axis_index("rcv")) & 3
    count, lanes = q0.shape[2:]
    half = lanes // 2
    span = right.shape[1] // 2
    per = half // NF
    lane = lax.broadcasted_iota(jnp.int32, (count, lanes), 1) % half // per
    for m, q in enumerate((q0, q1, q2, q3)):
        acc = jnp.zeros((NF * count, 2 * span), jnp.float32)
        for k in range(QUARTERS):
            for yh in range(2):
                rows = q[k, yh].astype(jnp.float32)
                left = jnp.concatenate([jnp.where(lane == f, rows, 0.0) for f in range(NF)], axis=0)
                acc = acc + lax.dot_general(
                    left.astype(jnp.bfloat16),
                    right[2 * k + yh],
                    (((1,), (1,)), ((), ())),
                    preferred_element_type=jnp.float32,
                )
        total[turn ^ m, : NF * count, :] = acc[:, :span] * scale
        total[turn ^ m, NF * count :, :] = acc[:, span:] * scale
    for n, out in enumerate((p0, p1, p2, p3)):
        out[...] = total[n].astype(out.dtype)


def local(kernel, name, out_shape, in_specs, scratch=(), limit=4):
    single = not isinstance(out_shape, tuple)
    return pl.pallas_call(
        kernel,
        out_shape=out_shape,
        in_specs=in_specs,
        out_specs=vmem(1)[0] if single else tuple(vmem(len(out_shape))),
        scratch_shapes=list(scratch),
        compiler_params=pltpu.CompilerParams(vmem_limit_bytes=limit << 20),
        name=name,
    )


def per_device(record, shot_fire_samples):
    receivers, samples = record.shape
    shots = shot_fire_samples.shape[0]
    pairs, late = shots // 2, LATE // 2
    lanes = ROWS * shots
    late_rows = ROWS * LATE
    count = receivers // QUARTERS
    bf16, f32 = jnp.bfloat16, jnp.float32
    shape = jax.ShapeDtypeStruct
    table = jnp.asarray(dft_master())
    smem, hbm = pl.BlockSpec(memory_space=pltpu.SMEM), pl.BlockSpec(memory_space=pltpu.HBM)

    message = local(
        tail_kernel,
        "tail_spectra",
        shape((late_rows + LATE, receivers), f32),
        [smem] + vmem(1) + [hbm],
        [pltpu.VMEM((late, 2 * ROWS, SPAN), bf16), pltpu.VMEM((receivers, WIN), bf16), pltpu.SemaphoreType.DMA],
        limit=63,
    )(shot_fire_samples, table, record)

    def following(yh, u, k, xh, v):
        shot = ((yh << 4 | u << 2 | k) + 1) % SHOT_DEVICES
        return shot >> 4, (shot >> 2) & 3, shot & 3, xh, v

    received = send(message, following)
    total, head = local(
        own_kernel,
        "own_spectra",
        (shape((lanes - late_rows, receivers), f32), shape((receivers, WIN), bf16)),
        [smem] + vmem(1) + [hbm],
        [
            pltpu.VMEM((pairs - late, 2 * ROWS, SPAN), bf16),
            pltpu.VMEM((receivers, samples), bf16),
            pltpu.SemaphoreType.DMA((4,)),
        ],
        limit=63,
    )(shot_fire_samples, table, record)
    y = local(
        finish_kernel,
        "finish_spectra",
        shape((QUARTERS, count, lanes), bf16),
        vmem(4),
        [pltpu.VMEM((lanes, receivers), f32), pltpu.VMEM((late, 2 * ROWS, SPAN), bf16)],
    )(total, head, table, received)

    y = local(pair_kernel, "both_halves", shape((2,) + y.shape, bf16), vmem(2))(
        y, send(y, lambda yh, u, k, xh, v: (1 - yh, u, k, xh, v))
    )
    ys = [send(y, lambda yh, u, k, xh, v, m=m: (yh, u, k ^ m, xh, v)) for m in (1, 2, 3)]
    gathered, quarter = local(
        collect_kernel,
        "collect",
        (shape((QUARTERS,) + y.shape, bf16), shape((QUARTERS, 2, count, lanes), bf16)),
        vmem(4),
    )(y, *ys)
    cross = send(quarter, lambda yh, u, k, xh, v: (yh, u, k, 1 - xh, v) if xh == yh else None)
    q = local(choose_kernel, "choose", shape(quarter.shape, bf16), vmem(2))(quarter, cross)
    qs = [q] + [send(q, lambda yh, u, k, xh, v, m=m: (yh, u, k, xh, v ^ m)) for m in (1, 2, 3)]
    right = local(right_kernel, "right_side", shape((2 * QUARTERS, 2 * receivers, lanes), bf16), vmem(1))(gathered)

    total_shots = shots * lax.axis_size("shot")
    rows = ROWS * count
    first, *others = local(
        lambda *refs: gram_kernel(1.0 / total_shots, *refs),
        "gram",
        (shape((rows, receivers), f32),) + (shape((rows, receivers), bf16),) * 3,
        vmem(5),
        [pltpu.VMEM((QUARTERS, rows, receivers), f32)],
        limit=8,
    )(right, *qs)
    sums = first
    for n, share in enumerate(others, 1):
        sums = sums + send(share, lambda yh, u, k, xh, v, n=n: (yh, u ^ n, k, xh, v)).astype(f32)
    return sums.reshape(2, NF, count, receivers).transpose(0, 1, 3, 2)


def solution(mesh):
    return jax.shard_map(
        per_device,
        mesh=mesh,
        in_specs=(P("rcv", "shot"), P("shot")),
        out_specs=P(None, None, "rcv", "shot"),
        check_vma=False,
    )
```

```python
import math

import jax
import jax.numpy as jnp
import numpy as np
from jax import lax
from jax.experimental import pallas as pl
from jax.experimental.pallas import tpu as pltpu
from jax.sharding import PartitionSpec as P

import ml_dtypes

WIN = 2048
SPACING = 256
PAIR = 2 * SPACING
SPAN = WIN + PAIR
FREQ_BINS = (24, 40, 56, 80)
NF = len(FREQ_BINS)
ROWS = 2 * NF

SHOT_DEVICES = 32
RCV_DEVICES = 8
QUARTERS = 4
LATE = WIN // SPACING


def dft_master():
    turns = np.arange(WIN)[None, :] * np.array(FREQ_BINS)[:, None] % WIN
    angle = 2.0 * math.pi / WIN * turns
    rows = np.concatenate([np.cos(angle), -np.sin(angle)], axis=0) / math.sqrt(WIN)
    rows = rows.astype(np.float32).astype(ml_dtypes.bfloat16).astype(np.float32)
    return np.concatenate([rows, np.zeros((ROWS, SPAN - WIN), np.float32)], axis=1)


def send(block, to):
    route = []
    for shot in range(SHOT_DEVICES):
        for rcv in range(RCV_DEVICES):
            target = to(shot >> 4, (shot >> 2) & 3, shot & 3, rcv >> 2, rcv & 3)
            if target is not None:
                yh, u, k, xh, v = target
                route.append((shot * RCV_DEVICES + rcv, (yh << 4 | u << 2 | k) * RCV_DEVICES + (xh << 2 | v)))
    return lax.ppermute(block, ("shot", "rcv"), route)


def shot_index():
    return lax.axis_index("shot")


def vmem(count):
    return [pl.BlockSpec(memory_space=pltpu.VMEM)] * count


def pair_tables(table, first, second):
    rows = [pltpu.roll(table, first, 1), pltpu.roll(table, second + SPACING, 1)]
    return jnp.concatenate(rows, axis=0).astype(jnp.bfloat16)


def delay(fire, shot):
    return fire[shot] & (SPACING - 1)


def add_products(total, tables, first_pair, blocks):
    reach = SPAN // PAIR
    last_pair = first_pair + tables.shape[0] - 1
    for u, samples in blocks:
        low, high = max(first_pair, u - reach + 1), min(u, last_pair)
        left = jnp.concatenate(
            [tables[p - first_pair, :, PAIR * (u - p) : PAIR * (u - p + 1)] for p in range(low, high + 1)], axis=0
        )
        part = lax.dot_general(left, samples, (((1,), (1,)), ((), ())), preferred_element_type=jnp.float32)
        total[2 * ROWS * (low - first_pair) : 2 * ROWS * (high + 1 - first_pair), :] += part


def tail_kernel(fire_hbm, table_hbm, record, message, fire, table, tables, samples, sems):
    pairs = fire.shape[0] // 2
    late = LATE // 2
    start = record.shape[1] - samples.shape[1]
    copies = [
        pltpu.make_async_copy(fire_hbm, fire, sems.at[0]),
        pltpu.make_async_copy(table_hbm, table, sems.at[1]),
        pltpu.make_async_copy(record.at[:, start:], samples, sems.at[2]),
    ]
    for copy in copies:
        copy.start()
    message[...] = jnp.zeros_like(message)
    copies[0].wait()
    row = lax.broadcasted_iota(jnp.int32, (LATE, message.shape[1]), 0)
    delays = jnp.zeros(row.shape, jnp.int32)
    for i in range(LATE):
        delays = jnp.where(row == i, delay(fire, 2 * (pairs - late) + i), delays)
    message[ROWS * LATE :, :] = delays.astype(jnp.float32)
    copies[1].wait()
    master = table[...]
    for p in range(late):
        shot = 2 * (pairs - late + p)
        tables[p] = pair_tables(master, delay(fire, shot), delay(fire, shot + 1))
    copies[2].wait()
    blocks = [(pairs - late + v, samples[:, PAIR * v : PAIR * (v + 1)]) for v in range(late)]
    add_products(message, tables, pairs - late, blocks)


def own_kernel(fire, table, record, total, tables):
    pairs = record.shape[1] // PAIR
    master = table[...]
    for p in range(tables.shape[0]):
        tables[p] = pair_tables(master, delay(fire, 2 * p), delay(fire, 2 * p + 1))
    total[...] = jnp.zeros_like(total)
    add_products(total, tables, 0, [(u, record[:, PAIR * u : PAIR * (u + 1)]) for u in range(pairs)])


def finish_kernel(total, head, table, message, out, scratch, tables):
    own_rows = total.shape[0]
    lanes = scratch.shape[0]
    late = LATE // 2
    follows = (shot_index() > 0).astype(jnp.float32)
    master = table[...]
    for p in range(late):
        rows = [message[ROWS * LATE + 2 * p + i : ROWS * LATE + 2 * p + i + 1, :] for i in range(2)]
        first, second = [jnp.max(r).astype(jnp.int32) for r in rows]
        tables[p] = pair_tables(master, first, second)
    scratch[:own_rows, :] = jnp.zeros_like(total)
    scratch[own_rows:, :] = jnp.zeros((lanes - own_rows, total.shape[1]), jnp.float32)
    blocks = [(late + v, head[:, PAIR * v : PAIR * (v + 1)]) for v in range(late)]
    add_products(scratch.at[own_rows:, :], tables, 0, blocks)
    scratch[own_rows:, :] = message[: ROWS * LATE, :] + follows * scratch[own_rows:, :]
    scratch[:own_rows, :] = total[...]
    ordered = jnp.concatenate([scratch[pl.ds(c, lanes // ROWS, stride=ROWS), :] for c in range(ROWS)], axis=0)
    turned = ordered.T
    count = out.shape[1]
    for k in range(QUARTERS):
        out[k] = turned[count * k : count * (k + 1), :].astype(out.dtype)


def join_kernel(place, own, other, out):
    here = place(shot_index())
    out[here] = own[...]
    out[1 - here] = other[...]


def collect_kernel(own, other, gathered, quarter):
    k = shot_index() & 3
    here = k & 1
    gathered[here] = own[...]
    gathered[1 - here] = other[...]
    quarter[here] = own[:, :, k]
    quarter[1 - here] = other[:, :, k]


def choose_kernel(own, cross, out):
    straight = (shot_index() >> 4) == (lax.axis_index("rcv") >> 2)

    @pl.when(straight)
    def _():
        out[...] = own[...]

    @pl.when(jnp.logical_not(straight))
    def _():
        out[...] = cross[...]


def right_kernel(gathered, right):
    half = right.shape[2] // 2
    for part in range(right.shape[0]):
        z = gathered[part >> 2, (part >> 1) & 1, part & 1].astype(jnp.float32).reshape(right.shape[1] // 2, 2 * half)
        w = jnp.concatenate([-z[:, half:], z[:, :half]], axis=1)
        right[part] = jnp.concatenate([z, w], axis=0).astype(jnp.bfloat16)


def gram_kernel(scale, right, q0, q1, q2, q3, p0, p1, p2, p3, total):
    turn = ((shot_index() >> 2) ^ lax.axis_index("rcv")) & 3
    count, lanes = q0.shape[3:]
    half = lanes // 2
    span = right.shape[1] // 2
    per = half // NF
    lane = lax.broadcasted_iota(jnp.int32, (count, lanes), 1) % half // per
    for m, q in enumerate((q0, q1, q2, q3)):
        acc = jnp.zeros((NF * count, 2 * span), jnp.float32)
        for part in range(right.shape[0]):
            rows = q[part >> 2, (part >> 1) & 1, part & 1].astype(jnp.float32)
            left = jnp.concatenate([jnp.where(lane == f, rows, 0.0) for f in range(NF)], axis=0)
            acc = acc + lax.dot_general(
                left.astype(jnp.bfloat16), right[part], (((1,), (1,)), ((), ())), preferred_element_type=jnp.float32
            )
        total[turn ^ m, : NF * count, :] = acc[:, :span] * scale
        total[turn ^ m, NF * count :, :] = acc[:, span:] * scale
    for n, out in enumerate((p0, p1, p2, p3)):
        out[...] = total[n].astype(out.dtype)


def local(kernel, name, out_shape, in_specs, scratch=(), limit=4):
    single = not isinstance(out_shape, tuple)
    return pl.pallas_call(
        kernel,
        out_shape=out_shape,
        in_specs=in_specs,
        out_specs=vmem(1)[0] if single else tuple(vmem(len(out_shape))),
        scratch_shapes=list(scratch),
        compiler_params=pltpu.CompilerParams(vmem_limit_bytes=limit << 20),
        name=name,
    )


def per_device(record, shot_fire_samples):
    receivers, samples = record.shape
    shots = shot_fire_samples.shape[0]
    pairs, late = shots // 2, LATE // 2
    lanes = ROWS * shots
    late_rows = ROWS * LATE
    count = receivers // QUARTERS
    bf16, f32 = jnp.bfloat16, jnp.float32
    shape = jax.ShapeDtypeStruct
    table = jnp.asarray(dft_master())
    smem, hbm = pl.BlockSpec(memory_space=pltpu.SMEM), pl.BlockSpec(memory_space=pltpu.HBM)

    message = local(
        tail_kernel,
        "tail_spectra",
        shape((late_rows + LATE, receivers), f32),
        [hbm] * 3,
        [
            pltpu.SMEM((shots,), jnp.int32),
            pltpu.VMEM(table.shape, f32),
            pltpu.VMEM((late, 2 * ROWS, SPAN), bf16),
            pltpu.VMEM((receivers, WIN), bf16),
            pltpu.SemaphoreType.DMA((3,)),
        ],
        limit=63,
    )(shot_fire_samples, table, record)

    def following(yh, u, k, xh, v):
        shot = ((yh << 4 | u << 2 | k) + 1) % SHOT_DEVICES
        return shot >> 4, (shot >> 2) & 3, shot & 3, xh, v

    received = send(message, following)
    total = local(
        own_kernel,
        "own_spectra",
        shape((lanes - late_rows, receivers), f32),
        [smem] + vmem(2),
        [pltpu.VMEM((pairs - late, 2 * ROWS, SPAN), bf16)],
    )(shot_fire_samples, table, record)
    y = pl.pallas_call(
        finish_kernel,
        grid=(1,),
        out_shape=shape((QUARTERS, count, lanes), bf16),
        in_specs=[
            pl.BlockSpec(total.shape, lambda i: (0, 0)),
            pl.BlockSpec((receivers, WIN), lambda i: (0, 0)),
            pl.BlockSpec(table.shape, lambda i: (0, 0)),
            pl.BlockSpec(received.shape, lambda i: (0, 0)),
        ],
        out_specs=pl.BlockSpec((QUARTERS, count, lanes), lambda i: (0, 0, 0)),
        scratch_shapes=[pltpu.VMEM((lanes, receivers), f32), pltpu.VMEM((late, 2 * ROWS, SPAN), bf16)],
        compiler_params=pltpu.CompilerParams(vmem_limit_bytes=4 << 20),
        name="finish_spectra",
    )(total, record, table, received)

    def join(own, other, place, name):
        return local(lambda *refs: join_kernel(place, *refs), name, shape((2,) + own.shape, bf16), vmem(2))(own, other)

    other = send(y, lambda yh, u, k, xh, v: (yh, u, k ^ 2, xh, v))
    y = join(y, other, lambda shot: (shot >> 1) & 1, "join_z0")
    other = send(y, lambda yh, u, k, xh, v: (1 - yh, u, k, xh, v))
    y = join(y, other, lambda shot: shot >> 4, "join_yh")
    other = send(y, lambda yh, u, k, xh, v: (yh, u, k ^ 1, xh, v))
    gathered, quarter = local(
        collect_kernel,
        "collect",
        (shape((2,) + y.shape, bf16), shape((2,) + y.shape[:2] + (count, lanes), bf16)),
        vmem(2),
    )(y, other)
    cross = send(quarter, lambda yh, u, k, xh, v: (yh, u, k, 1 - xh, v) if xh == yh else None)
    q = local(choose_kernel, "choose", shape(quarter.shape, bf16), vmem(2))(quarter, cross)
    qs = [q] + [send(q, lambda yh, u, k, xh, v, m=m: (yh, u, k, xh, v ^ m)) for m in (1, 2, 3)]
    right = local(right_kernel, "right_side", shape((2 * QUARTERS, 2 * receivers, lanes), bf16), vmem(1))(gathered)

    total_shots = shots * lax.axis_size("shot")
    rows = ROWS * count
    first, *others = local(
        lambda *refs: gram_kernel(1.0 / total_shots, *refs),
        "gram",
        (shape((rows, receivers), f32),) + (shape((rows, receivers), bf16),) * 3,
        vmem(5),
        [pltpu.VMEM((QUARTERS, rows, receivers), f32)],
        limit=8,
    )(right, *qs)
    sums = first
    for n in (1, 3, 2):
        sums = sums + send(others[n - 1], lambda yh, u, k, xh, v, n=n: (yh, u ^ n, k, xh, v)).astype(f32)
    return sums.reshape(2, NF, count, receivers).transpose(0, 1, 3, 2)


def solution(mesh):
    return jax.shard_map(
        per_device,
        mesh=mesh,
        in_specs=(P("rcv", "shot"), P("shot")),
        out_specs=P(None, None, "rcv", "shot"),
        check_vma=False,
    )
```

```python
import math

import jax
import jax.numpy as jnp
import numpy as np
from jax import lax
from jax.experimental import pallas as pl
from jax.experimental.pallas import tpu as pltpu
from jax.sharding import PartitionSpec as P

import ml_dtypes

WIN = 2048
SPACING = 256
PAIR = 2 * SPACING
SPAN = WIN + PAIR
FREQ_BINS = (24, 40, 56, 80)
NF = len(FREQ_BINS)
ROWS = 2 * NF

SHOT_DEVICES = 32
RCV_DEVICES = 8
QUARTERS = 4
LATE = WIN // SPACING


def dft_master():
    turns = np.arange(WIN)[None, :] * np.array(FREQ_BINS)[:, None] % WIN
    angle = 2.0 * math.pi / WIN * turns
    rows = np.concatenate([np.cos(angle), -np.sin(angle)], axis=0) / math.sqrt(WIN)
    rows = rows.astype(np.float32).astype(ml_dtypes.bfloat16).astype(np.float32)
    return np.concatenate([rows, np.zeros((ROWS, SPAN - WIN), np.float32)], axis=1)


def send(block, to):
    route = []
    for shot in range(SHOT_DEVICES):
        for rcv in range(RCV_DEVICES):
            target = to(shot >> 4, (shot >> 2) & 3, shot & 3, rcv >> 2, rcv & 3)
            if target is not None:
                yh, u, k, xh, v = target
                route.append((shot * RCV_DEVICES + rcv, (yh << 4 | u << 2 | k) * RCV_DEVICES + (xh << 2 | v)))
    return lax.ppermute(block, ("shot", "rcv"), route)


shape = jax.ShapeDtypeStruct


def shot_index():
    return lax.axis_index("shot")


def vmem(count):
    return [pl.BlockSpec(memory_space=pltpu.VMEM)] * count


def pair_tables(table, first, second):
    rows = [pltpu.roll(table, first, 1), pltpu.roll(table, second + SPACING, 1)]
    return jnp.concatenate(rows, axis=0).astype(jnp.bfloat16)


def delay(fire, shot):
    return fire[shot] & (SPACING - 1)


def add_products(total, tables, first_pair, blocks):
    reach = SPAN // PAIR
    last_pair = first_pair + tables.shape[0] - 1
    for u, samples in blocks:
        low, high = max(first_pair, u - reach + 1), min(u, last_pair)
        left = jnp.concatenate(
            [tables[p - first_pair, :, PAIR * (u - p) : PAIR * (u - p + 1)] for p in range(low, high + 1)], axis=0
        )
        part = lax.dot_general(left, samples, (((1,), (1,)), ((), ())), preferred_element_type=jnp.float32)
        total[2 * ROWS * (low - first_pair) : 2 * ROWS * (high + 1 - first_pair), :] += part


def tail_kernel(fire_hbm, table_hbm, record, message, fire, table, tables, samples, sems):
    pairs = fire.shape[0] // 2
    late = LATE // 2
    start = record.shape[1] - samples.shape[1]
    copies = [
        pltpu.make_async_copy(fire_hbm, fire, sems.at[0]),
        pltpu.make_async_copy(table_hbm, table, sems.at[1]),
        pltpu.make_async_copy(record.at[:, start:], samples, sems.at[2]),
    ]
    for copy in copies:
        copy.start()
    message[...] = jnp.zeros_like(message)
    copies[0].wait()
    row = lax.broadcasted_iota(jnp.int32, (LATE, message.shape[1]), 0)
    delays = jnp.zeros(row.shape, jnp.int32)
    for i in range(LATE):
        delays = jnp.where(row == i, delay(fire, 2 * (pairs - late) + i), delays)
    message[ROWS * LATE :, :] = delays.astype(jnp.float32)
    copies[1].wait()
    master = table[...]
    for p in range(late):
        shot = 2 * (pairs - late + p)
        tables[p] = pair_tables(master, delay(fire, shot), delay(fire, shot + 1))
    copies[2].wait()
    blocks = [(pairs - late + v, samples[:, PAIR * v : PAIR * (v + 1)]) for v in range(late)]
    add_products(message, tables, pairs - late, blocks)


def own_kernel(fire, table, record, total, tables):
    pairs = record.shape[1] // PAIR
    master = table[...]
    for p in range(tables.shape[0]):
        tables[p] = pair_tables(master, delay(fire, 2 * p), delay(fire, 2 * p + 1))
    total[...] = jnp.zeros_like(total)
    add_products(total, tables, 0, [(u, record[:, PAIR * u : PAIR * (u + 1)]) for u in range(pairs)])


def finish_kernel(total, head, table, message, out, scratch, tables):
    own_rows = total.shape[0]
    lanes = scratch.shape[0]
    late = LATE // 2
    follows = (shot_index() > 0).astype(jnp.float32)
    master = table[...]
    for p in range(late):
        rows = [message[ROWS * LATE + 2 * p + i : ROWS * LATE + 2 * p + i + 1, :] for i in range(2)]
        first, second = [jnp.max(r).astype(jnp.int32) for r in rows]
        tables[p] = pair_tables(master, first, second)
    scratch[:own_rows, :] = jnp.zeros_like(total)
    scratch[own_rows:, :] = jnp.zeros((lanes - own_rows, total.shape[1]), jnp.float32)
    blocks = [(late + v, head[:, PAIR * v : PAIR * (v + 1)]) for v in range(late)]
    add_products(scratch.at[own_rows:, :], tables, 0, blocks)
    scratch[own_rows:, :] = message[: ROWS * LATE, :] + follows * scratch[own_rows:, :]
    scratch[:own_rows, :] = total[...]
    turn_over(scratch, out)


def turn_over(scratch, out):
    shots = scratch.shape[0] // ROWS
    ordered = jnp.concatenate([scratch[pl.ds(c, shots, stride=ROWS), :] for c in range(ROWS)], axis=0)
    turned = ordered.T
    count = out.shape[1]
    for k in range(QUARTERS):
        out[k] = turned[count * k : count * (k + 1), :].astype(out.dtype)


def wrap_kernel(message, out, scratch):
    late_rows = ROWS * LATE
    own_rows = scratch.shape[0] - late_rows
    scratch[:own_rows, :] = jnp.zeros((own_rows, scratch.shape[1]), jnp.float32)
    scratch[own_rows:, :] = message[:late_rows, :]
    turn_over(scratch, out)


def yh_kernel(own, other, extra1, extra0, out):
    yh = shot_index() >> 4
    out[yh] = own[...]
    out[1 - yh] = other[...]
    extra = extra1[...].astype(jnp.float32) + extra0[...].astype(jnp.float32)
    out[0] = (out[0].astype(jnp.float32) + extra).astype(out.dtype)


def z0_kernel(own, other, out, mine, theirs):
    k = shot_index() & 3
    z0 = k >> 1
    for here, block in ((z0, own), (1 - z0, other)):
        out[here] = block[...]
        mine[here] = block[:, k]
        theirs[here] = block[:, k ^ 1]


def core_kernel(own, other, out):
    c = shot_index() & 1
    out[c] = own[...]
    out[1 - c] = other[...]


def choose_kernel(own, cross, out):
    straight = (shot_index() >> 4) == (lax.axis_index("rcv") >> 2)

    @pl.when(straight)
    def _():
        out[...] = own[...]

    @pl.when(jnp.logical_not(straight))
    def _():
        out[...] = cross[...]


def right_kernel(own, other, right):
    c = shot_index() & 1
    half = right.shape[2] // 2
    parts = right.shape[0] // 2
    for here, block in ((c, own), (1 - c, other)):
        for part in range(parts):
            z = block[part >> 1, part & 1].astype(jnp.float32).reshape(right.shape[1] // 2, 2 * half)
            w = jnp.concatenate([-z[:, half:], z[:, :half]], axis=1)
            right[parts * here + part] = jnp.concatenate([z, w], axis=0).astype(jnp.bfloat16)


def products(scale, right, q):
    count, lanes = q.shape[3:]
    half = lanes // 2
    span = right.shape[1] // 2
    lane = lax.broadcasted_iota(jnp.int32, (count, lanes), 1) % half // (half // NF)
    acc = jnp.zeros((NF * count, 2 * span), jnp.float32)
    for part in range(right.shape[0]):
        rows = q[part >> 2, (part >> 1) & 1, part & 1].astype(jnp.float32)
        left = jnp.concatenate([jnp.where(lane == f, rows, 0.0) for f in range(NF)], axis=0)
        acc = acc + lax.dot_general(
            left.astype(jnp.bfloat16), right[part], (((1,), (1,)), ((), ())), preferred_element_type=jnp.float32
        )
    return jnp.concatenate([acc[:, :span] * scale, acc[:, span:] * scale], axis=0)


def gram_kernel(scale, right, q, before, out):
    out[...] = products(scale, right, q)


def last_kernel(scale, right, q, g0, g3, g1, p0, p1, p2, p3, total):
    turn = ((shot_index() >> 2) ^ lax.axis_index("rcv")) & 3
    total[turn] = g0[...]
    total[turn ^ 3] = g3[...]
    total[turn ^ 1] = g1[...]
    total[turn ^ 2] = products(scale, right, q)
    for n, out in enumerate((p0, p1, p2, p3)):
        out[...] = total[n].astype(out.dtype)


def local(kernel, name, out_shape, in_specs, scratch=(), limit=4):
    single = not isinstance(out_shape, tuple)
    return pl.pallas_call(
        kernel,
        out_shape=out_shape,
        in_specs=in_specs,
        out_specs=vmem(1)[0] if single else tuple(vmem(len(out_shape))),
        scratch_shapes=list(scratch),
        compiler_params=pltpu.CompilerParams(vmem_limit_bytes=limit << 20),
        name=name,
    )


def per_device(record, shot_fire_samples):
    receivers, samples = record.shape
    shots = shot_fire_samples.shape[0]
    pairs, late = shots // 2, LATE // 2
    lanes = ROWS * shots
    late_rows = ROWS * LATE
    count = receivers // QUARTERS
    bf16, f32 = jnp.bfloat16, jnp.float32
    table = jnp.asarray(dft_master())
    smem, hbm = pl.BlockSpec(memory_space=pltpu.SMEM), pl.BlockSpec(memory_space=pltpu.HBM)

    message = local(
        tail_kernel,
        "tail_spectra",
        shape((late_rows + LATE, receivers), f32),
        [hbm] * 3,
        [
            pltpu.SMEM((shots,), jnp.int32),
            pltpu.VMEM(table.shape, f32),
            pltpu.VMEM((late, 2 * ROWS, SPAN), bf16),
            pltpu.VMEM((receivers, WIN), bf16),
            pltpu.SemaphoreType.DMA((3,)),
        ],
        limit=63,
    )(shot_fire_samples, table, record)

    def following(yh, u, k, xh, v):
        shot = (yh << 4 | u << 2 | k) + 1
        return (shot >> 4, (shot >> 2) & 3, shot & 3, xh, v) if shot < SHOT_DEVICES else None

    received = send(message, following)
    block = local(
        wrap_kernel,
        "wrap_spectra",
        shape((QUARTERS, count, lanes), bf16),
        vmem(1),
        [pltpu.VMEM((lanes, receivers), f32)],
    )(message)
    extras = [
        send(block, lambda yh, u, k, xh, v, to=to: (to, 0, 0, xh, v) if (yh, u, k) == (1, 3, 3) else None)
        for to in (1, 0)
    ]
    total = local(
        own_kernel,
        "own_spectra",
        shape((lanes - late_rows, receivers), f32),
        [smem] + vmem(2),
        [pltpu.VMEM((pairs - late, 2 * ROWS, SPAN), bf16)],
    )(shot_fire_samples, table, record)
    y = pl.pallas_call(
        finish_kernel,
        grid=(1,),
        out_shape=shape((QUARTERS, count, lanes), bf16),
        in_specs=[
            pl.BlockSpec(total.shape, lambda i: (0, 0)),
            pl.BlockSpec((receivers, WIN), lambda i: (0, 0)),
            pl.BlockSpec(table.shape, lambda i: (0, 0)),
            pl.BlockSpec(received.shape, lambda i: (0, 0)),
        ],
        out_specs=pl.BlockSpec((QUARTERS, count, lanes), lambda i: (0, 0, 0)),
        scratch_shapes=[pltpu.VMEM((lanes, receivers), f32), pltpu.VMEM((late, 2 * ROWS, SPAN), bf16)],
        compiler_params=pltpu.CompilerParams(vmem_limit_bytes=4 << 20),
        name="finish_spectra",
    )(total, record, table, received)

    other = send(y, lambda yh, u, k, xh, v: (1 - yh, u, k, xh, v))
    y = local(yh_kernel, "join_yh", shape((2,) + y.shape, bf16), vmem(4))(y, other, *extras)
    other = send(y, lambda yh, u, k, xh, v: (yh, u, k ^ 2, xh, v))
    slices = shape((2, 2, count, lanes), bf16)
    y, mine, theirs = local(z0_kernel, "join_z0", (shape((2,) + y.shape, bf16), slices, slices), vmem(2))(y, other)

    def to_partner(yh, u, k, xh, v):
        return yh, u, k ^ 1, xh, v

    quarter = local(core_kernel, "join_core", shape((2,) + mine.shape, bf16), vmem(2))(mine, send(theirs, to_partner))
    cross = send(quarter, lambda yh, u, k, xh, v: (yh, u, k, 1 - xh, v) if xh == yh else None)
    q = local(choose_kernel, "choose", shape(quarter.shape, bf16), vmem(2))(quarter, cross)
    qs = [q] + [send(q, lambda yh, u, k, xh, v, m=m: (yh, u, k, xh, v ^ m)) for m in (1, 2, 3)]
    right = local(right_kernel, "right_side", shape((2 * QUARTERS, 2 * receivers, lanes), bf16), vmem(2))(
        y, send(y, to_partner)
    )

    total_shots = shots * lax.axis_size("shot")
    rows = ROWS * count
    scale = 1.0 / total_shots
    share = shape((rows, receivers), f32)
    wire = shape((rows, receivers), bf16)
    early = []
    for m in (0, 3, 1):
        early += [
            local(
                lambda *refs: gram_kernel(scale, *refs),
                "gram",
                share,
                vmem(2) + [pl.BlockSpec(memory_space=pl.ANY)],
            )(right, qs[m], early[-1] if early else right)
        ]
    sums, p1, p2, p3 = local(
        lambda *refs: last_kernel(scale, *refs),
        "last_gram",
        (share, wire, wire, wire),
        vmem(5),
        [pltpu.VMEM((QUARTERS, rows, receivers), f32)],
    )(right, qs[2], *early)
    for n, p in ((2, p2), (3, p3), (1, p1)):
        sums = sums + send(p, lambda yh, u, k, xh, v, n=n: (yh, u ^ n, k, xh, v)).astype(f32)
    return sums.reshape(2, NF, count, receivers).transpose(0, 1, 3, 2)


def solution(mesh):
    return jax.shard_map(
        per_device,
        mesh=mesh,
        in_specs=(P("rcv", "shot"), P("shot")),
        out_specs=P(None, None, "rcv", "shot"),
        check_vma=False,
    )
```

```python
import math

import jax
import jax.numpy as jnp
import numpy as np
from jax import lax
from jax.experimental import pallas as pl
from jax.experimental.pallas import tpu as pltpu
from jax.sharding import PartitionSpec as P

import ml_dtypes

WIN = 2048
SPACING = 256
PAIR = 2 * SPACING
SPAN = WIN + PAIR
FREQ_BINS = (24, 40, 56, 80)
NF = len(FREQ_BINS)
ROWS = 2 * NF

SHOT_DEVICES = 32
RCV_DEVICES = 8
QUARTERS = 4
LATE = WIN // SPACING


def dft_master():
    turns = np.arange(WIN)[None, :] * np.array(FREQ_BINS)[:, None] % WIN
    angle = 2.0 * math.pi / WIN * turns
    rows = np.concatenate([np.cos(angle), -np.sin(angle)], axis=0) / math.sqrt(WIN)
    rows = rows.astype(np.float32).astype(ml_dtypes.bfloat16).astype(np.float32)
    return np.concatenate([rows, np.zeros((ROWS, SPAN - WIN), np.float32)], axis=1)


def send(block, to):
    route = []
    for shot in range(SHOT_DEVICES):
        for rcv in range(RCV_DEVICES):
            target = to(shot >> 4, (shot >> 2) & 3, shot & 3, rcv >> 2, rcv & 3)
            if target is not None:
                yh, u, k, xh, v = target
                route.append((shot * RCV_DEVICES + rcv, (yh << 4 | u << 2 | k) * RCV_DEVICES + (xh << 2 | v)))
    return lax.ppermute(block, ("shot", "rcv"), route)


shape = jax.ShapeDtypeStruct


def shot_index():
    return lax.axis_index("shot")


def vmem(count):
    return [pl.BlockSpec(memory_space=pltpu.VMEM)] * count


def pair_tables(table, first, second):
    rows = [pltpu.roll(table, first, 1), pltpu.roll(table, second + SPACING, 1)]
    return jnp.concatenate(rows, axis=0).astype(jnp.bfloat16)


def delay(fire, shot):
    return fire[shot] & (SPACING - 1)


def add_products(total, tables, first_pair, blocks):
    reach = SPAN // PAIR
    last_pair = first_pair + tables.shape[0] - 1
    for u, samples in blocks:
        low, high = max(first_pair, u - reach + 1), min(u, last_pair)
        left = jnp.concatenate(
            [tables[p - first_pair, :, PAIR * (u - p) : PAIR * (u - p + 1)] for p in range(low, high + 1)], axis=0
        )
        part = lax.dot_general(left, samples, (((1,), (1,)), ((), ())), preferred_element_type=jnp.float32)
        total[2 * ROWS * (low - first_pair) : 2 * ROWS * (high + 1 - first_pair), :] += part


def tail_kernel(fire_hbm, table_hbm, record, message, fire, table, tables, samples, sems):
    pairs = fire.shape[0] // 2
    late = LATE // 2
    start = record.shape[1] - samples.shape[1]
    copies = [
        pltpu.make_async_copy(fire_hbm, fire, sems.at[0]),
        pltpu.make_async_copy(table_hbm, table, sems.at[1]),
        pltpu.make_async_copy(record.at[:, start:], samples, sems.at[2]),
    ]
    for copy in copies:
        copy.start()
    message[...] = jnp.zeros_like(message)
    copies[0].wait()
    row = lax.broadcasted_iota(jnp.int32, (LATE, message.shape[1]), 0)
    delays = jnp.zeros(row.shape, jnp.int32)
    for i in range(LATE):
        delays = jnp.where(row == i, delay(fire, 2 * (pairs - late) + i), delays)
    message[ROWS * LATE :, :] = delays.astype(jnp.float32)
    copies[1].wait()
    master = table[...]
    for p in range(late):
        shot = 2 * (pairs - late + p)
        tables[p] = pair_tables(master, delay(fire, shot), delay(fire, shot + 1))
    copies[2].wait()
    blocks = [(pairs - late + v, samples[:, PAIR * v : PAIR * (v + 1)]) for v in range(late)]
    add_products(message, tables, pairs - late, blocks)


def own_kernel(fire, table, record, total, tables):
    pairs = record.shape[1] // PAIR
    master = table[...]
    for p in range(tables.shape[0]):
        tables[p] = pair_tables(master, delay(fire, 2 * p), delay(fire, 2 * p + 1))
    total[...] = jnp.zeros_like(total)
    add_products(total, tables, 0, [(u, record[:, PAIR * u : PAIR * (u + 1)]) for u in range(pairs)])


def finish_kernel(total, head, table, message, out, scratch, tables):
    own_rows = total.shape[0]
    lanes = scratch.shape[0]
    late = LATE // 2
    follows = (shot_index() > 0).astype(jnp.float32)
    master = table[...]
    for p in range(late):
        rows = [message[ROWS * LATE + 2 * p + i : ROWS * LATE + 2 * p + i + 1, :] for i in range(2)]
        first, second = [jnp.max(r).astype(jnp.int32) for r in rows]
        tables[p] = pair_tables(master, first, second)
    scratch[:own_rows, :] = jnp.zeros_like(total)
    scratch[own_rows:, :] = jnp.zeros((lanes - own_rows, total.shape[1]), jnp.float32)
    blocks = [(late + v, head[:, PAIR * v : PAIR * (v + 1)]) for v in range(late)]
    add_products(scratch.at[own_rows:, :], tables, 0, blocks)
    scratch[own_rows:, :] = message[: ROWS * LATE, :] + follows * scratch[own_rows:, :]
    scratch[:own_rows, :] = total[...]
    turn_over(scratch, out)


def turn_over(scratch, out):
    shots = scratch.shape[0] // ROWS
    ordered = jnp.concatenate([scratch[pl.ds(c, shots, stride=ROWS), :] for c in range(ROWS)], axis=0)
    turned = ordered.T
    count = out.shape[1]
    for k in range(QUARTERS):
        out[k] = turned[count * k : count * (k + 1), :].astype(out.dtype)


def yh_kernel(own, other, out):
    yh = shot_index() >> 4
    out[yh] = own[...]
    out[1 - yh] = other[...]


def z0_kernel(own, other, out, mine, theirs):
    k = shot_index() & 3
    z0 = k >> 1
    for here, block in ((z0, own), (1 - z0, other)):
        out[here] = block[...]
        mine[here] = block[:, k]
        theirs[here] = block[:, k ^ 1]


def core_kernel(own, other, out):
    c = shot_index() & 1
    out[c] = own[...]
    out[1 - c] = other[...]


def choose_kernel(own, cross, out):
    straight = (shot_index() >> 4) == (lax.axis_index("rcv") >> 2)

    @pl.when(straight)
    def _():
        out[...] = own[...]

    @pl.when(jnp.logical_not(straight))
    def _():
        out[...] = cross[...]


def right_kernel(own, other, right):
    c = shot_index() & 1
    half = right.shape[2] // 2
    parts = right.shape[0] // 2
    for here, block in ((c, own), (1 - c, other)):
        for part in range(parts):
            z = block[part >> 1, part & 1].astype(jnp.float32).reshape(right.shape[1] // 2, 2 * half)
            w = jnp.concatenate([-z[:, half:], z[:, :half]], axis=1)
            right[parts * here + part] = jnp.concatenate([z, w], axis=0).astype(jnp.bfloat16)


def products(scale, right, q):
    count, lanes = q.shape[3:]
    half = lanes // 2
    span = right.shape[1] // 2
    lane = lax.broadcasted_iota(jnp.int32, (count, lanes), 1) % half // (half // NF)
    acc = jnp.zeros((NF * count, 2 * span), jnp.float32)
    for part in range(right.shape[0]):
        rows = q[part >> 2, (part >> 1) & 1, part & 1].astype(jnp.float32)
        left = jnp.concatenate([jnp.where(lane == f, rows, 0.0) for f in range(NF)], axis=0)
        acc = acc + lax.dot_general(
            left.astype(jnp.bfloat16), right[part], (((1,), (1,)), ((), ())), preferred_element_type=jnp.float32
        )
    return jnp.concatenate([acc[:, :span] * scale, acc[:, span:] * scale], axis=0)


def gram_kernel(scale, right, q, before, out):
    out[...] = products(scale, right, q)


def last_kernel(scale, right, q, g0, g3, g1, p0, p1, p2, p3, total):
    turn = ((shot_index() >> 2) ^ lax.axis_index("rcv")) & 3
    total[turn] = g0[...]
    total[turn ^ 3] = g3[...]
    total[turn ^ 1] = g1[...]
    total[turn ^ 2] = products(scale, right, q)
    for n, out in enumerate((p0, p1, p2, p3)):
        out[...] = total[n].astype(out.dtype)


def local(kernel, name, out_shape, in_specs, scratch=(), limit=4):
    single = not isinstance(out_shape, tuple)
    return pl.pallas_call(
        kernel,
        out_shape=out_shape,
        in_specs=in_specs,
        out_specs=vmem(1)[0] if single else tuple(vmem(len(out_shape))),
        scratch_shapes=list(scratch),
        compiler_params=pltpu.CompilerParams(vmem_limit_bytes=limit << 20),
        name=name,
    )


def per_device(record, shot_fire_samples):
    receivers, samples = record.shape
    shots = shot_fire_samples.shape[0]
    pairs, late = shots // 2, LATE // 2
    lanes = ROWS * shots
    late_rows = ROWS * LATE
    count = receivers // QUARTERS
    bf16, f32 = jnp.bfloat16, jnp.float32
    table = jnp.asarray(dft_master())
    smem, hbm = pl.BlockSpec(memory_space=pltpu.SMEM), pl.BlockSpec(memory_space=pltpu.HBM)

    message = local(
        tail_kernel,
        "tail_spectra",
        shape((late_rows + LATE, receivers), f32),
        [hbm] * 3,
        [
            pltpu.SMEM((shots,), jnp.int32),
            pltpu.VMEM(table.shape, f32),
            pltpu.VMEM((late, 2 * ROWS, SPAN), bf16),
            pltpu.VMEM((receivers, WIN), bf16),
            pltpu.SemaphoreType.DMA((3,)),
        ],
        limit=63,
    )(shot_fire_samples, table, record)

    def following(yh, u, k, xh, v):
        shot = ((yh << 4 | u << 2 | k) + 1) % SHOT_DEVICES
        return shot >> 4, (shot >> 2) & 3, shot & 3, xh, v

    received = send(message, following)
    total = local(
        own_kernel,
        "own_spectra",
        shape((lanes - late_rows, receivers), f32),
        [smem] + vmem(2),
        [pltpu.VMEM((pairs - late, 2 * ROWS, SPAN), bf16)],
    )(shot_fire_samples, table, record)
    y = pl.pallas_call(
        finish_kernel,
        grid=(1,),
        out_shape=shape((QUARTERS, count, lanes), bf16),
        in_specs=[
            pl.BlockSpec(total.shape, lambda i: (0, 0)),
            pl.BlockSpec((receivers, WIN), lambda i: (0, 0)),
            pl.BlockSpec(table.shape, lambda i: (0, 0)),
            pl.BlockSpec(received.shape, lambda i: (0, 0)),
        ],
        out_specs=pl.BlockSpec((QUARTERS, count, lanes), lambda i: (0, 0, 0)),
        scratch_shapes=[pltpu.VMEM((lanes, receivers), f32), pltpu.VMEM((late, 2 * ROWS, SPAN), bf16)],
        compiler_params=pltpu.CompilerParams(vmem_limit_bytes=4 << 20),
        name="finish_spectra",
    )(total, record, table, received)

    other = send(y, lambda yh, u, k, xh, v: (1 - yh, u, k, xh, v))
    y = local(yh_kernel, "join_yh", shape((2,) + y.shape, bf16), vmem(2))(y, other)
    other = send(y, lambda yh, u, k, xh, v: (yh, u, k ^ 2, xh, v))
    slices = shape((2, 2, count, lanes), bf16)
    y, mine, theirs = local(z0_kernel, "join_z0", (shape((2,) + y.shape, bf16), slices, slices), vmem(2))(y, other)

    def to_partner(yh, u, k, xh, v):
        return yh, u, k ^ 1, xh, v

    quarter = local(core_kernel, "join_core", shape((2,) + mine.shape, bf16), vmem(2))(mine, send(theirs, to_partner))
    cross = send(quarter, lambda yh, u, k, xh, v: (yh, u, k, 1 - xh, v))
    q = local(choose_kernel, "choose", shape(quarter.shape, bf16), vmem(2))(quarter, cross)
    qs = [q] + [send(q, lambda yh, u, k, xh, v, m=m: (yh, u, k, xh, v ^ m)) for m in (1, 2, 3)]
    right = local(right_kernel, "right_side", shape((2 * QUARTERS, 2 * receivers, lanes), bf16), vmem(2))(
        y, send(y, to_partner)
    )

    total_shots = shots * lax.axis_size("shot")
    rows = ROWS * count
    scale = 1.0 / total_shots
    share = shape((rows, receivers), f32)
    wire = shape((rows, receivers), bf16)
    early = []
    for m in (0, 3, 1):
        early += [
            local(
                lambda *refs: gram_kernel(scale, *refs),
                "gram",
                share,
                vmem(2) + [pl.BlockSpec(memory_space=pl.ANY)],
            )(right, qs[m], early[-1] if early else right)
        ]
    sums, p1, p2, p3 = local(
        lambda *refs: last_kernel(scale, *refs),
        "last_gram",
        (share, wire, wire, wire),
        vmem(5),
        [pltpu.VMEM((QUARTERS, rows, receivers), f32)],
    )(right, qs[2], *early)
    for n, p in ((1, p1), (2, p2), (3, p3)):
        sums = sums + send(p, lambda yh, u, k, xh, v, n=n: (yh, u ^ n, k, xh, v)).astype(f32)
    return sums.reshape(2, NF, count, receivers).transpose(0, 1, 3, 2)


def solution(mesh):
    return jax.shard_map(
        per_device,
        mesh=mesh,
        in_specs=(P("rcv", "shot"), P("shot")),
        out_specs=P(None, None, "rcv", "shot"),
        check_vma=False,
    )
```

```python
import math

import jax
import jax.numpy as jnp
import numpy as np
from jax import lax
from jax.experimental import pallas as pl
from jax.experimental.pallas import tpu as pltpu
from jax.sharding import PartitionSpec as P

import ml_dtypes

WIN = 2048
SPACING = 256
PAIR = 2 * SPACING
SPAN = WIN + PAIR
FREQ_BINS = (24, 40, 56, 80)
NF = len(FREQ_BINS)
ROWS = 2 * NF

SHOT_DEVICES = 32
RCV_DEVICES = 8
QUARTERS = 4
LATE = WIN // SPACING


def dft_master():
    turns = np.arange(WIN)[None, :] * np.array(FREQ_BINS)[:, None] % WIN
    angle = 2.0 * math.pi / WIN * turns
    rows = np.concatenate([np.cos(angle), -np.sin(angle)], axis=0) / math.sqrt(WIN)
    rows = rows.astype(np.float32).astype(ml_dtypes.bfloat16).astype(np.float32)
    return np.concatenate([rows, np.zeros((ROWS, SPAN - WIN), np.float32)], axis=1)


def send(block, to):
    route = []
    for shot in range(SHOT_DEVICES):
        for rcv in range(RCV_DEVICES):
            target = to(shot >> 4, (shot >> 2) & 3, shot & 3, rcv >> 2, rcv & 3)
            if target is not None:
                yh, u, k, xh, v = target
                route.append((shot * RCV_DEVICES + rcv, (yh << 4 | u << 2 | k) * RCV_DEVICES + (xh << 2 | v)))
    return lax.ppermute(block, ("shot", "rcv"), route)


shape = jax.ShapeDtypeStruct


def shot_index():
    return lax.axis_index("shot")


def vmem(count):
    return [pl.BlockSpec(memory_space=pltpu.VMEM)] * count


def pair_tables(table, first, second, length=SPAN):
    if length < SPAN:
        table = jnp.concatenate([table[:, :length], jnp.zeros((ROWS, PAIR), table.dtype)], axis=1)
    rows = [pltpu.roll(table, first, 1)[:, :length], pltpu.roll(table, second + SPACING, 1)[:, :length]]
    return jnp.concatenate(rows, axis=0).astype(jnp.bfloat16)


def delay(fire, shot):
    return fire[shot] & (SPACING - 1)


def add_products(total, tables, first_pair, blocks):
    reach = SPAN // PAIR
    last_pair = first_pair + tables.shape[0] - 1
    for u, samples in blocks:
        low, high = max(first_pair, u - reach + 1), min(u, last_pair)
        left = jnp.concatenate(
            [tables[p - first_pair, :, PAIR * (u - p) : PAIR * (u - p + 1)] for p in range(low, high + 1)], axis=0
        )
        part = lax.dot_general(left, samples, (((1,), (1,)), ((), ())), preferred_element_type=jnp.float32)
        total[2 * ROWS * (low - first_pair) : 2 * ROWS * (high + 1 - first_pair), :] += part


def tail_kernel(fire_hbm, table_hbm, record, message, fire, table, tables, samples, sems):
    pairs = fire.shape[0] // 2
    late = LATE // 2
    start = record.shape[1] - samples.shape[1]
    copies = [
        pltpu.make_async_copy(fire_hbm, fire, sems.at[0]),
        pltpu.make_async_copy(table_hbm, table, sems.at[1]),
        pltpu.make_async_copy(record.at[:, start:], samples, sems.at[2]),
    ]
    for copy in copies:
        copy.start()
    message[...] = jnp.zeros_like(message)
    copies[0].wait()
    row = lax.broadcasted_iota(jnp.int32, (LATE, message.shape[1]), 0)
    delays = jnp.zeros(row.shape, jnp.int32)
    for i in range(LATE):
        delays = jnp.where(row == i, delay(fire, 2 * (pairs - late) + i), delays)
    message[ROWS * LATE :, :] = delays.astype(jnp.float32)
    copies[1].wait()
    master = table[...]
    for p in range(late):
        shot = 2 * (pairs - late + p)
        length = PAIR * (late - p)
        tables[p, :, :length] = pair_tables(master, delay(fire, shot), delay(fire, shot + 1), length)
    copies[2].wait()
    blocks = [(pairs - late + v, samples[:, PAIR * v : PAIR * (v + 1)]) for v in range(late)]
    add_products(message, tables, pairs - late, blocks)


def own_kernel(fire, table, record, total, tables):
    pairs = record.shape[1] // PAIR
    master = table[...]
    for p in range(tables.shape[0]):
        tables[p] = pair_tables(master, delay(fire, 2 * p), delay(fire, 2 * p + 1))
    total[...] = jnp.zeros_like(total)
    add_products(total, tables, 0, [(u, record[:, PAIR * u : PAIR * (u + 1)]) for u in range(pairs)])


def finish_kernel(total, head, table, message, out, scratch, tables):
    own_rows = total.shape[0]
    lanes = scratch.shape[0]
    late = LATE // 2
    follows = (shot_index() > 0).astype(jnp.float32)
    master = table[...]
    for p in range(late):
        rows = [message[ROWS * LATE + 2 * p + i : ROWS * LATE + 2 * p + i + 1, :] for i in range(2)]
        first, second = [jnp.max(r).astype(jnp.int32) for r in rows]
        tables[p] = pair_tables(master, first, second)
    scratch[:own_rows, :] = jnp.zeros_like(total)
    scratch[own_rows:, :] = jnp.zeros((lanes - own_rows, total.shape[1]), jnp.float32)
    blocks = [(late + v, head[:, PAIR * v : PAIR * (v + 1)]) for v in range(late)]
    add_products(scratch.at[own_rows:, :], tables, 0, blocks)
    scratch[own_rows:, :] = message[: ROWS * LATE, :] + follows * scratch[own_rows:, :]
    scratch[:own_rows, :] = total[...]
    turn_over(scratch, out)


def turn_over(scratch, out):
    shots = scratch.shape[0] // ROWS
    ordered = jnp.concatenate([scratch[pl.ds(c, shots, stride=ROWS), :] for c in range(ROWS)], axis=0)
    turned = ordered.T
    count = out.shape[1]
    for k in range(QUARTERS):
        out[k] = turned[count * k : count * (k + 1), :].astype(out.dtype)


def yh_kernel(own, other, out):
    yh = shot_index() >> 4
    out[yh] = own[...]
    out[1 - yh] = other[...]


def z0_kernel(own, other, out, mine, theirs):
    k = shot_index() & 3
    z0 = k >> 1
    for here, block in ((z0, own), (1 - z0, other)):
        out[here] = block[...]
        mine[here] = block[:, k]
        theirs[here] = block[:, k ^ 1]


def core_kernel(own, other, out):
    c = shot_index() & 1
    out[c] = own[...]
    out[1 - c] = other[...]


def choose_kernel(own, cross, out):
    straight = (shot_index() >> 4) == (lax.axis_index("rcv") >> 2)

    @pl.when(straight)
    def _():
        out[...] = own[...]

    @pl.when(jnp.logical_not(straight))
    def _():
        out[...] = cross[...]


def right_kernel(own, other, right):
    c = shot_index() & 1
    half = right.shape[2] // 2
    parts = right.shape[0] // 2
    for here, block in ((c, own), (1 - c, other)):
        for part in range(parts):
            z = block[part >> 1, part & 1].astype(jnp.float32).reshape(right.shape[1] // 2, 2 * half)
            w = jnp.concatenate([-z[:, half:], z[:, :half]], axis=1)
            right[parts * here + part] = jnp.concatenate([z, w], axis=0).astype(jnp.bfloat16)


def products(scale, right, q):
    count, lanes = q.shape[3:]
    half = lanes // 2
    span = right.shape[1] // 2
    lane = lax.broadcasted_iota(jnp.int32, (count, lanes), 1) % half // (half // NF)
    acc = jnp.zeros((NF * count, 2 * span), jnp.float32)
    for part in range(right.shape[0]):
        rows = q[part >> 2, (part >> 1) & 1, part & 1].astype(jnp.float32)
        left = jnp.concatenate([jnp.where(lane == f, rows, 0.0) for f in range(NF)], axis=0)
        acc = acc + lax.dot_general(
            left.astype(jnp.bfloat16), right[part], (((1,), (1,)), ((), ())), preferred_element_type=jnp.float32
        )
    return jnp.concatenate([acc[:, :span] * scale, acc[:, span:] * scale], axis=0)


def gram_kernel(scale, right, q, before, out):
    out[...] = products(scale, right, q)


def last_kernel(scale, right, q, g0, g3, g1, p0, p1, p2, p3, total):
    turn = ((shot_index() >> 2) ^ lax.axis_index("rcv")) & 3
    total[turn] = g0[...]
    total[turn ^ 3] = g3[...]
    total[turn ^ 1] = g1[...]
    total[turn ^ 2] = products(scale, right, q)
    for n, out in enumerate((p0, p1, p2, p3)):
        out[...] = total[n].astype(out.dtype)


def local(kernel, name, out_shape, in_specs, scratch=(), limit=4):
    single = not isinstance(out_shape, tuple)
    return pl.pallas_call(
        kernel,
        out_shape=out_shape,
        in_specs=in_specs,
        out_specs=vmem(1)[0] if single else tuple(vmem(len(out_shape))),
        scratch_shapes=list(scratch),
        compiler_params=pltpu.CompilerParams(vmem_limit_bytes=limit << 20),
        name=name,
    )


def per_device(record, shot_fire_samples):
    receivers, samples = record.shape
    shots = shot_fire_samples.shape[0]
    pairs, late = shots // 2, LATE // 2
    lanes = ROWS * shots
    late_rows = ROWS * LATE
    count = receivers // QUARTERS
    bf16, f32 = jnp.bfloat16, jnp.float32
    table = jnp.asarray(dft_master())
    smem, hbm = pl.BlockSpec(memory_space=pltpu.SMEM), pl.BlockSpec(memory_space=pltpu.HBM)

    message = local(
        tail_kernel,
        "tail_spectra",
        shape((late_rows + LATE, receivers), f32),
        [hbm] * 3,
        [
            pltpu.SMEM((shots,), jnp.int32),
            pltpu.VMEM(table.shape, f32),
            pltpu.VMEM((late, 2 * ROWS, SPAN), bf16),
            pltpu.VMEM((receivers, WIN), bf16),
            pltpu.SemaphoreType.DMA((3,)),
        ],
    )(*(pltpu.with_memory_space_constraint(a, pltpu.HBM) for a in (shot_fire_samples, table, record)))

    def following(yh, u, k, xh, v):
        shot = ((yh << 4 | u << 2 | k) + 1) % SHOT_DEVICES
        return shot >> 4, (shot >> 2) & 3, shot & 3, xh, v

    received = send(message, following)
    total = local(
        own_kernel,
        "own_spectra",
        shape((lanes - late_rows, receivers), f32),
        [smem] + vmem(2),
        [pltpu.VMEM((pairs - late, 2 * ROWS, SPAN), bf16)],
    )(shot_fire_samples, table, record)
    y = pl.pallas_call(
        finish_kernel,
        grid=(1,),
        out_shape=shape((QUARTERS, count, lanes), bf16),
        in_specs=[
            pl.BlockSpec(total.shape, lambda i: (0, 0)),
            pl.BlockSpec((receivers, WIN), lambda i: (0, 0)),
            pl.BlockSpec(table.shape, lambda i: (0, 0)),
            pl.BlockSpec(received.shape, lambda i: (0, 0)),
        ],
        out_specs=pl.BlockSpec((QUARTERS, count, lanes), lambda i: (0, 0, 0)),
        scratch_shapes=[pltpu.VMEM((lanes, receivers), f32), pltpu.VMEM((late, 2 * ROWS, SPAN), bf16)],
        compiler_params=pltpu.CompilerParams(vmem_limit_bytes=4 << 20),
        name="finish_spectra",
    )(total, record, table, received)

    other = send(y, lambda yh, u, k, xh, v: (1 - yh, u, k, xh, v))
    y = local(yh_kernel, "join_yh", shape((2,) + y.shape, bf16), vmem(2))(y, other)
    other = send(y, lambda yh, u, k, xh, v: (yh, u, k ^ 2, xh, v))
    slices = shape((2, 2, count, lanes), bf16)
    y, mine, theirs = local(z0_kernel, "join_z0", (shape((2,) + y.shape, bf16), slices, slices), vmem(2))(y, other)

    def to_partner(yh, u, k, xh, v):
        return yh, u, k ^ 1, xh, v

    quarter = local(core_kernel, "join_core", shape((2,) + mine.shape, bf16), vmem(2))(mine, send(theirs, to_partner))
    cross = send(quarter, lambda yh, u, k, xh, v: (yh, u, k, 1 - xh, v))
    q = local(choose_kernel, "choose", shape(quarter.shape, bf16), vmem(2))(quarter, cross)
    qs = [q] + [send(q, lambda yh, u, k, xh, v, m=m: (yh, u, k, xh, v ^ m)) for m in (1, 2, 3)]
    right = local(right_kernel, "right_side", shape((2 * QUARTERS, 2 * receivers, lanes), bf16), vmem(2))(
        y, send(y, to_partner)
    )

    total_shots = shots * lax.axis_size("shot")
    rows = ROWS * count
    scale = 1.0 / total_shots
    share = shape((rows, receivers), f32)
    wire = shape((rows, receivers), bf16)
    early = []
    for m in (0, 3, 1):
        early += [
            local(
                lambda *refs: gram_kernel(scale, *refs),
                "gram",
                share,
                vmem(2) + [pl.BlockSpec(memory_space=pl.ANY)],
            )(right, qs[m], early[-1] if early else right)
        ]
    sums, p1, p2, p3 = local(
        lambda *refs: last_kernel(scale, *refs),
        "last_gram",
        (share, wire, wire, wire),
        vmem(5),
        [pltpu.VMEM((QUARTERS, rows, receivers), f32)],
    )(right, qs[2], *early)
    for n, p in ((1, p1), (2, p2), (3, p3)):
        sums = sums + send(p, lambda yh, u, k, xh, v, n=n: (yh, u ^ n, k, xh, v)).astype(f32)
    return sums.reshape(2, NF, count, receivers).transpose(0, 1, 3, 2)


def solution(mesh):
    return jax.shard_map(
        per_device,
        mesh=mesh,
        in_specs=(P("rcv", "shot"), P("shot")),
        out_specs=P(None, None, "rcv", "shot"),
        check_vma=False,
    )
```

```python
import math

import jax
import jax.numpy as jnp
import numpy as np
from jax import lax
from jax.experimental import pallas as pl
from jax.experimental.pallas import tpu as pltpu
from jax.sharding import PartitionSpec as P

import ml_dtypes

WIN = 2048
SPACING = 256
PAIR = 2 * SPACING
SPAN = WIN + PAIR
FREQ_BINS = (24, 40, 56, 80)
NF = len(FREQ_BINS)
ROWS = 2 * NF

SHOT_DEVICES = 32
RCV_DEVICES = 8
QUARTERS = 4
LATE = WIN // SPACING


def dft_master():
    turns = np.arange(WIN)[None, :] * np.array(FREQ_BINS)[:, None] % WIN
    angle = 2.0 * math.pi / WIN * turns
    rows = np.concatenate([np.cos(angle), -np.sin(angle)], axis=0) / math.sqrt(WIN)
    rows = rows.astype(np.float32).astype(ml_dtypes.bfloat16).astype(np.float32)
    return np.concatenate([rows, np.zeros((ROWS, SPAN - WIN), np.float32)], axis=1)


def send(block, to):
    route = []
    for shot in range(SHOT_DEVICES):
        for rcv in range(RCV_DEVICES):
            target = to(shot >> 4, (shot >> 2) & 3, shot & 3, rcv >> 2, rcv & 3)
            if target is not None:
                yh, u, k, xh, v = target
                route.append((shot * RCV_DEVICES + rcv, (yh << 4 | u << 2 | k) * RCV_DEVICES + (xh << 2 | v)))
    return lax.ppermute(block, ("shot", "rcv"), route)


shape = jax.ShapeDtypeStruct


def shot_index():
    return lax.axis_index("shot")


def vmem(count):
    return [pl.BlockSpec(memory_space=pltpu.VMEM)] * count


def pair_tables(table, first, second, length=SPAN):
    if length < SPAN:
        table = jnp.concatenate([table[:, :length], jnp.zeros((ROWS, PAIR), table.dtype)], axis=1)
    rows = [pltpu.roll(table, first, 1)[:, :length], pltpu.roll(table, second + SPACING, 1)[:, :length]]
    return jnp.concatenate(rows, axis=0).astype(jnp.bfloat16)


def delay(fire, shot):
    return fire[shot] & (SPACING - 1)


def add_products(total, tables, first_pair, blocks):
    reach = SPAN // PAIR
    last_pair = first_pair + tables.shape[0] - 1
    for u, samples in blocks:
        low, high = max(first_pair, u - reach + 1), min(u, last_pair)
        left = jnp.concatenate(
            [tables[p - first_pair, :, PAIR * (u - p) : PAIR * (u - p + 1)] for p in range(low, high + 1)], axis=0
        )
        part = lax.dot_general(left, samples, (((1,), (1,)), ((), ())), preferred_element_type=jnp.float32)
        total[2 * ROWS * (low - first_pair) : 2 * ROWS * (high + 1 - first_pair), :] += part


def tail_kernel(fire_hbm, table_hbm, record, message, fire, table, tables, samples, sems):
    pairs = fire.shape[0] // 2
    late = LATE // 2
    start = record.shape[1] - samples.shape[1]
    copies = [
        pltpu.make_async_copy(fire_hbm, fire, sems.at[0]),
        pltpu.make_async_copy(table_hbm, table, sems.at[1]),
        pltpu.make_async_copy(record.at[:, start:], samples, sems.at[2]),
    ]
    for copy in copies:
        copy.start()
    message[...] = jnp.zeros_like(message)
    copies[0].wait()
    row = lax.broadcasted_iota(jnp.int32, (LATE, message.shape[1]), 0)
    delays = jnp.zeros(row.shape, jnp.int32)
    for i in range(LATE):
        delays = jnp.where(row == i, delay(fire, 2 * (pairs - late) + i), delays)
    message[ROWS * LATE :, :] = delays.astype(jnp.float32)
    copies[1].wait()
    master = table[...]
    for p in range(late):
        shot = 2 * (pairs - late + p)
        length = PAIR * (late - p)
        tables[p, :, :length] = pair_tables(master, delay(fire, shot), delay(fire, shot + 1), length)
    copies[2].wait()
    blocks = [(pairs - late + v, samples[:, PAIR * v : PAIR * (v + 1)]) for v in range(late)]
    add_products(message, tables, pairs - late, blocks)


def own_kernel(fire, table, record, total, tables):
    pairs = record.shape[1] // PAIR
    master = table[...]
    for p in range(tables.shape[0]):
        tables[p] = pair_tables(master, delay(fire, 2 * p), delay(fire, 2 * p + 1))
    total[...] = jnp.zeros_like(total)
    add_products(total, tables, 0, [(u, record[:, PAIR * u : PAIR * (u + 1)]) for u in range(pairs)])


def finish_kernel(total, head, table, message, out, scratch, tables):
    own_rows = total.shape[0]
    lanes = scratch.shape[0]
    late = LATE // 2
    follows = (shot_index() > 0).astype(jnp.float32)
    master = table[...]
    for p in range(late):
        rows = [message[ROWS * LATE + 2 * p + i : ROWS * LATE + 2 * p + i + 1, :] for i in range(2)]
        first, second = [jnp.max(r).astype(jnp.int32) for r in rows]
        tables[p] = pair_tables(master, first, second)
    scratch[:own_rows, :] = jnp.zeros_like(total)
    scratch[own_rows:, :] = jnp.zeros((lanes - own_rows, total.shape[1]), jnp.float32)
    blocks = [(late + v, head[:, PAIR * v : PAIR * (v + 1)]) for v in range(late)]
    add_products(scratch.at[own_rows:, :], tables, 0, blocks)
    scratch[own_rows:, :] = message[: ROWS * LATE, :] + follows * scratch[own_rows:, :]
    scratch[:own_rows, :] = total[...]
    turn_over(scratch, out)


def turn_over(scratch, out):
    shots = scratch.shape[0] // ROWS
    ordered = jnp.concatenate([scratch[pl.ds(c, shots, stride=ROWS), :] for c in range(ROWS)], axis=0)
    turned = ordered.T
    count = out.shape[1]
    for k in range(QUARTERS):
        out[k] = turned[count * k : count * (k + 1), :].astype(out.dtype)


def join_kernel(y3, y2, y1, y0, out, mine, theirs):
    shot = shot_index()
    yh, k = shot >> 4, shot & 3
    z0 = k >> 1
    for m, block in enumerate((y0, y1, y2, y3)):
        place = z0 ^ (m & 1), yh ^ (m >> 1)
        out[place] = block[...]
        mine[place] = block[k]
        theirs[place] = block[k ^ 1]


def core_kernel(own, other, out):
    c = shot_index() & 1
    out[c] = own[...]
    out[1 - c] = other[...]


def choose_kernel(own, cross, out):
    straight = (shot_index() >> 4) == (lax.axis_index("rcv") >> 2)

    @pl.when(straight)
    def _():
        out[...] = own[...]

    @pl.when(jnp.logical_not(straight))
    def _():
        out[...] = cross[...]


def right_kernel(own, other, right):
    c = shot_index() & 1
    half = right.shape[2] // 2
    parts = right.shape[0] // 2
    for here, block in ((c, own), (1 - c, other)):
        for part in range(parts):
            z = block[part >> 1, part & 1].astype(jnp.float32).reshape(right.shape[1] // 2, 2 * half)
            w = jnp.concatenate([-z[:, half:], z[:, :half]], axis=1)
            right[parts * here + part] = jnp.concatenate([z, w], axis=0).astype(jnp.bfloat16)


def products(scale, right, q):
    count, lanes = q.shape[3:]
    half = lanes // 2
    span = right.shape[1] // 2
    lane = lax.broadcasted_iota(jnp.int32, (count, lanes), 1) % half // (half // NF)
    acc = jnp.zeros((NF * count, 2 * span), jnp.float32)
    for part in range(right.shape[0]):
        rows = q[part >> 2, (part >> 1) & 1, part & 1].astype(jnp.float32)
        left = jnp.concatenate([jnp.where(lane == f, rows, 0.0) for f in range(NF)], axis=0)
        acc = acc + lax.dot_general(
            left.astype(jnp.bfloat16), right[part], (((1,), (1,)), ((), ())), preferred_element_type=jnp.float32
        )
    return jnp.concatenate([acc[:, :span] * scale, acc[:, span:] * scale], axis=0)


def gram_kernel(scale, right, q, before, out):
    out[...] = products(scale, right, q)


def last_kernel(scale, right, q, g0, g3, g1, p0, p1, p2, p3, total):
    turn = ((shot_index() >> 2) ^ lax.axis_index("rcv")) & 3
    total[turn] = g0[...]
    total[turn ^ 3] = g3[...]
    total[turn ^ 1] = g1[...]
    total[turn ^ 2] = products(scale, right, q)
    for n, out in enumerate((p0, p1, p2, p3)):
        out[...] = total[n].astype(out.dtype)


def local(kernel, name, out_shape, in_specs, scratch=(), limit=4):
    single = not isinstance(out_shape, tuple)
    return pl.pallas_call(
        kernel,
        out_shape=out_shape,
        in_specs=in_specs,
        out_specs=vmem(1)[0] if single else tuple(vmem(len(out_shape))),
        scratch_shapes=list(scratch),
        compiler_params=pltpu.CompilerParams(vmem_limit_bytes=limit << 20),
        name=name,
    )


def per_device(record, shot_fire_samples):
    receivers, samples = record.shape
    shots = shot_fire_samples.shape[0]
    pairs, late = shots // 2, LATE // 2
    lanes = ROWS * shots
    late_rows = ROWS * LATE
    count = receivers // QUARTERS
    bf16, f32 = jnp.bfloat16, jnp.float32
    table = jnp.asarray(dft_master())
    smem, hbm = pl.BlockSpec(memory_space=pltpu.SMEM), pl.BlockSpec(memory_space=pltpu.HBM)

    message = local(
        tail_kernel,
        "tail_spectra",
        shape((late_rows + LATE, receivers), f32),
        [hbm] * 3,
        [
            pltpu.SMEM((shots,), jnp.int32),
            pltpu.VMEM(table.shape, f32),
            pltpu.VMEM((late, 2 * ROWS, SPAN), bf16),
            pltpu.VMEM((receivers, WIN), bf16),
            pltpu.SemaphoreType.DMA((3,)),
        ],
    )(*(pltpu.with_memory_space_constraint(a, pltpu.HBM) for a in (shot_fire_samples, table, record)))

    def following(yh, u, k, xh, v):
        shot = ((yh << 4 | u << 2 | k) + 1) % SHOT_DEVICES
        return shot >> 4, (shot >> 2) & 3, shot & 3, xh, v

    received = send(message, following)
    total = local(
        own_kernel,
        "own_spectra",
        shape((lanes - late_rows, receivers), f32),
        [smem] + vmem(2),
        [pltpu.VMEM((pairs - late, 2 * ROWS, SPAN), bf16)],
    )(shot_fire_samples, table, record)
    y = pl.pallas_call(
        finish_kernel,
        grid=(1,),
        out_shape=shape((QUARTERS, count, lanes), bf16),
        in_specs=[
            pl.BlockSpec(total.shape, lambda i: (0, 0)),
            pl.BlockSpec((receivers, WIN), lambda i: (0, 0)),
            pl.BlockSpec(table.shape, lambda i: (0, 0)),
            pl.BlockSpec(received.shape, lambda i: (0, 0)),
        ],
        out_specs=pl.BlockSpec((QUARTERS, count, lanes), lambda i: (0, 0, 0)),
        scratch_shapes=[pltpu.VMEM((lanes, receivers), f32), pltpu.VMEM((late, 2 * ROWS, SPAN), bf16)],
        compiler_params=pltpu.CompilerParams(vmem_limit_bytes=4 << 20),
        name="finish_spectra",
    )(total, record, table, received)

    y3, y2, y1 = [send(y, lambda yh, u, k, xh, v, m=m: (yh ^ m >> 1, u, k ^ (m & 1) << 1, xh, v)) for m in (3, 2, 1)]
    slices = shape((2, 2, count, lanes), bf16)
    y, mine, theirs = local(join_kernel, "join", (shape((2, 2) + y.shape, bf16), slices, slices), vmem(4))(
        y3, y2, y1, y
    )

    def to_partner(yh, u, k, xh, v):
        return yh, u, k ^ 1, xh, v

    quarter = local(core_kernel, "join_core", shape((2,) + mine.shape, bf16), vmem(2))(mine, send(theirs, to_partner))
    cross = send(quarter, lambda yh, u, k, xh, v: (yh, u, k, 1 - xh, v))
    q = local(choose_kernel, "choose", shape(quarter.shape, bf16), vmem(2))(quarter, cross)
    qs = [q] + [send(q, lambda yh, u, k, xh, v, m=m: (yh, u, k, xh, v ^ m)) for m in (1, 2, 3)]
    right = local(right_kernel, "right_side", shape((2 * QUARTERS, 2 * receivers, lanes), bf16), vmem(2))(
        y, send(y, to_partner)
    )

    total_shots = shots * lax.axis_size("shot")
    rows = ROWS * count
    scale = 1.0 / total_shots
    share = shape((rows, receivers), f32)
    wire = shape((rows, receivers), bf16)
    early = []
    for m in (0, 3, 1):
        early += [
            local(
                lambda *refs: gram_kernel(scale, *refs),
                "gram",
                share,
                vmem(2) + [pl.BlockSpec(memory_space=pl.ANY)],
            )(right, qs[m], early[-1] if early else right)
        ]
    sums, p1, p2, p3 = local(
        lambda *refs: last_kernel(scale, *refs),
        "last_gram",
        (share, wire, wire, wire),
        vmem(5),
        [pltpu.VMEM((QUARTERS, rows, receivers), f32)],
    )(right, qs[2], *early)
    for n, p in ((1, p1), (2, p2), (3, p3)):
        sums = sums + send(p, lambda yh, u, k, xh, v, n=n: (yh, u ^ n, k, xh, v)).astype(f32)
    return sums.reshape(2, NF, count, receivers).transpose(0, 1, 3, 2)


def solution(mesh):
    return jax.shard_map(
        per_device,
        mesh=mesh,
        in_specs=(P("rcv", "shot"), P("shot")),
        out_specs=P(None, None, "rcv", "shot"),
        check_vma=False,
    )
```

```python
import math

import jax
import jax.numpy as jnp
import numpy as np
from jax import lax
from jax.experimental import pallas as pl
from jax.experimental.pallas import tpu as pltpu
from jax.sharding import PartitionSpec as P

import ml_dtypes

WIN = 2048
SPACING = 256
PAIR = 2 * SPACING
SPAN = WIN + PAIR
FREQ_BINS = (24, 40, 56, 80)
NF = len(FREQ_BINS)
ROWS = 2 * NF

SHOT_DEVICES = 32
RCV_DEVICES = 8
QUARTERS = 4
LATE = WIN // SPACING


def dft_master():
    turns = np.arange(WIN)[None, :] * np.array(FREQ_BINS)[:, None] % WIN
    angle = 2.0 * math.pi / WIN * turns
    rows = np.concatenate([np.cos(angle), -np.sin(angle)], axis=0) / math.sqrt(WIN)
    rows = rows.astype(np.float32).astype(ml_dtypes.bfloat16).astype(np.float32)
    return np.concatenate([rows, np.zeros((ROWS, SPAN - WIN), np.float32)], axis=1)


def send(block, to):
    route = []
    for shot in range(SHOT_DEVICES):
        for rcv in range(RCV_DEVICES):
            target = to(shot >> 4, (shot >> 2) & 3, shot & 3, rcv >> 2, rcv & 3)
            if target is not None:
                yh, u, k, xh, v = target
                route.append((shot * RCV_DEVICES + rcv, (yh << 4 | u << 2 | k) * RCV_DEVICES + (xh << 2 | v)))
    return lax.ppermute(block, ("shot", "rcv"), route)


shape = jax.ShapeDtypeStruct


def shot_index():
    return lax.axis_index("shot")


def vmem(count):
    return [pl.BlockSpec(memory_space=pltpu.VMEM)] * count


def pair_tables(table, first, second, length=SPAN):
    if length < SPAN:
        table = jnp.concatenate([table[:, :length], jnp.zeros((ROWS, PAIR), table.dtype)], axis=1)
    rows = [pltpu.roll(table, first, 1)[:, :length], pltpu.roll(table, second + SPACING, 1)[:, :length]]
    return jnp.concatenate(rows, axis=0).astype(jnp.bfloat16)


def delay(fire, shot):
    return fire[shot] & (SPACING - 1)


def add_products(total, tables, first_pair, blocks):
    reach = SPAN // PAIR
    last_pair = first_pair + tables.shape[0] - 1
    for u, samples in blocks:
        low, high = max(first_pair, u - reach + 1), min(u, last_pair)
        left = jnp.concatenate(
            [tables[p - first_pair, :, PAIR * (u - p) : PAIR * (u - p + 1)] for p in range(low, high + 1)], axis=0
        )
        part = lax.dot_general(left, samples, (((1,), (1,)), ((), ())), preferred_element_type=jnp.float32)
        total[2 * ROWS * (low - first_pair) : 2 * ROWS * (high + 1 - first_pair), :] += part


def tail_kernel(fire_hbm, table_hbm, record, message, fire, table, tables, samples, sems):
    pairs = fire.shape[0] // 2
    late = LATE // 2
    start = record.shape[1] - samples.shape[1]
    copies = [
        pltpu.make_async_copy(fire_hbm, fire, sems.at[0]),
        pltpu.make_async_copy(table_hbm, table, sems.at[1]),
        pltpu.make_async_copy(record.at[:, start:], samples, sems.at[2]),
    ]
    for copy in copies:
        copy.start()
    message[...] = jnp.zeros_like(message)
    copies[0].wait()
    row = lax.broadcasted_iota(jnp.int32, (LATE, message.shape[1]), 0)
    delays = jnp.zeros(row.shape, jnp.int32)
    for i in range(LATE):
        delays = jnp.where(row == i, delay(fire, 2 * (pairs - late) + i), delays)
    message[ROWS * LATE :, :] = delays.astype(jnp.float32)
    copies[1].wait()
    master = table[...]
    for p in range(late):
        shot = 2 * (pairs - late + p)
        length = PAIR * (late - p)
        tables[p, :, :length] = pair_tables(master, delay(fire, shot), delay(fire, shot + 1), length)
    copies[2].wait()
    blocks = [(pairs - late + v, samples[:, PAIR * v : PAIR * (v + 1)]) for v in range(late)]
    add_products(message, tables, pairs - late, blocks)


def own_kernel(fire, table, record, total, tables):
    pairs = record.shape[1] // PAIR
    master = table[...]
    for p in range(tables.shape[0]):
        tables[p] = pair_tables(master, delay(fire, 2 * p), delay(fire, 2 * p + 1))
    total[...] = jnp.zeros_like(total)
    add_products(total, tables, 0, [(u, record[:, PAIR * u : PAIR * (u + 1)]) for u in range(pairs)])


def finish_kernel(total, head, table, message, out, scratch, tables):
    own_rows = total.shape[0]
    lanes = scratch.shape[0]
    late = LATE // 2
    follows = (shot_index() > 0).astype(jnp.float32)
    master = table[...]
    for p in range(late):
        rows = [message[ROWS * LATE + 2 * p + i : ROWS * LATE + 2 * p + i + 1, :] for i in range(2)]
        first, second = [jnp.max(r).astype(jnp.int32) for r in rows]
        tables[p] = pair_tables(master, first, second)
    scratch[:own_rows, :] = jnp.zeros_like(total)
    scratch[own_rows:, :] = jnp.zeros((lanes - own_rows, total.shape[1]), jnp.float32)
    blocks = [(late + v, head[:, PAIR * v : PAIR * (v + 1)]) for v in range(late)]
    add_products(scratch.at[own_rows:, :], tables, 0, blocks)
    scratch[own_rows:, :] = message[: ROWS * LATE, :] + follows * scratch[own_rows:, :]
    scratch[:own_rows, :] = total[...]
    turn_over(scratch, out)


def turn_over(scratch, out):
    shots = scratch.shape[0] // ROWS
    ordered = jnp.concatenate([scratch[pl.ds(c, shots, stride=ROWS), :] for c in range(ROWS)], axis=0)
    turned = ordered.T
    count = out.shape[1]
    for k in range(QUARTERS):
        out[k] = turned[count * k : count * (k + 1), :].astype(out.dtype)


def join_kernel(y3, y2, y1, y0, out, mine, theirs):
    shot = shot_index()
    yh, k = shot >> 4, shot & 3
    z0 = k >> 1
    for m, block in enumerate((y0, y1, y2, y3)):
        place = z0 ^ (m & 1), yh ^ (m >> 1)
        out[place] = block[...]
        mine[place] = block[k]
        theirs[place] = block[k ^ 1]


def core_kernel(own, other, out):
    c = shot_index() & 1
    out[c] = own[...]
    out[1 - c] = other[...]


def choose_kernel(own, cross, out):
    straight = (shot_index() >> 4) == (lax.axis_index("rcv") >> 2)

    @pl.when(straight)
    def _():
        out[...] = own[...]

    @pl.when(jnp.logical_not(straight))
    def _():
        out[...] = cross[...]


def right_kernel(own, other, right):
    c = shot_index() & 1
    half = right.shape[2] // 2
    parts = right.shape[0] // 2
    for here, block in ((c, own), (1 - c, other)):
        for part in range(parts):
            z = block[part >> 1, part & 1].astype(jnp.float32).reshape(right.shape[1] // 2, 2 * half)
            w = jnp.concatenate([-z[:, half:], z[:, :half]], axis=1)
            right[parts * here + part] = jnp.concatenate([z, w], axis=0).astype(jnp.bfloat16)


def products(scale, right, q):
    count, lanes = q.shape[3:]
    half = lanes // 2
    span = right.shape[1] // 2
    lane = lax.broadcasted_iota(jnp.int32, (count, lanes), 1) % half // (half // NF)
    acc = jnp.zeros((NF * count, 2 * span), jnp.float32)
    for part in range(right.shape[0]):
        rows = q[part >> 2, (part >> 1) & 1, part & 1].astype(jnp.float32)
        left = jnp.concatenate([jnp.where(lane == f, rows, 0.0) for f in range(NF)], axis=0)
        acc = acc + lax.dot_general(
            left.astype(jnp.bfloat16), right[part], (((1,), (1,)), ((), ())), preferred_element_type=jnp.float32
        )
    return jnp.concatenate([acc[:, :span] * scale, acc[:, span:] * scale], axis=0)


def gram_kernel(scale, right, q, before, out):
    out[...] = products(scale, right, q)


def last_kernel(scale, right, q, g0, g3, g1, p0, p1, p2, p3, total):
    turn = ((shot_index() >> 2) ^ lax.axis_index("rcv")) & 3
    total[turn] = g0[...]
    total[turn ^ 3] = g3[...]
    total[turn ^ 1] = g1[...]
    total[turn ^ 2] = products(scale, right, q)
    p0[...] = total[0]
    for n, out in ((1, p1), (2, p2), (3, p3)):
        pack(total[n], out)


def pack(share, out):
    rows, width = out.shape
    lanes = share.shape[1]
    rest = width - lanes
    out[:, :lanes] = share[:rows].astype(out.dtype)
    pieces = [share[rows:, rest * g : rest * (g + 1)] for g in range(lanes // rest)]
    out[:, lanes:] = jnp.concatenate(pieces, axis=0).astype(out.dtype)


def sum_kernel(r2, r3, r1, p0, out):
    shares = r1[...].astype(jnp.float32) + r2[...].astype(jnp.float32) + r3[...].astype(jnp.float32)
    rows = shares.shape[0]
    lanes = out.shape[1]
    high = out.shape[0] - rows
    out[:rows] = p0[:rows] + shares[:, :lanes]
    pieces = [shares[high * g : high * (g + 1), lanes:] for g in range(rows // high)]
    out[rows:] = p0[rows:] + jnp.concatenate(pieces, axis=1)


def local(kernel, name, out_shape, in_specs, scratch=(), limit=4):
    single = not isinstance(out_shape, tuple)
    return pl.pallas_call(
        kernel,
        out_shape=out_shape,
        in_specs=in_specs,
        out_specs=vmem(1)[0] if single else tuple(vmem(len(out_shape))),
        scratch_shapes=list(scratch),
        compiler_params=pltpu.CompilerParams(vmem_limit_bytes=limit << 20),
        name=name,
    )


def per_device(record, shot_fire_samples):
    receivers, samples = record.shape
    shots = shot_fire_samples.shape[0]
    pairs, late = shots // 2, LATE // 2
    lanes = ROWS * shots
    late_rows = ROWS * LATE
    count = receivers // QUARTERS
    bf16, f32 = jnp.bfloat16, jnp.float32
    table = jnp.asarray(dft_master())
    smem, hbm = pl.BlockSpec(memory_space=pltpu.SMEM), pl.BlockSpec(memory_space=pltpu.HBM)

    message = local(
        tail_kernel,
        "tail_spectra",
        shape((late_rows + LATE, receivers), f32),
        [hbm] * 3,
        [
            pltpu.SMEM((shots,), jnp.int32),
            pltpu.VMEM(table.shape, f32),
            pltpu.VMEM((late, 2 * ROWS, SPAN), bf16),
            pltpu.VMEM((receivers, WIN), bf16),
            pltpu.SemaphoreType.DMA((3,)),
        ],
    )(*(pltpu.with_memory_space_constraint(a, pltpu.HBM) for a in (shot_fire_samples, table, record)))

    def following(yh, u, k, xh, v):
        shot = ((yh << 4 | u << 2 | k) + 1) % SHOT_DEVICES
        return shot >> 4, (shot >> 2) & 3, shot & 3, xh, v

    received = send(message, following)
    total = local(
        own_kernel,
        "own_spectra",
        shape((lanes - late_rows, receivers), f32),
        [smem] + vmem(2),
        [pltpu.VMEM((pairs - late, 2 * ROWS, SPAN), bf16)],
    )(shot_fire_samples, table, record)
    y = pl.pallas_call(
        finish_kernel,
        grid=(1,),
        out_shape=shape((QUARTERS, count, lanes), bf16),
        in_specs=[
            pl.BlockSpec(total.shape, lambda i: (0, 0)),
            pl.BlockSpec((receivers, WIN), lambda i: (0, 0)),
            pl.BlockSpec(table.shape, lambda i: (0, 0)),
            pl.BlockSpec(received.shape, lambda i: (0, 0)),
        ],
        out_specs=pl.BlockSpec((QUARTERS, count, lanes), lambda i: (0, 0, 0)),
        scratch_shapes=[pltpu.VMEM((lanes, receivers), f32), pltpu.VMEM((late, 2 * ROWS, SPAN), bf16)],
        compiler_params=pltpu.CompilerParams(vmem_limit_bytes=4 << 20),
        name="finish_spectra",
    )(total, record, table, received)

    y3, y2, y1 = [send(y, lambda yh, u, k, xh, v, m=m: (yh ^ m >> 1, u, k ^ (m & 1) << 1, xh, v)) for m in (3, 2, 1)]
    slices = shape((2, 2, count, lanes), bf16)
    y, mine, theirs = local(join_kernel, "join", (shape((2, 2) + y.shape, bf16), slices, slices), vmem(4))(
        y3, y2, y1, y
    )

    def to_partner(yh, u, k, xh, v):
        return yh, u, k ^ 1, xh, v

    quarter = local(core_kernel, "join_core", shape((2,) + mine.shape, bf16), vmem(2))(mine, send(theirs, to_partner))
    cross = send(quarter, lambda yh, u, k, xh, v: (yh, u, k, 1 - xh, v))
    q = local(choose_kernel, "choose", shape(quarter.shape, bf16), vmem(2))(quarter, cross)
    qs = [q] + [send(q, lambda yh, u, k, xh, v, m=m: (yh, u, k, xh, v ^ m)) for m in (1, 2, 3)]
    right = local(right_kernel, "right_side", shape((2 * QUARTERS, 2 * receivers, lanes), bf16), vmem(2))(
        y, send(y, to_partner)
    )

    total_shots = shots * lax.axis_size("shot")
    rows = ROWS * count
    scale = 1.0 / total_shots
    share = shape((rows, receivers), f32)
    width = 128
    wire = shape((rows * receivers // width, width), bf16)
    early = []
    for m in (0, 3, 1):
        early += [
            local(
                lambda *refs: gram_kernel(scale, *refs),
                "gram",
                share,
                vmem(2) + [pl.BlockSpec(memory_space=pl.ANY)],
            )(right, qs[m], early[-1] if early else right)
        ]
    p0, p1, p2, p3 = local(
        lambda *refs: last_kernel(scale, *refs),
        "last_gram",
        (share, wire, wire, wire),
        vmem(5),
        [pltpu.VMEM((QUARTERS, rows, receivers), f32)],
    )(right, qs[2], *early)
    r1, r2, r3 = [send(p, lambda yh, u, k, xh, v, n=n: (yh, u ^ n, k, xh, v)) for n, p in ((1, p1), (2, p2), (3, p3))]
    sums = local(sum_kernel, "sum", share, vmem(4))(r2, r3, r1, p0)
    return sums.reshape(2, NF, count, receivers).transpose(0, 1, 3, 2)


def solution(mesh):
    return jax.shard_map(
        per_device,
        mesh=mesh,
        in_specs=(P("rcv", "shot"), P("shot")),
        out_specs=P(None, None, "rcv", "shot"),
        check_vma=False,
    )
```

```python
import math

import jax
import jax.numpy as jnp
import numpy as np
from jax import lax
from jax.experimental import pallas as pl
from jax.experimental.pallas import tpu as pltpu
from jax.sharding import PartitionSpec as P

import ml_dtypes

WIN = 2048
SPACING = 256
PAIR = 2 * SPACING
SPAN = WIN + PAIR
FREQ_BINS = (24, 40, 56, 80)
NF = len(FREQ_BINS)
ROWS = 2 * NF

SHOT_DEVICES = 32
RCV_DEVICES = 8
QUARTERS = 4
LATE = WIN // SPACING


def dft_master():
    turns = np.arange(WIN)[None, :] * np.array(FREQ_BINS)[:, None] % WIN
    angle = 2.0 * math.pi / WIN * turns
    rows = np.concatenate([np.cos(angle), -np.sin(angle)], axis=0) / math.sqrt(WIN)
    rows = rows.astype(np.float32).astype(ml_dtypes.bfloat16).astype(np.float32)
    return np.concatenate([rows, np.zeros((ROWS, SPAN - WIN), np.float32)], axis=1)


def send(block, to):
    route = []
    for shot in range(SHOT_DEVICES):
        for rcv in range(RCV_DEVICES):
            target = to(shot >> 4, (shot >> 2) & 3, shot & 3, rcv >> 2, rcv & 3)
            if target is not None:
                yh, u, k, xh, v = target
                route.append((shot * RCV_DEVICES + rcv, (yh << 4 | u << 2 | k) * RCV_DEVICES + (xh << 2 | v)))
    return lax.ppermute(block, ("shot", "rcv"), route)


shape = jax.ShapeDtypeStruct


def shot_index():
    return lax.axis_index("shot")


def vmem(count):
    return [pl.BlockSpec(memory_space=pltpu.VMEM)] * count


def pair_tables(table, first, second, length=SPAN):
    if length < SPAN:
        table = jnp.concatenate([table[:, :length], jnp.zeros((ROWS, PAIR), table.dtype)], axis=1)
    rows = [pltpu.roll(table, first, 1)[:, :length], pltpu.roll(table, second + SPACING, 1)[:, :length]]
    return jnp.concatenate(rows, axis=0).astype(jnp.bfloat16)


def delay(fire, shot):
    return fire[shot] & (SPACING - 1)


def add_products(total, tables, first_pair, blocks):
    reach = SPAN // PAIR
    last_pair = first_pair + tables.shape[0] - 1
    for u, samples in blocks:
        low, high = max(first_pair, u - reach + 1), min(u, last_pair)
        left = jnp.concatenate(
            [tables[p - first_pair, :, PAIR * (u - p) : PAIR * (u - p + 1)] for p in range(low, high + 1)], axis=0
        )
        part = lax.dot_general(left, samples, (((1,), (1,)), ((), ())), preferred_element_type=jnp.float32)
        total[2 * ROWS * (low - first_pair) : 2 * ROWS * (high + 1 - first_pair), :] += part


def tail_kernel(fire_hbm, table_hbm, record, message, fire, table, tables, samples, sems):
    pairs = fire.shape[0] // 2
    late = LATE // 2
    start = record.shape[1] - samples.shape[1]
    copies = [
        pltpu.make_async_copy(fire_hbm, fire, sems.at[0]),
        pltpu.make_async_copy(table_hbm, table, sems.at[1]),
        pltpu.make_async_copy(record.at[:, start:], samples, sems.at[2]),
    ]
    for copy in copies:
        copy.start()
    message[...] = jnp.zeros_like(message)
    copies[0].wait()
    row = lax.broadcasted_iota(jnp.int32, (LATE, message.shape[1]), 0)
    delays = jnp.zeros(row.shape, jnp.int32)
    for i in range(LATE):
        delays = jnp.where(row == i, delay(fire, 2 * (pairs - late) + i), delays)
    message[ROWS * LATE :, :] = delays.astype(jnp.float32)
    copies[1].wait()
    master = table[...]
    for p in range(late):
        shot = 2 * (pairs - late + p)
        length = PAIR * (late - p)
        tables[p, :, :length] = pair_tables(master, delay(fire, shot), delay(fire, shot + 1), length)
    copies[2].wait()
    blocks = [(pairs - late + v, samples[:, PAIR * v : PAIR * (v + 1)]) for v in range(late)]
    add_products(message, tables, pairs - late, blocks)


def own_kernel(fire, table, record, total, tables):
    pairs = record.shape[1] // PAIR
    master = table[...]
    for p in range(tables.shape[0]):
        tables[p] = pair_tables(master, delay(fire, 2 * p), delay(fire, 2 * p + 1))
    total[...] = jnp.zeros_like(total)
    add_products(total, tables, 0, [(u, record[:, PAIR * u : PAIR * (u + 1)]) for u in range(pairs)])


def finish_kernel(total, head, table, message, out, scratch, tables):
    own_rows = total.shape[0]
    lanes = scratch.shape[0]
    late = LATE // 2
    follows = (shot_index() > 0).astype(jnp.float32)
    master = table[...]
    for p in range(late):
        rows = [message[ROWS * LATE + 2 * p + i : ROWS * LATE + 2 * p + i + 1, :] for i in range(2)]
        first, second = [jnp.max(r).astype(jnp.int32) for r in rows]
        tables[p] = pair_tables(master, first, second)
    scratch[:own_rows, :] = jnp.zeros_like(total)
    scratch[own_rows:, :] = jnp.zeros((lanes - own_rows, total.shape[1]), jnp.float32)
    blocks = [(late + v, head[:, PAIR * v : PAIR * (v + 1)]) for v in range(late)]
    add_products(scratch.at[own_rows:, :], tables, 0, blocks)
    scratch[own_rows:, :] = message[: ROWS * LATE, :] + follows * scratch[own_rows:, :]
    scratch[:own_rows, :] = total[...]
    turn_over(scratch, out)


def turn_over(scratch, out):
    shots = scratch.shape[0] // ROWS
    ordered = jnp.concatenate([scratch[pl.ds(c, shots, stride=ROWS), :] for c in range(ROWS)], axis=0)
    turned = ordered.T
    count = out.shape[1]
    for k in range(QUARTERS):
        out[k] = turned[count * k : count * (k + 1), :].astype(out.dtype)


def join_kernel(y3, y2, y1, y0, out, mine, theirs):
    shot = shot_index()
    yh, k = shot >> 4, shot & 3
    z0 = k >> 1
    for m, block in enumerate((y0, y1, y2, y3)):
        place = z0 ^ (m & 1), yh ^ (m >> 1)
        out[place] = block[...]
        mine[place] = block[k]
        theirs[place] = block[k ^ 1]


def core_kernel(own, other, out):
    c = shot_index() & 1
    out[c] = own[...]
    out[1 - c] = other[...]


def choose_kernel(own, cross, out):
    straight = (shot_index() >> 4) == (lax.axis_index("rcv") >> 2)

    @pl.when(straight)
    def _():
        out[...] = own[...]

    @pl.when(jnp.logical_not(straight))
    def _():
        out[...] = cross[...]


def right_kernel(own, other, right):
    c = shot_index() & 1
    half = right.shape[2] // 2
    parts = right.shape[0] // 2
    for here, block in ((c, own), (1 - c, other)):
        for part in range(parts):
            z = block[part >> 1, part & 1].astype(jnp.float32).reshape(right.shape[1] // 2, 2 * half)
            w = jnp.concatenate([-z[:, half:], z[:, :half]], axis=1)
            right[parts * here + part] = jnp.concatenate([z, w], axis=0).astype(jnp.bfloat16)


def products(scale, right, q):
    count, lanes = q.shape[3:]
    half = lanes // 2
    span = right.shape[1] // 2
    lane = lax.broadcasted_iota(jnp.int32, (count, lanes), 1) % half // (half // NF)
    acc = jnp.zeros((NF * count, 2 * span), jnp.float32)
    for part in range(right.shape[0]):
        rows = q[part >> 2, (part >> 1) & 1, part & 1].astype(jnp.float32)
        left = jnp.concatenate([jnp.where(lane == f, rows, 0.0) for f in range(NF)], axis=0)
        acc = acc + lax.dot_general(
            left.astype(jnp.bfloat16), right[part], (((1,), (1,)), ((), ())), preferred_element_type=jnp.float32
        )
    return jnp.concatenate([acc[:, :span] * scale, acc[:, span:] * scale], axis=0)


def gram_kernel(scale, right, q, before, out, packed):
    out[...] = products(scale, right, q)
    pack(out, packed)


def last_kernel(scale, right, q, *refs):
    early, (p0, p1, p2, p3, total, wire) = refs[:-6], refs[-6:]
    turn = ((shot_index() >> 2) ^ lax.axis_index("rcv")) & 3
    for m in range(QUARTERS - 1):
        total[turn ^ m] = early[2 * m][...]
        wire[turn ^ m] = early[2 * m + 1][...]
    last = turn ^ (QUARTERS - 1)
    total[last] = products(scale, right, q)
    pack(total.at[last], wire.at[last])
    p0[...] = total[0]
    for n, out in ((1, p1), (2, p2), (3, p3)):
        out[...] = wire[n]


def pack(share, out):
    rows, width = out.shape
    lanes = share.shape[1]
    rest = width - lanes
    out[:, :lanes] = share[:rows].astype(out.dtype)
    pieces = [share[rows:, rest * g : rest * (g + 1)] for g in range(lanes // rest)]
    out[:, lanes:] = jnp.concatenate(pieces, axis=0).astype(out.dtype)


def sum_kernel(r2, r3, r1, p0, out):
    shares = r1[...].astype(jnp.float32) + r2[...].astype(jnp.float32) + r3[...].astype(jnp.float32)
    rows = shares.shape[0]
    lanes = out.shape[1]
    high = out.shape[0] - rows
    out[:rows] = p0[:rows] + shares[:, :lanes]
    pieces = [shares[high * g : high * (g + 1), lanes:] for g in range(rows // high)]
    out[rows:] = p0[rows:] + jnp.concatenate(pieces, axis=1)


def local(kernel, name, out_shape, in_specs, scratch=(), limit=4):
    single = not isinstance(out_shape, tuple)
    return pl.pallas_call(
        kernel,
        out_shape=out_shape,
        in_specs=in_specs,
        out_specs=vmem(1)[0] if single else tuple(vmem(len(out_shape))),
        scratch_shapes=list(scratch),
        compiler_params=pltpu.CompilerParams(vmem_limit_bytes=limit << 20),
        name=name,
    )


def per_device(record, shot_fire_samples):
    receivers, samples = record.shape
    shots = shot_fire_samples.shape[0]
    pairs, late = shots // 2, LATE // 2
    lanes = ROWS * shots
    late_rows = ROWS * LATE
    count = receivers // QUARTERS
    bf16, f32 = jnp.bfloat16, jnp.float32
    table = jnp.asarray(dft_master())
    smem, hbm = pl.BlockSpec(memory_space=pltpu.SMEM), pl.BlockSpec(memory_space=pltpu.HBM)

    message = local(
        tail_kernel,
        "tail_spectra",
        shape((late_rows + LATE, receivers), f32),
        [hbm] * 3,
        [
            pltpu.SMEM((shots,), jnp.int32),
            pltpu.VMEM(table.shape, f32),
            pltpu.VMEM((late, 2 * ROWS, SPAN), bf16),
            pltpu.VMEM((receivers, WIN), bf16),
            pltpu.SemaphoreType.DMA((3,)),
        ],
    )(*(pltpu.with_memory_space_constraint(a, pltpu.HBM) for a in (shot_fire_samples, table, record)))

    def following(yh, u, k, xh, v):
        shot = ((yh << 4 | u << 2 | k) + 1) % SHOT_DEVICES
        return shot >> 4, (shot >> 2) & 3, shot & 3, xh, v

    received = send(message, following)
    total = local(
        own_kernel,
        "own_spectra",
        shape((lanes - late_rows, receivers), f32),
        [smem] + vmem(2),
        [pltpu.VMEM((pairs - late, 2 * ROWS, SPAN), bf16)],
    )(shot_fire_samples, table, record)
    y = pl.pallas_call(
        finish_kernel,
        grid=(1,),
        out_shape=shape((QUARTERS, count, lanes), bf16),
        in_specs=[
            pl.BlockSpec(total.shape, lambda i: (0, 0)),
            pl.BlockSpec((receivers, WIN), lambda i: (0, 0)),
            pl.BlockSpec(table.shape, lambda i: (0, 0)),
            pl.BlockSpec(received.shape, lambda i: (0, 0)),
        ],
        out_specs=pl.BlockSpec((QUARTERS, count, lanes), lambda i: (0, 0, 0)),
        scratch_shapes=[pltpu.VMEM((lanes, receivers), f32), pltpu.VMEM((late, 2 * ROWS, SPAN), bf16)],
        compiler_params=pltpu.CompilerParams(vmem_limit_bytes=4 << 20),
        name="finish_spectra",
    )(total, record, table, received)

    y3, y2, y1 = [send(y, lambda yh, u, k, xh, v, m=m: (yh ^ m >> 1, u, k ^ (m & 1) << 1, xh, v)) for m in (3, 2, 1)]
    slices = shape((2, 2, count, lanes), bf16)
    y, mine, theirs = local(join_kernel, "join", (shape((2, 2) + y.shape, bf16), slices, slices), vmem(4))(
        y3, y2, y1, y
    )

    def to_partner(yh, u, k, xh, v):
        return yh, u, k ^ 1, xh, v

    quarter = local(core_kernel, "join_core", shape((2,) + mine.shape, bf16), vmem(2))(mine, send(theirs, to_partner))
    cross = send(quarter, lambda yh, u, k, xh, v: (yh, u, k, 1 - xh, v))
    q = local(choose_kernel, "choose", shape(quarter.shape, bf16), vmem(2))(quarter, cross)
    qs = [q] + [send(q, lambda yh, u, k, xh, v, m=m: (yh, u, k, xh, v ^ m)) for m in (1, 2, 3)]
    right = local(right_kernel, "right_side", shape((2 * QUARTERS, 2 * receivers, lanes), bf16), vmem(2))(
        y, send(y, to_partner)
    )

    total_shots = shots * lax.axis_size("shot")
    rows = ROWS * count
    scale = 1.0 / total_shots
    share = shape((rows, receivers), f32)
    width = 128
    wire = shape((rows * receivers // width, width), bf16)
    early = []
    for m in range(QUARTERS - 1):
        early += local(
            lambda *refs: gram_kernel(scale, *refs),
            "gram",
            (share, wire),
            vmem(2) + [pl.BlockSpec(memory_space=pl.ANY)],
        )(right, qs[m], early[-2] if early else right)
    p0, p1, p2, p3 = local(
        lambda *refs: last_kernel(scale, *refs),
        "last_gram",
        (share, wire, wire, wire),
        vmem(2 + len(early)),
        [pltpu.VMEM((QUARTERS,) + share.shape, f32), pltpu.VMEM((QUARTERS,) + wire.shape, bf16)],
    )(right, qs[3], *early)
    r1, r2, r3 = [send(p, lambda yh, u, k, xh, v, n=n: (yh, u ^ n, k, xh, v)) for n, p in ((1, p1), (2, p2), (3, p3))]
    sums = local(sum_kernel, "sum", share, vmem(4))(r2, r3, r1, p0)
    return sums.reshape(2, NF, count, receivers).transpose(0, 1, 3, 2)


def solution(mesh):
    return jax.shard_map(
        per_device,
        mesh=mesh,
        in_specs=(P("rcv", "shot"), P("shot")),
        out_specs=P(None, None, "rcv", "shot"),
        check_vma=False,
    )
```

```python
import math

import jax
import jax.numpy as jnp
import numpy as np
from jax import lax
from jax.experimental import pallas as pl
from jax.experimental.pallas import tpu as pltpu
from jax.sharding import PartitionSpec as P

import ml_dtypes

WIN = 2048
SPACING = 256
PAIR = 2 * SPACING
SPAN = WIN + PAIR
FREQ_BINS = (24, 40, 56, 80)
NF = len(FREQ_BINS)
ROWS = 2 * NF

SHOT_DEVICES = 32
RCV_DEVICES = 8
QUARTERS = 4
LATE = WIN // SPACING
MIDDLE = SHOT_DEVICES // 2


def dft_master():
    turns = np.arange(WIN)[None, :] * np.array(FREQ_BINS)[:, None] % WIN
    angle = 2.0 * math.pi / WIN * turns
    rows = np.concatenate([np.cos(angle), -np.sin(angle)], axis=0) / math.sqrt(WIN)
    rows = rows.astype(np.float32).astype(ml_dtypes.bfloat16).astype(np.float32)
    return np.concatenate([rows, np.zeros((ROWS, SPAN - WIN), np.float32)], axis=1)


def send(block, to):
    route = []
    for shot in range(SHOT_DEVICES):
        for rcv in range(RCV_DEVICES):
            target = to(shot >> 4, (shot >> 2) & 3, shot & 3, rcv >> 2, rcv & 3)
            if target is not None:
                yh, u, k, xh, v = target
                route.append((shot * RCV_DEVICES + rcv, (yh << 4 | u << 2 | k) * RCV_DEVICES + (xh << 2 | v)))
    return lax.ppermute(block, ("shot", "rcv"), route)


shape = jax.ShapeDtypeStruct


def shot_index():
    return lax.axis_index("shot")


def vmem(count):
    return [pl.BlockSpec(memory_space=pltpu.VMEM)] * count


def pair_tables(table, first, second, length=SPAN):
    if length < SPAN:
        table = jnp.concatenate([table[:, :length], jnp.zeros((ROWS, PAIR), table.dtype)], axis=1)
    rows = [pltpu.roll(table, first, 1)[:, :length], pltpu.roll(table, second + SPACING, 1)[:, :length]]
    return jnp.concatenate(rows, axis=0).astype(jnp.bfloat16)


def delay(fire, shot):
    return fire[shot] & (SPACING - 1)


def add_products(total, tables, first_pair, blocks):
    reach = SPAN // PAIR
    last_pair = first_pair + tables.shape[0] - 1
    for u, samples in blocks:
        low, high = max(first_pair, u - reach + 1), min(u, last_pair)
        left = jnp.concatenate(
            [tables[p - first_pair, :, PAIR * (u - p) : PAIR * (u - p + 1)] for p in range(low, high + 1)], axis=0
        )
        part = lax.dot_general(left, samples, (((1,), (1,)), ((), ())), preferred_element_type=jnp.float32)
        total[2 * ROWS * (low - first_pair) : 2 * ROWS * (high + 1 - first_pair), :] += part


def tail_kernel(fire_hbm, table_hbm, record, message, fire, table, tables, samples, sems):
    pairs = fire.shape[0] // 2
    late = LATE // 2
    start = record.shape[1] - samples.shape[1]
    copies = [
        pltpu.make_async_copy(fire_hbm, fire, sems.at[0]),
        pltpu.make_async_copy(table_hbm, table, sems.at[1]),
        pltpu.make_async_copy(record.at[:, start:], samples, sems.at[2]),
    ]
    for copy in copies:
        copy.start()
    message[...] = jnp.zeros_like(message)
    copies[0].wait()
    row = lax.broadcasted_iota(jnp.int32, (LATE, message.shape[1]), 0)
    delays = jnp.zeros(row.shape, jnp.int32)
    for i in range(LATE):
        delays = jnp.where(row == i, delay(fire, 2 * (pairs - late) + i), delays)
    message[ROWS * LATE :, :] = delays.astype(jnp.float32)
    copies[1].wait()
    master = table[...]
    for p in range(late):
        shot = 2 * (pairs - late + p)
        length = PAIR * (late - p)
        tables[p, :, :length] = pair_tables(master, delay(fire, shot), delay(fire, shot + 1), length)
    copies[2].wait()
    blocks = [(pairs - late + v, samples[:, PAIR * v : PAIR * (v + 1)]) for v in range(late)]
    add_products(message, tables, pairs - late, blocks)


def own_kernel(fire, table, record, total, first, tables):
    pairs = record.shape[1] // PAIR
    master = table[...]
    for p in range(tables.shape[0]):
        tables[p] = pair_tables(master, delay(fire, 2 * p), delay(fire, 2 * p + 1))
    total[...] = jnp.zeros_like(total)
    add_products(total, tables, 0, [(u, record[:, PAIR * u : PAIR * (u + 1)]) for u in range(pairs)])
    first[...] = total[: first.shape[0], :]


def finish_kernel(total, head, table, received, moved, given, out, scratch, tables, message):
    own_rows = total.shape[0]
    late_rows = ROWS * LATE
    late = LATE // 2
    shot = shot_index()
    master = table[...]
    message[...] = jnp.where(shot == MIDDLE - 1, moved[...], received[...])
    for p in range(late):
        rows = [message[late_rows + 2 * p + i : late_rows + 2 * p + i + 1, :] for i in range(2)]
        first, second = [jnp.max(r).astype(jnp.int32) for r in rows]
        tables[p] = pair_tables(master, first, second)
    scratch[own_rows:, :] = message[:late_rows, :]
    blocks = [(late + v, head[:, PAIR * v : PAIR * (v + 1)]) for v in range(late)]
    add_products(scratch.at[own_rows:, :], tables, 0, blocks)
    scratch[own_rows:, :] = jnp.where(shot == 0, given[...], scratch[own_rows:, :])
    scratch[late_rows:own_rows, :] = total[late_rows:, :]
    scratch[:late_rows, :] = jnp.where(shot == MIDDLE, moved[:late_rows, :], total[:late_rows, :])
    turn_over(scratch, out)


def turn_over(scratch, out):
    shots = scratch.shape[0] // ROWS
    ordered = jnp.concatenate([scratch[pl.ds(c, shots, stride=ROWS), :] for c in range(ROWS)], axis=0)
    turned = ordered.T
    count = out.shape[1]
    for k in range(QUARTERS):
        out[k] = turned[count * k : count * (k + 1), :].astype(out.dtype)


def join_kernel(y3, y2, y1, y0, out, mine, theirs):
    shot = shot_index()
    yh, k = shot >> 4, shot & 3
    z0 = k >> 1
    for m, block in enumerate((y0, y1, y2, y3)):
        place = z0 ^ (m & 1), yh ^ (m >> 1)
        out[place] = block[...]
        mine[place] = block[k]
        theirs[place] = block[k ^ 1]


def core_kernel(own, other, out):
    c = shot_index() & 1
    out[c] = own[...]
    out[1 - c] = other[...]


def choose_kernel(own, cross, out):
    straight = (shot_index() >> 4) == (lax.axis_index("rcv") >> 2)

    @pl.when(straight)
    def _():
        out[...] = own[...]

    @pl.when(jnp.logical_not(straight))
    def _():
        out[...] = cross[...]


def right_kernel(own, other, right):
    c = shot_index() & 1
    half = right.shape[2] // 2
    parts = right.shape[0] // 2
    for here, block in ((c, own), (1 - c, other)):
        for part in range(parts):
            z = block[part >> 1, part & 1].astype(jnp.float32).reshape(right.shape[1] // 2, 2 * half)
            w = jnp.concatenate([-z[:, half:], z[:, :half]], axis=1)
            right[parts * here + part] = jnp.concatenate([z, w], axis=0).astype(jnp.bfloat16)


def products(scale, right, q):
    count, lanes = q.shape[3:]
    half = lanes // 2
    span = right.shape[1] // 2
    lane = lax.broadcasted_iota(jnp.int32, (count, lanes), 1) % half // (half // NF)
    acc = jnp.zeros((NF * count, 2 * span), jnp.float32)
    for part in range(right.shape[0]):
        rows = q[part >> 2, (part >> 1) & 1, part & 1].astype(jnp.float32)
        left = jnp.concatenate([jnp.where(lane == f, rows, 0.0) for f in range(NF)], axis=0)
        acc = acc + lax.dot_general(
            left.astype(jnp.bfloat16), right[part], (((1,), (1,)), ((), ())), preferred_element_type=jnp.float32
        )
    return jnp.concatenate([acc[:, :span] * scale, acc[:, span:] * scale], axis=0)


def gram_kernel(scale, right, q, before, out, packed):
    out[...] = products(scale, right, q)
    pack(out, packed)


def last_kernel(scale, right, q, *refs):
    early, (p0, p1, p2, p3, total, wire) = refs[:-6], refs[-6:]
    turn = ((shot_index() >> 2) ^ lax.axis_index("rcv")) & 3
    for m in range(QUARTERS - 1):
        total[turn ^ m] = early[2 * m][...]
        wire[turn ^ m] = early[2 * m + 1][...]
    last = turn ^ (QUARTERS - 1)
    total[last] = products(scale, right, q)
    pack(total.at[last], wire.at[last])
    p0[...] = total[0]
    for n, out in ((1, p1), (2, p2), (3, p3)):
        out[...] = wire[n]


def pack(share, out):
    rows, width = out.shape
    lanes = share.shape[1]
    rest = width - lanes
    out[:, :lanes] = share[:rows].astype(out.dtype)
    pieces = [share[rows:, rest * g : rest * (g + 1)] for g in range(lanes // rest)]
    out[:, lanes:] = jnp.concatenate(pieces, axis=0).astype(out.dtype)


def sum_kernel(r2, r3, r1, p0, out):
    shares = r1[...].astype(jnp.float32) + r2[...].astype(jnp.float32) + r3[...].astype(jnp.float32)
    rows = shares.shape[0]
    lanes = out.shape[1]
    high = out.shape[0] - rows
    out[:rows] = p0[:rows] + shares[:, :lanes]
    pieces = [shares[high * g : high * (g + 1), lanes:] for g in range(rows // high)]
    out[rows:] = p0[rows:] + jnp.concatenate(pieces, axis=1)


def local(kernel, name, out_shape, in_specs, scratch=(), limit=4):
    single = not isinstance(out_shape, tuple)
    return pl.pallas_call(
        kernel,
        out_shape=out_shape,
        in_specs=in_specs,
        out_specs=vmem(1)[0] if single else tuple(vmem(len(out_shape))),
        scratch_shapes=list(scratch),
        compiler_params=pltpu.CompilerParams(vmem_limit_bytes=limit << 20),
        name=name,
    )


def per_device(record, shot_fire_samples):
    receivers, samples = record.shape
    shots = shot_fire_samples.shape[0]
    pairs, late = shots // 2, LATE // 2
    lanes = ROWS * shots
    late_rows = ROWS * LATE
    count = receivers // QUARTERS
    bf16, f32 = jnp.bfloat16, jnp.float32
    table = jnp.asarray(dft_master())
    smem, hbm = pl.BlockSpec(memory_space=pltpu.SMEM), pl.BlockSpec(memory_space=pltpu.HBM)

    message = local(
        tail_kernel,
        "tail_spectra",
        shape((late_rows + LATE, receivers), f32),
        [hbm] * 3,
        [
            pltpu.SMEM((shots,), jnp.int32),
            pltpu.VMEM(table.shape, f32),
            pltpu.VMEM((late, 2 * ROWS, SPAN), bf16),
            pltpu.VMEM((receivers, WIN), bf16),
            pltpu.SemaphoreType.DMA((3,)),
        ],
    )(*(pltpu.with_memory_space_constraint(a, pltpu.HBM) for a in (shot_fire_samples, table, record)))

    def chain(route):
        def to(yh, u, k, xh, v):
            shot = route(yh << 4 | u << 2 | k)
            return None if shot is None else (shot >> 4, (shot >> 2) & 3, shot & 3, xh, v)

        return to

    ends = {MIDDLE - 2: 0, SHOT_DEVICES - 1: MIDDLE - 1}
    received = send(message, chain(lambda shot: ends.get(shot, shot + 1)))
    moved = send(message, chain({MIDDLE - 2: MIDDLE - 1, SHOT_DEVICES - 1: MIDDLE}.get))
    total, first = local(
        own_kernel,
        "own_spectra",
        (shape((lanes - late_rows, receivers), f32), shape((late_rows, receivers), f32)),
        [smem] + vmem(2),
        [pltpu.VMEM((pairs - late, 2 * ROWS, SPAN), bf16)],
    )(shot_fire_samples, table, record)
    given = send(first, chain({MIDDLE: 0}.get))
    y = pl.pallas_call(
        finish_kernel,
        grid=(1,),
        out_shape=shape((QUARTERS, count, lanes), bf16),
        in_specs=[
            pl.BlockSpec(total.shape, lambda i: (0, 0)),
            pl.BlockSpec((receivers, WIN), lambda i: (0, 0)),
            pl.BlockSpec(table.shape, lambda i: (0, 0)),
            pl.BlockSpec(received.shape, lambda i: (0, 0)),
            pl.BlockSpec(moved.shape, lambda i: (0, 0)),
            pl.BlockSpec(given.shape, lambda i: (0, 0)),
        ],
        out_specs=pl.BlockSpec((QUARTERS, count, lanes), lambda i: (0, 0, 0)),
        scratch_shapes=[
            pltpu.VMEM((lanes, receivers), f32),
            pltpu.VMEM((late, 2 * ROWS, SPAN), bf16),
            pltpu.VMEM(message.shape, f32),
        ],
        compiler_params=pltpu.CompilerParams(vmem_limit_bytes=4 << 20),
        name="finish_spectra",
    )(total, record, table, received, moved, given)

    y3, y2, y1 = [send(y, lambda yh, u, k, xh, v, m=m: (yh ^ m >> 1, u, k ^ (m & 1) << 1, xh, v)) for m in (3, 2, 1)]
    slices = shape((2, 2, count, lanes), bf16)
    y, mine, theirs = local(join_kernel, "join", (shape((2, 2) + y.shape, bf16), slices, slices), vmem(4))(
        y3, y2, y1, y
    )

    def to_partner(yh, u, k, xh, v):
        return yh, u, k ^ 1, xh, v

    quarter = local(core_kernel, "join_core", shape((2,) + mine.shape, bf16), vmem(2))(mine, send(theirs, to_partner))
    cross = send(quarter, lambda yh, u, k, xh, v: (yh, u, k, 1 - xh, v))
    q = local(choose_kernel, "choose", shape(quarter.shape, bf16), vmem(2))(quarter, cross)
    qs = [q] + [send(q, lambda yh, u, k, xh, v, m=m: (yh, u, k, xh, v ^ m)) for m in (1, 2, 3)]
    right = local(right_kernel, "right_side", shape((2 * QUARTERS, 2 * receivers, lanes), bf16), vmem(2))(
        y, send(y, to_partner)
    )

    total_shots = shots * lax.axis_size("shot")
    rows = ROWS * count
    scale = 1.0 / total_shots
    share = shape((rows, receivers), f32)
    width = 128
    wire = shape((rows * receivers // width, width), bf16)
    early = []
    for m in range(QUARTERS - 1):
        early += local(
            lambda *refs: gram_kernel(scale, *refs),
            "gram",
            (share, wire),
            vmem(2) + [pl.BlockSpec(memory_space=pl.ANY)],
        )(right, qs[m], early[-2] if early else right)
    p0, p1, p2, p3 = local(
        lambda *refs: last_kernel(scale, *refs),
        "last_gram",
        (share, wire, wire, wire),
        vmem(2 + len(early)),
        [pltpu.VMEM((QUARTERS,) + share.shape, f32), pltpu.VMEM((QUARTERS,) + wire.shape, bf16)],
    )(right, qs[3], *early)
    r1, r2, r3 = [send(p, lambda yh, u, k, xh, v, n=n: (yh, u ^ n, k, xh, v)) for n, p in ((1, p1), (2, p2), (3, p3))]
    sums = local(sum_kernel, "sum", share, vmem(4))(r2, r3, r1, p0)
    return sums.reshape(2, NF, count, receivers).transpose(0, 1, 3, 2)


def solution(mesh):
    return jax.shard_map(
        per_device,
        mesh=mesh,
        in_specs=(P("rcv", "shot"), P("shot")),
        out_specs=P(None, None, "rcv", "shot"),
        check_vma=False,
    )
```

```python
import math

import jax
import jax.numpy as jnp
import numpy as np
from jax import lax
from jax.experimental import pallas as pl
from jax.experimental.pallas import tpu as pltpu
from jax.sharding import PartitionSpec as P

import ml_dtypes

WIN = 2048
SPACING = 256
PAIR = 2 * SPACING
SPAN = WIN + PAIR
FREQ_BINS = (24, 40, 56, 80)
NF = len(FREQ_BINS)
ROWS = 2 * NF

SHOT_DEVICES = 32
RCV_DEVICES = 8
QUARTERS = 4
BLOCK = 128
LATE = WIN // SPACING


def dft_master():
    turns = np.arange(WIN)[None, :] * np.array(FREQ_BINS)[:, None] % WIN
    angle = 2.0 * math.pi / WIN * turns
    rows = np.concatenate([np.cos(angle), -np.sin(angle)], axis=0) / math.sqrt(WIN)
    rows = rows.astype(np.float32).astype(ml_dtypes.bfloat16).astype(np.float32)
    return rows


def send(block, to):
    route = []
    for shot in range(SHOT_DEVICES):
        for rcv in range(RCV_DEVICES):
            target = to(shot >> 4, (shot >> 2) & 3, shot & 3, rcv >> 2, rcv & 3)
            if target is not None:
                yh, u, k, xh, v = target
                route.append((shot * RCV_DEVICES + rcv, (yh << 4 | u << 2 | k) * RCV_DEVICES + (xh << 2 | v)))
    return lax.ppermute(block, ("shot", "rcv"), route)


shape = jax.ShapeDtypeStruct


def shot_index():
    return lax.axis_index("shot")


def vmem(count):
    return [pl.BlockSpec(memory_space=pltpu.VMEM)] * count


def shifted_blocks(table, by):
    rest, whole = by & (BLOCK - 1), by >= BLOCK
    zero = jnp.zeros((ROWS, BLOCK), table.dtype)
    turned = [pltpu.roll(table[:, BLOCK * i : BLOCK * (i + 1)], rest, 1) for i in range(WIN // BLOCK)]
    early = lax.broadcasted_iota(jnp.int32, zero.shape, 1) < rest
    part = [jnp.where(early, a, b) for a, b in zip([zero, *turned], [*turned, zero])]
    return [jnp.where(whole, a, b) for a, b in zip([zero, *part], [*part, zero])]


def pair_tables(table, first, second, low=0, high=SPAN):
    zero = jnp.zeros((ROWS, BLOCK), table.dtype)
    ahead = [zero] * (SPACING // BLOCK)
    rows = [shifted_blocks(table, first) + ahead, ahead + shifted_blocks(table, second)]
    rows = [jnp.concatenate(blocks[low // BLOCK : high // BLOCK], axis=1) for blocks in rows]
    return jnp.concatenate(rows, axis=0).astype(jnp.bfloat16)


def delay(fire, shot):
    return fire[shot] & (SPACING - 1)


def add_products(total, tables, first_pair, blocks):
    reach = SPAN // PAIR
    last_pair = first_pair + tables.shape[0] - 1
    for u, samples in blocks:
        low, high = max(first_pair, u - reach + 1), min(u, last_pair)
        left = jnp.concatenate(
            [tables[p - first_pair, :, PAIR * (u - p) : PAIR * (u - p + 1)] for p in range(low, high + 1)], axis=0
        )
        part = lax.dot_general(left, samples, (((1,), (1,)), ((), ())), preferred_element_type=jnp.float32)
        total[2 * ROWS * (low - first_pair) : 2 * ROWS * (high + 1 - first_pair), :] += part


def tail_kernel(fire_hbm, table_hbm, record, message, fire, table, tables, samples, sems):
    pairs = fire.shape[0] // 2
    late = LATE // 2
    start = record.shape[1] - samples.shape[1]
    copies = [
        pltpu.make_async_copy(fire_hbm, fire, sems.at[0]),
        pltpu.make_async_copy(table_hbm, table, sems.at[1]),
        pltpu.make_async_copy(record.at[:, start:], samples, sems.at[2]),
    ]
    for copy in copies:
        copy.start()
    message[...] = jnp.zeros_like(message)
    copies[0].wait()
    row = lax.broadcasted_iota(jnp.int32, (LATE, message.shape[1]), 0)
    delays = jnp.zeros(row.shape, jnp.int32)
    for i in range(LATE):
        delays = jnp.where(row == i, delay(fire, 2 * (pairs - late) + i), delays)
    message[ROWS * LATE :, :] = delays.astype(jnp.float32)
    copies[1].wait()
    master = table[...]
    for p in range(late):
        shot = 2 * (pairs - late + p)
        length = PAIR * (late - p)
        tables[p, :, :length] = pair_tables(master, delay(fire, shot), delay(fire, shot + 1), 0, length)
    copies[2].wait()
    blocks = [(pairs - late + v, samples[:, PAIR * v : PAIR * (v + 1)]) for v in range(late)]
    add_products(message, tables, pairs - late, blocks)


def own_kernel(fire, table, record, total, tables):
    pairs = record.shape[1] // PAIR
    master = table[...]
    for p in range(tables.shape[0]):
        tables[p] = pair_tables(master, delay(fire, 2 * p), delay(fire, 2 * p + 1))
    total[...] = jnp.zeros_like(total)
    add_products(total, tables, 0, [(u, record[:, PAIR * u : PAIR * (u + 1)]) for u in range(pairs)])


def finish_kernel(total, head, table, message, out, scratch, tables):
    own_rows = total.shape[0]
    lanes = scratch.shape[0]
    late = LATE // 2
    follows = (shot_index() > 0).astype(jnp.float32)
    master = table[...]
    for p in range(late):
        rows = [message[ROWS * LATE + 2 * p + i : ROWS * LATE + 2 * p + i + 1, :] for i in range(2)]
        first, second = [jnp.max(r).astype(jnp.int32) for r in rows]
        low = PAIR * (late - p)
        tables[p, :, low:] = pair_tables(master, first, second, low)
    scratch[own_rows:, :] = jnp.zeros((lanes - own_rows, total.shape[1]), jnp.float32)
    blocks = [(late + v, head[:, PAIR * v : PAIR * (v + 1)]) for v in range(late)]
    add_products(scratch.at[own_rows:, :], tables, 0, blocks)
    scratch[own_rows:, :] = message[: ROWS * LATE, :] + follows * scratch[own_rows:, :]
    scratch[:own_rows, :] = total[...]
    turn_over(scratch, out)


def turn_over(scratch, out):
    shots = scratch.shape[0] // ROWS
    ordered = jnp.concatenate([scratch[pl.ds(c, shots, stride=ROWS), :] for c in range(ROWS)], axis=0)
    turned = ordered.T
    count = out.shape[1]
    for k in range(QUARTERS):
        out[k] = turned[count * k : count * (k + 1), :].astype(out.dtype)


def join_kernel(y3, y2, y1, y0, out, mine, theirs):
    shot = shot_index()
    yh, k = shot >> 4, shot & 3
    z0 = k >> 1
    for m, block in enumerate((y0, y1, y2, y3)):
        place = z0 ^ (m & 1), yh ^ (m >> 1)
        out[place] = block[...]
        mine[place] = block[k]
        theirs[place] = block[k ^ 1]


def core_kernel(own, other, out):
    c = shot_index() & 1
    out[c] = own[...]
    out[1 - c] = other[...]


def choose_kernel(own, cross, out):
    straight = (shot_index() >> 4) == (lax.axis_index("rcv") >> 2)

    @pl.when(straight)
    def _():
        out[...] = own[...]

    @pl.when(jnp.logical_not(straight))
    def _():
        out[...] = cross[...]


def right_kernel(own, other, right):
    c = shot_index() & 1
    half = right.shape[2] // 2
    parts = right.shape[0] // 2
    for here, block in ((c, own), (1 - c, other)):
        for part in range(parts):
            z = block[part >> 1, part & 1].astype(jnp.float32).reshape(right.shape[1] // 2, 2 * half)
            w = jnp.concatenate([-z[:, half:], z[:, :half]], axis=1)
            right[parts * here + part] = jnp.concatenate([z, w], axis=0).astype(jnp.bfloat16)


def products(scale, right, q):
    count, lanes = q.shape[3:]
    half = lanes // 2
    span = right.shape[1] // 2
    lane = lax.broadcasted_iota(jnp.int32, (count, lanes), 1) % half // (half // NF)
    acc = jnp.zeros((NF * count, 2 * span), jnp.float32)
    for part in range(right.shape[0]):
        rows = q[part >> 2, (part >> 1) & 1, part & 1].astype(jnp.float32)
        left = jnp.concatenate([jnp.where(lane == f, rows, 0.0) for f in range(NF)], axis=0)
        acc = acc + lax.dot_general(
            left.astype(jnp.bfloat16), right[part], (((1,), (1,)), ((), ())), preferred_element_type=jnp.float32
        )
    return jnp.concatenate([acc[:, :span] * scale, acc[:, span:] * scale], axis=0)


def gram_kernel(scale, right, q, before, out, packed):
    out[...] = products(scale, right, q)
    pack(out, packed)


def last_kernel(scale, right, q, *refs):
    early, (p0, p1, p2, p3, total, wire) = refs[:-6], refs[-6:]
    turn = ((shot_index() >> 2) ^ lax.axis_index("rcv")) & 3
    for m in range(QUARTERS - 1):
        total[turn ^ m] = early[2 * m][...]
        wire[turn ^ m] = early[2 * m + 1][...]
    last = turn ^ (QUARTERS - 1)
    total[last] = products(scale, right, q)
    pack(total.at[last], wire.at[last])
    p0[...] = total[0]
    for n, out in ((1, p1), (2, p2), (3, p3)):
        out[...] = wire[n]


def pack(share, out):
    rows, width = out.shape
    lanes = share.shape[1]
    rest = width - lanes
    out[:, :lanes] = share[:rows].astype(out.dtype)
    pieces = [share[rows:, rest * g : rest * (g + 1)] for g in range(lanes // rest)]
    out[:, lanes:] = jnp.concatenate(pieces, axis=0).astype(out.dtype)


def sum_kernel(r2, r3, r1, p0, out):
    shares = r1[...].astype(jnp.float32) + r2[...].astype(jnp.float32) + r3[...].astype(jnp.float32)
    rows = shares.shape[0]
    lanes = out.shape[1]
    high = out.shape[0] - rows
    out[:rows] = p0[:rows] + shares[:, :lanes]
    pieces = [shares[high * g : high * (g + 1), lanes:] for g in range(rows // high)]
    out[rows:] = p0[rows:] + jnp.concatenate(pieces, axis=1)


def local(kernel, name, out_shape, in_specs, scratch=(), limit=4):
    single = not isinstance(out_shape, tuple)
    return pl.pallas_call(
        kernel,
        out_shape=out_shape,
        in_specs=in_specs,
        out_specs=vmem(1)[0] if single else tuple(vmem(len(out_shape))),
        scratch_shapes=list(scratch),
        compiler_params=pltpu.CompilerParams(vmem_limit_bytes=limit << 20),
        name=name,
    )


def per_device(record, shot_fire_samples):
    receivers, samples = record.shape
    shots = shot_fire_samples.shape[0]
    pairs, late = shots // 2, LATE // 2
    lanes = ROWS * shots
    late_rows = ROWS * LATE
    count = receivers // QUARTERS
    bf16, f32 = jnp.bfloat16, jnp.float32
    table = jnp.asarray(dft_master())
    smem, hbm = pl.BlockSpec(memory_space=pltpu.SMEM), pl.BlockSpec(memory_space=pltpu.HBM)

    message = local(
        tail_kernel,
        "tail_spectra",
        shape((late_rows + LATE, receivers), f32),
        [hbm] * 3,
        [
            pltpu.SMEM((shots,), jnp.int32),
            pltpu.VMEM(table.shape, f32),
            pltpu.VMEM((late, 2 * ROWS, SPAN), bf16),
            pltpu.VMEM((receivers, WIN), bf16),
            pltpu.SemaphoreType.DMA((3,)),
        ],
    )(*(pltpu.with_memory_space_constraint(a, pltpu.HBM) for a in (shot_fire_samples, table, record)))

    def following(yh, u, k, xh, v):
        shot = ((yh << 4 | u << 2 | k) + 1) % SHOT_DEVICES
        return shot >> 4, (shot >> 2) & 3, shot & 3, xh, v

    received = send(message, following)
    total = local(
        own_kernel,
        "own_spectra",
        shape((lanes - late_rows, receivers), f32),
        [smem] + vmem(2),
        [pltpu.VMEM((pairs - late, 2 * ROWS, SPAN), bf16)],
    )(shot_fire_samples, table, record)
    y = pl.pallas_call(
        finish_kernel,
        grid=(1,),
        out_shape=shape((QUARTERS, count, lanes), bf16),
        in_specs=[
            pl.BlockSpec(total.shape, lambda i: (0, 0)),
            pl.BlockSpec((receivers, WIN), lambda i: (0, 0)),
            pl.BlockSpec(table.shape, lambda i: (0, 0)),
            pl.BlockSpec(received.shape, lambda i: (0, 0)),
        ],
        out_specs=pl.BlockSpec((QUARTERS, count, lanes), lambda i: (0, 0, 0)),
        scratch_shapes=[pltpu.VMEM((lanes, receivers), f32), pltpu.VMEM((late, 2 * ROWS, SPAN), bf16)],
        compiler_params=pltpu.CompilerParams(vmem_limit_bytes=4 << 20),
        name="finish_spectra",
    )(total, record, table, received)

    y3, y2, y1 = [send(y, lambda yh, u, k, xh, v, m=m: (yh ^ m >> 1, u, k ^ (m & 1) << 1, xh, v)) for m in (3, 2, 1)]
    slices = shape((2, 2, count, lanes), bf16)
    y, mine, theirs = local(join_kernel, "join", (shape((2, 2) + y.shape, bf16), slices, slices), vmem(4))(
        y3, y2, y1, y
    )

    def to_partner(yh, u, k, xh, v):
        return yh, u, k ^ 1, xh, v

    quarter = local(core_kernel, "join_core", shape((2,) + mine.shape, bf16), vmem(2))(mine, send(theirs, to_partner))
    cross = send(quarter, lambda yh, u, k, xh, v: (yh, u, k, 1 - xh, v))
    q = local(choose_kernel, "choose", shape(quarter.shape, bf16), vmem(2))(quarter, cross)
    qs = [q] + [send(q, lambda yh, u, k, xh, v, m=m: (yh, u, k, xh, v ^ m)) for m in (1, 2, 3)]
    right = local(right_kernel, "right_side", shape((2 * QUARTERS, 2 * receivers, lanes), bf16), vmem(2))(
        y, send(y, to_partner)
    )

    total_shots = shots * lax.axis_size("shot")
    rows = ROWS * count
    scale = 1.0 / total_shots
    share = shape((rows, receivers), f32)
    width = 128
    wire = shape((rows * receivers // width, width), bf16)
    early = []
    for m in range(QUARTERS - 1):
        early += local(
            lambda *refs: gram_kernel(scale, *refs),
            "gram",
            (share, wire),
            vmem(2) + [pl.BlockSpec(memory_space=pl.ANY)],
        )(right, qs[m], early[-2] if early else right)
    p0, p1, p2, p3 = local(
        lambda *refs: last_kernel(scale, *refs),
        "last_gram",
        (share, wire, wire, wire),
        vmem(2 + len(early)),
        [pltpu.VMEM((QUARTERS,) + share.shape, f32), pltpu.VMEM((QUARTERS,) + wire.shape, bf16)],
    )(right, qs[3], *early)
    r1, r2, r3 = [send(p, lambda yh, u, k, xh, v, n=n: (yh, u ^ n, k, xh, v)) for n, p in ((1, p1), (2, p2), (3, p3))]
    sums = local(sum_kernel, "sum", share, vmem(4))(r2, r3, r1, p0)
    return sums.reshape(2, NF, count, receivers).transpose(0, 1, 3, 2)


def solution(mesh):
    return jax.shard_map(
        per_device,
        mesh=mesh,
        in_specs=(P("rcv", "shot"), P("shot")),
        out_specs=P(None, None, "rcv", "shot"),
        check_vma=False,
    )
```

```python
import math

import jax
import jax.numpy as jnp
import numpy as np
from jax import lax
from jax.experimental import pallas as pl
from jax.experimental.pallas import tpu as pltpu
from jax.sharding import PartitionSpec as P

import ml_dtypes

WIN = 2048
SPACING = 256
PAIR = 2 * SPACING
SPAN = WIN + PAIR
FREQ_BINS = (24, 40, 56, 80)
NF = len(FREQ_BINS)
ROWS = 2 * NF

SHOT_DEVICES = 32
RCV_DEVICES = 8
QUARTERS = 4
BLOCK = 128
LATE = WIN // SPACING


def dft_master():
    turns = np.arange(WIN)[None, :] * np.array(FREQ_BINS)[:, None] % WIN
    angle = 2.0 * math.pi / WIN * turns
    rows = np.concatenate([np.cos(angle), -np.sin(angle)], axis=0) / math.sqrt(WIN)
    rows = rows.astype(np.float32).astype(ml_dtypes.bfloat16).astype(np.float32)
    return rows


def send(block, to):
    route = []
    for shot in range(SHOT_DEVICES):
        for rcv in range(RCV_DEVICES):
            target = to(shot >> 4, (shot >> 2) & 3, shot & 3, rcv >> 2, rcv & 3)
            if target is not None:
                yh, u, k, xh, v = target
                route.append((shot * RCV_DEVICES + rcv, (yh << 4 | u << 2 | k) * RCV_DEVICES + (xh << 2 | v)))
    return lax.ppermute(block, ("shot", "rcv"), route)


shape = jax.ShapeDtypeStruct


def shot_index():
    return lax.axis_index("shot")


def vmem(count):
    return [pl.BlockSpec(memory_space=pltpu.VMEM)] * count


def shifted_blocks(table, by):
    rest, whole = by & (BLOCK - 1), by >= BLOCK
    zero = jnp.zeros((ROWS, BLOCK), table.dtype)
    turned = [pltpu.roll(table[:, BLOCK * i : BLOCK * (i + 1)], rest, 1) for i in range(WIN // BLOCK)]
    early = lax.broadcasted_iota(jnp.int32, zero.shape, 1) < rest
    part = [jnp.where(early, a, b) for a, b in zip([zero, *turned], [*turned, zero])]
    return [jnp.where(whole, a, b) for a, b in zip([zero, *part], [*part, zero])]


def pair_tables(table, first, second, low=0, high=SPAN):
    zero = jnp.zeros((ROWS, BLOCK), table.dtype)
    ahead = [zero] * (SPACING // BLOCK)
    rows = [shifted_blocks(table, first) + ahead, ahead + shifted_blocks(table, second)]
    rows = [jnp.concatenate(blocks[low // BLOCK : high // BLOCK], axis=1) for blocks in rows]
    return jnp.concatenate(rows, axis=0).astype(jnp.bfloat16)


def delay(fire, shot):
    return fire[shot] & (SPACING - 1)


def add_products(total, tables, first_pair, blocks):
    reach = SPAN // PAIR
    last_pair = first_pair + tables.shape[0] - 1
    for u, samples in blocks:
        low, high = max(first_pair, u - reach + 1), min(u, last_pair)
        left = jnp.concatenate(
            [tables[p - first_pair, :, PAIR * (u - p) : PAIR * (u - p + 1)] for p in range(low, high + 1)], axis=0
        )
        part = lax.dot_general(left, samples, (((1,), (1,)), ((), ())), preferred_element_type=jnp.float32)
        total[2 * ROWS * (low - first_pair) : 2 * ROWS * (high + 1 - first_pair), :] += part


def tail_kernel(fire_hbm, table_hbm, record, message, fire, table, tables, samples, sems):
    pairs = fire.shape[0] // 2
    late = LATE // 2
    start = record.shape[1] - samples.shape[1]
    columns = [slice(PAIR * v, PAIR * (v + 1)) for v in range(late)]
    copies = [
        pltpu.make_async_copy(fire_hbm, fire, sems.at[0]),
        pltpu.make_async_copy(table_hbm, table, sems.at[1]),
    ] + [
        pltpu.make_async_copy(record.at[:, start + c.start : start + c.stop], samples.at[:, c], sems.at[2 + v])
        for v, c in enumerate(columns)
    ]
    for copy in copies:
        copy.start()
    message[...] = jnp.zeros_like(message)
    copies[0].wait()
    row = lax.broadcasted_iota(jnp.int32, (LATE, message.shape[1]), 0)
    delays = jnp.zeros(row.shape, jnp.int32)
    for i in range(LATE):
        delays = jnp.where(row == i, delay(fire, 2 * (pairs - late) + i), delays)
    message[ROWS * LATE :, :] = delays.astype(jnp.float32)
    copies[1].wait()
    master = table[...]
    for p in range(late):
        shot = 2 * (pairs - late + p)
        length = PAIR * (late - p)
        tables[p, :, :length] = pair_tables(master, delay(fire, shot), delay(fire, shot + 1), 0, length)
    for v, c in enumerate(columns):
        copies[2 + v].wait()
        add_products(message, tables, pairs - late, [(pairs - late + v, samples[:, c])])


def own_kernel(fire, table, record, total, tables):
    pairs = record.shape[1] // PAIR
    master = table[...]
    for p in range(tables.shape[0]):
        tables[p] = pair_tables(master, delay(fire, 2 * p), delay(fire, 2 * p + 1))
    total[...] = jnp.zeros_like(total)
    add_products(total, tables, 0, [(u, record[:, PAIR * u : PAIR * (u + 1)]) for u in range(pairs)])


def finish_kernel(total, head, table, message, out, scratch, tables):
    own_rows = total.shape[0]
    lanes = scratch.shape[0]
    late = LATE // 2
    follows = (shot_index() > 0).astype(jnp.float32)
    master = table[...]
    for p in range(late):
        rows = [message[ROWS * LATE + 2 * p + i : ROWS * LATE + 2 * p + i + 1, :] for i in range(2)]
        first, second = [jnp.max(r).astype(jnp.int32) for r in rows]
        low = PAIR * (late - p)
        tables[p, :, low:] = pair_tables(master, first, second, low)
    scratch[own_rows:, :] = jnp.zeros((lanes - own_rows, total.shape[1]), jnp.float32)
    blocks = [(late + v, head[:, PAIR * v : PAIR * (v + 1)]) for v in range(late)]
    add_products(scratch.at[own_rows:, :], tables, 0, blocks)
    scratch[own_rows:, :] = message[: ROWS * LATE, :] + follows * scratch[own_rows:, :]
    scratch[:own_rows, :] = total[...]
    turn_over(scratch, out)


def turn_over(scratch, out):
    shots = scratch.shape[0] // ROWS
    ordered = jnp.concatenate([scratch[pl.ds(c, shots, stride=ROWS), :] for c in range(ROWS)], axis=0)
    turned = ordered.T
    count = out.shape[1]
    for k in range(QUARTERS):
        out[k] = turned[count * k : count * (k + 1), :].astype(out.dtype)


def join_kernel(y3, y2, y1, y0, out, mine, theirs):
    shot = shot_index()
    yh, k = shot >> 4, shot & 3
    z0 = k >> 1
    for m, block in enumerate((y0, y1, y2, y3)):
        place = z0 ^ (m & 1), yh ^ (m >> 1)
        out[place] = block[...]
        mine[place] = block[k]
        theirs[place] = block[k ^ 1]


def core_kernel(own, other, out):
    c = shot_index() & 1
    out[c] = own[...]
    out[1 - c] = other[...]


def choose_kernel(own, cross, out):
    straight = (shot_index() >> 4) == (lax.axis_index("rcv") >> 2)

    @pl.when(straight)
    def _():
        out[...] = own[...]

    @pl.when(jnp.logical_not(straight))
    def _():
        out[...] = cross[...]


def right_kernel(own, other, right):
    c = shot_index() & 1
    half = right.shape[2] // 2
    parts = right.shape[0] // 2
    for here, block in ((c, own), (1 - c, other)):
        for part in range(parts):
            z = block[part >> 1, part & 1].astype(jnp.float32).reshape(right.shape[1] // 2, 2 * half)
            w = jnp.concatenate([-z[:, half:], z[:, :half]], axis=1)
            right[parts * here + part] = jnp.concatenate([z, w], axis=0).astype(jnp.bfloat16)


def products(scale, right, q):
    count, lanes = q.shape[3:]
    half = lanes // 2
    span = right.shape[1] // 2
    lane = lax.broadcasted_iota(jnp.int32, (count, lanes), 1) % half // (half // NF)
    acc = jnp.zeros((NF * count, 2 * span), jnp.float32)
    for part in range(right.shape[0]):
        rows = q[part >> 2, (part >> 1) & 1, part & 1].astype(jnp.float32)
        left = jnp.concatenate([jnp.where(lane == f, rows, 0.0) for f in range(NF)], axis=0)
        acc = acc + lax.dot_general(
            left.astype(jnp.bfloat16), right[part], (((1,), (1,)), ((), ())), preferred_element_type=jnp.float32
        )
    return jnp.concatenate([acc[:, :span] * scale, acc[:, span:] * scale], axis=0)


def gram_kernel(scale, right, q, before, out, packed):
    out[...] = products(scale, right, q)
    pack(out, packed)


def last_kernel(scale, right, q, *refs):
    early, (p0, p1, p2, p3, total, wire) = refs[:-6], refs[-6:]
    turn = ((shot_index() >> 2) ^ lax.axis_index("rcv")) & 3
    for m in range(QUARTERS - 1):
        total[turn ^ m] = early[2 * m][...]
        wire[turn ^ m] = early[2 * m + 1][...]
    last = turn ^ (QUARTERS - 1)
    total[last] = products(scale, right, q)
    pack(total.at[last], wire.at[last])
    p0[...] = total[0]
    for n, out in ((1, p1), (2, p2), (3, p3)):
        out[...] = wire[n]


def pack(share, out):
    rows, width = out.shape
    lanes = share.shape[1]
    rest = width - lanes
    out[:, :lanes] = share[:rows].astype(out.dtype)
    pieces = [share[rows:, rest * g : rest * (g + 1)] for g in range(lanes // rest)]
    out[:, lanes:] = jnp.concatenate(pieces, axis=0).astype(out.dtype)


def sum_kernel(r2, r3, r1, p0, out):
    shares = r1[...].astype(jnp.float32) + r2[...].astype(jnp.float32) + r3[...].astype(jnp.float32)
    rows = shares.shape[0]
    lanes = out.shape[1]
    high = out.shape[0] - rows
    out[:rows] = p0[:rows] + shares[:, :lanes]
    pieces = [shares[high * g : high * (g + 1), lanes:] for g in range(rows // high)]
    out[rows:] = p0[rows:] + jnp.concatenate(pieces, axis=1)


def local(kernel, name, out_shape, in_specs, scratch=(), limit=4):
    single = not isinstance(out_shape, tuple)
    return pl.pallas_call(
        kernel,
        out_shape=out_shape,
        in_specs=in_specs,
        out_specs=vmem(1)[0] if single else tuple(vmem(len(out_shape))),
        scratch_shapes=list(scratch),
        compiler_params=pltpu.CompilerParams(vmem_limit_bytes=limit << 20),
        name=name,
    )


def per_device(record, shot_fire_samples):
    receivers, samples = record.shape
    shots = shot_fire_samples.shape[0]
    pairs, late = shots // 2, LATE // 2
    lanes = ROWS * shots
    late_rows = ROWS * LATE
    count = receivers // QUARTERS
    bf16, f32 = jnp.bfloat16, jnp.float32
    table = jnp.asarray(dft_master())
    smem, hbm = pl.BlockSpec(memory_space=pltpu.SMEM), pl.BlockSpec(memory_space=pltpu.HBM)

    message = local(
        tail_kernel,
        "tail_spectra",
        shape((late_rows + LATE, receivers), f32),
        [hbm] * 3,
        [
            pltpu.SMEM((shots,), jnp.int32),
            pltpu.VMEM(table.shape, f32),
            pltpu.VMEM((late, 2 * ROWS, SPAN), bf16),
            pltpu.VMEM((receivers, WIN), bf16),
            pltpu.SemaphoreType.DMA((2 + late,)),
        ],
    )(*(pltpu.with_memory_space_constraint(a, pltpu.HBM) for a in (shot_fire_samples, table, record)))

    def following(yh, u, k, xh, v):
        shot = ((yh << 4 | u << 2 | k) + 1) % SHOT_DEVICES
        return shot >> 4, (shot >> 2) & 3, shot & 3, xh, v

    received = send(message, following)
    total = local(
        own_kernel,
        "own_spectra",
        shape((lanes - late_rows, receivers), f32),
        [smem] + vmem(2),
        [pltpu.VMEM((pairs - late, 2 * ROWS, SPAN), bf16)],
    )(shot_fire_samples, table, record)
    y = pl.pallas_call(
        finish_kernel,
        grid=(1,),
        out_shape=shape((QUARTERS, count, lanes), bf16),
        in_specs=[
            pl.BlockSpec(total.shape, lambda i: (0, 0)),
            pl.BlockSpec((receivers, WIN), lambda i: (0, 0)),
            pl.BlockSpec(table.shape, lambda i: (0, 0)),
            pl.BlockSpec(received.shape, lambda i: (0, 0)),
        ],
        out_specs=pl.BlockSpec((QUARTERS, count, lanes), lambda i: (0, 0, 0)),
        scratch_shapes=[pltpu.VMEM((lanes, receivers), f32), pltpu.VMEM((late, 2 * ROWS, SPAN), bf16)],
        compiler_params=pltpu.CompilerParams(vmem_limit_bytes=4 << 20),
        name="finish_spectra",
    )(total, record, table, received)

    y3, y2, y1 = [send(y, lambda yh, u, k, xh, v, m=m: (yh ^ m >> 1, u, k ^ (m & 1) << 1, xh, v)) for m in (3, 2, 1)]
    slices = shape((2, 2, count, lanes), bf16)
    y, mine, theirs = local(join_kernel, "join", (shape((2, 2) + y.shape, bf16), slices, slices), vmem(4))(
        y3, y2, y1, y
    )

    def to_partner(yh, u, k, xh, v):
        return yh, u, k ^ 1, xh, v

    quarter = local(core_kernel, "join_core", shape((2,) + mine.shape, bf16), vmem(2))(mine, send(theirs, to_partner))
    cross = send(quarter, lambda yh, u, k, xh, v: (yh, u, k, 1 - xh, v))
    q = local(choose_kernel, "choose", shape(quarter.shape, bf16), vmem(2))(quarter, cross)
    qs = [q] + [send(q, lambda yh, u, k, xh, v, m=m: (yh, u, k, xh, v ^ m)) for m in (1, 2, 3)]
    right = local(right_kernel, "right_side", shape((2 * QUARTERS, 2 * receivers, lanes), bf16), vmem(2))(
        y, send(y, to_partner)
    )

    total_shots = shots * lax.axis_size("shot")
    rows = ROWS * count
    scale = 1.0 / total_shots
    share = shape((rows, receivers), f32)
    width = 128
    wire = shape((rows * receivers // width, width), bf16)
    early = []
    for m in range(QUARTERS - 1):
        early += local(
            lambda *refs: gram_kernel(scale, *refs),
            "gram",
            (share, wire),
            vmem(2) + [pl.BlockSpec(memory_space=pl.ANY)],
        )(right, qs[m], early[-2] if early else right)
    p0, p1, p2, p3 = local(
        lambda *refs: last_kernel(scale, *refs),
        "last_gram",
        (share, wire, wire, wire),
        vmem(2 + len(early)),
        [pltpu.VMEM((QUARTERS,) + share.shape, f32), pltpu.VMEM((QUARTERS,) + wire.shape, bf16)],
    )(right, qs[3], *early)
    r1, r2, r3 = [send(p, lambda yh, u, k, xh, v, n=n: (yh, u ^ n, k, xh, v)) for n, p in ((1, p1), (2, p2), (3, p3))]
    sums = local(sum_kernel, "sum", share, vmem(4))(r2, r3, r1, p0)
    return sums.reshape(2, NF, count, receivers).transpose(0, 1, 3, 2)


def solution(mesh):
    return jax.shard_map(
        per_device,
        mesh=mesh,
        in_specs=(P("rcv", "shot"), P("shot")),
        out_specs=P(None, None, "rcv", "shot"),
        check_vma=False,
    )
```

```python
import math

import jax
import jax.numpy as jnp
import numpy as np
from jax import lax
from jax.experimental import pallas as pl
from jax.experimental.pallas import tpu as pltpu
from jax.sharding import PartitionSpec as P

import ml_dtypes

WIN = 2048
SPACING = 256
PAIR = 2 * SPACING
SPAN = WIN + PAIR
FREQ_BINS = (24, 40, 56, 80)
NF = len(FREQ_BINS)
ROWS = 2 * NF

SHOT_DEVICES = 32
RCV_DEVICES = 8
QUARTERS = 4
BLOCK = 128
LATE = WIN // SPACING


def dft_master():
    turns = np.arange(WIN)[None, :] * np.array(FREQ_BINS)[:, None] % WIN
    angle = 2.0 * math.pi / WIN * turns
    rows = np.concatenate([np.cos(angle), -np.sin(angle)], axis=0) / math.sqrt(WIN)
    rows = rows.astype(np.float32).astype(ml_dtypes.bfloat16).astype(np.float32)
    return rows


def send(block, to):
    route = []
    for shot in range(SHOT_DEVICES):
        for rcv in range(RCV_DEVICES):
            target = to(shot >> 4, (shot >> 2) & 3, shot & 3, rcv >> 2, rcv & 3)
            if target is not None:
                yh, u, k, xh, v = target
                route.append((shot * RCV_DEVICES + rcv, (yh << 4 | u << 2 | k) * RCV_DEVICES + (xh << 2 | v)))
    return lax.ppermute(block, ("shot", "rcv"), route)


shape = jax.ShapeDtypeStruct


def shot_index():
    return lax.axis_index("shot")


def vmem(count):
    return [pl.BlockSpec(memory_space=pltpu.VMEM)] * count


def shifted_blocks(table, by):
    rest, whole = by & (BLOCK - 1), by >= BLOCK
    zero = jnp.zeros((ROWS, BLOCK), table.dtype)
    turned = [pltpu.roll(table[:, BLOCK * i : BLOCK * (i + 1)], rest, 1) for i in range(WIN // BLOCK)]
    early = lax.broadcasted_iota(jnp.int32, zero.shape, 1) < rest
    part = [jnp.where(early, a, b) for a, b in zip([zero, *turned], [*turned, zero])]
    return [jnp.where(whole, a, b) for a, b in zip([zero, *part], [*part, zero])]


def pair_tables(table, first, second, low=0, high=SPAN):
    zero = jnp.zeros((ROWS, BLOCK), table.dtype)
    ahead = [zero] * (SPACING // BLOCK)
    rows = [shifted_blocks(table, first) + ahead, ahead + shifted_blocks(table, second)]
    rows = [jnp.concatenate(blocks[low // BLOCK : high // BLOCK], axis=1) for blocks in rows]
    return jnp.concatenate(rows, axis=0).astype(jnp.bfloat16)


def delay(fire, shot):
    return fire[shot] & (SPACING - 1)


def add_products(total, tables, first_pair, blocks):
    reach = SPAN // PAIR
    last_pair = first_pair + tables.shape[0] - 1
    for u, samples in blocks:
        low, high = max(first_pair, u - reach + 1), min(u, last_pair)
        left = jnp.concatenate(
            [tables[p - first_pair, :, PAIR * (u - p) : PAIR * (u - p + 1)] for p in range(low, high + 1)], axis=0
        )
        part = lax.dot_general(left, samples, (((1,), (1,)), ((), ())), preferred_element_type=jnp.float32)
        total[2 * ROWS * (low - first_pair) : 2 * ROWS * (high + 1 - first_pair), :] += part


def tail_kernel(fire_hbm, table_hbm, record, message, fire, table, tables, samples, sems):
    pairs = fire.shape[0] // 2
    late = LATE // 2
    start = record.shape[1] - samples.shape[1]
    copies = [
        pltpu.make_async_copy(fire_hbm, fire, sems.at[0]),
        pltpu.make_async_copy(table_hbm, table, sems.at[1]),
        pltpu.make_async_copy(record.at[:, start:], samples, sems.at[2]),
    ]
    for copy in reversed(copies):
        copy.start()
    message[...] = jnp.zeros_like(message)
    copies[0].wait()
    row = lax.broadcasted_iota(jnp.int32, (LATE, message.shape[1]), 0)
    delays = jnp.zeros(row.shape, jnp.int32)
    for i in range(LATE):
        delays = jnp.where(row == i, delay(fire, 2 * (pairs - late) + i), delays)
    message[ROWS * LATE :, :] = delays.astype(jnp.float32)
    copies[1].wait()
    master = table[...]
    for p in range(late):
        shot = 2 * (pairs - late + p)
        length = PAIR * (late - p)
        tables[p, :, :length] = pair_tables(master, delay(fire, shot), delay(fire, shot + 1), 0, length)
    copies[2].wait()
    blocks = [(pairs - late + v, samples[:, PAIR * v : PAIR * (v + 1)]) for v in range(late)]
    add_products(message, tables, pairs - late, blocks)


def own_kernel(fire, table, record, total, tables):
    pairs = record.shape[1] // PAIR
    master = table[...]
    for p in range(tables.shape[0]):
        tables[p] = pair_tables(master, delay(fire, 2 * p), delay(fire, 2 * p + 1))
    total[...] = jnp.zeros_like(total)
    add_products(total, tables, 0, [(u, record[:, PAIR * u : PAIR * (u + 1)]) for u in range(pairs)])


def finish_kernel(total, head, table, message, out, scratch, tables):
    own_rows = total.shape[0]
    lanes = scratch.shape[0]
    late = LATE // 2
    follows = (shot_index() > 0).astype(jnp.float32)
    master = table[...]
    for p in range(late):
        rows = [message[ROWS * LATE + 2 * p + i : ROWS * LATE + 2 * p + i + 1, :] for i in range(2)]
        first, second = [jnp.max(r).astype(jnp.int32) for r in rows]
        low = PAIR * (late - p)
        tables[p, :, low:] = pair_tables(master, first, second, low)
    scratch[own_rows:, :] = jnp.zeros((lanes - own_rows, total.shape[1]), jnp.float32)
    blocks = [(late + v, head[:, PAIR * v : PAIR * (v + 1)]) for v in range(late)]
    add_products(scratch.at[own_rows:, :], tables, 0, blocks)
    scratch[own_rows:, :] = message[: ROWS * LATE, :] + follows * scratch[own_rows:, :]
    scratch[:own_rows, :] = total[...]
    turn_over(scratch, out)


def turn_over(scratch, out):
    shots = scratch.shape[0] // ROWS
    ordered = jnp.concatenate([scratch[pl.ds(c, shots, stride=ROWS), :] for c in range(ROWS)], axis=0)
    turned = ordered.T
    count = out.shape[1]
    for k in range(QUARTERS):
        out[k] = turned[count * k : count * (k + 1), :].astype(out.dtype)


def join_kernel(y3, y2, y1, y0, out, mine, theirs):
    shot = shot_index()
    yh, k = shot >> 4, shot & 3
    z0 = k >> 1
    for m, block in enumerate((y0, y1, y2, y3)):
        place = z0 ^ (m & 1), yh ^ (m >> 1)
        out[place] = block[...]
        mine[place] = block[k]
        theirs[place] = block[k ^ 1]


def core_kernel(own, other, out):
    c = shot_index() & 1
    out[c] = own[...]
    out[1 - c] = other[...]


def choose_kernel(own, cross, out):
    straight = (shot_index() >> 4) == (lax.axis_index("rcv") >> 2)

    @pl.when(straight)
    def _():
        out[...] = own[...]

    @pl.when(jnp.logical_not(straight))
    def _():
        out[...] = cross[...]


def right_kernel(own, other, right):
    c = shot_index() & 1
    half = right.shape[2] // 2
    parts = right.shape[0] // 2
    for here, block in ((c, own), (1 - c, other)):
        for part in range(parts):
            z = block[part >> 1, part & 1].astype(jnp.float32).reshape(right.shape[1] // 2, 2 * half)
            w = jnp.concatenate([-z[:, half:], z[:, :half]], axis=1)
            right[parts * here + part] = jnp.concatenate([z, w], axis=0).astype(jnp.bfloat16)


def products(scale, right, q):
    count, lanes = q.shape[3:]
    half = lanes // 2
    span = right.shape[1] // 2
    lane = lax.broadcasted_iota(jnp.int32, (count, lanes), 1) % half // (half // NF)
    acc = jnp.zeros((NF * count, 2 * span), jnp.float32)
    for part in range(right.shape[0]):
        rows = q[part >> 2, (part >> 1) & 1, part & 1].astype(jnp.float32)
        left = jnp.concatenate([jnp.where(lane == f, rows, 0.0) for f in range(NF)], axis=0)
        acc = acc + lax.dot_general(
            left.astype(jnp.bfloat16), right[part], (((1,), (1,)), ((), ())), preferred_element_type=jnp.float32
        )
    return jnp.concatenate([acc[:, :span] * scale, acc[:, span:] * scale], axis=0)


def gram_kernel(scale, right, q, before, out, packed):
    out[...] = products(scale, right, q)
    pack(out, packed)


def last_kernel(scale, right, q, *refs):
    early, (p0, p1, p2, p3, total, wire) = refs[:-6], refs[-6:]
    turn = ((shot_index() >> 2) ^ lax.axis_index("rcv")) & 3
    for m in range(QUARTERS - 1):
        total[turn ^ m] = early[2 * m][...]
        wire[turn ^ m] = early[2 * m + 1][...]
    last = turn ^ (QUARTERS - 1)
    total[last] = products(scale, right, q)
    pack(total.at[last], wire.at[last])
    p0[...] = total[0]
    for n, out in ((1, p1), (2, p2), (3, p3)):
        out[...] = wire[n]


def pack(share, out):
    rows, width = out.shape
    lanes = share.shape[1]
    rest = width - lanes
    out[:, :lanes] = share[:rows].astype(out.dtype)
    pieces = [share[rows:, rest * g : rest * (g + 1)] for g in range(lanes // rest)]
    out[:, lanes:] = jnp.concatenate(pieces, axis=0).astype(out.dtype)


def sum_kernel(r2, r3, r1, p0, out):
    shares = r1[...].astype(jnp.float32) + r2[...].astype(jnp.float32) + r3[...].astype(jnp.float32)
    rows = shares.shape[0]
    lanes = out.shape[1]
    high = out.shape[0] - rows
    out[:rows] = p0[:rows] + shares[:, :lanes]
    pieces = [shares[high * g : high * (g + 1), lanes:] for g in range(rows // high)]
    out[rows:] = p0[rows:] + jnp.concatenate(pieces, axis=1)


def local(kernel, name, out_shape, in_specs, scratch=(), limit=4):
    single = not isinstance(out_shape, tuple)
    return pl.pallas_call(
        kernel,
        out_shape=out_shape,
        in_specs=in_specs,
        out_specs=vmem(1)[0] if single else tuple(vmem(len(out_shape))),
        scratch_shapes=list(scratch),
        compiler_params=pltpu.CompilerParams(vmem_limit_bytes=limit << 20),
        name=name,
    )


def per_device(record, shot_fire_samples):
    receivers, samples = record.shape
    shots = shot_fire_samples.shape[0]
    pairs, late = shots // 2, LATE // 2
    lanes = ROWS * shots
    late_rows = ROWS * LATE
    count = receivers // QUARTERS
    bf16, f32 = jnp.bfloat16, jnp.float32
    table = jnp.asarray(dft_master())
    smem, hbm = pl.BlockSpec(memory_space=pltpu.SMEM), pl.BlockSpec(memory_space=pltpu.HBM)

    message = local(
        tail_kernel,
        "tail_spectra",
        shape((late_rows + LATE, receivers), f32),
        [hbm] * 3,
        [
            pltpu.SMEM((shots,), jnp.int32),
            pltpu.VMEM(table.shape, f32),
            pltpu.VMEM((late, 2 * ROWS, SPAN), bf16),
            pltpu.VMEM((receivers, WIN), bf16),
            pltpu.SemaphoreType.DMA((3,)),
        ],
    )(*(pltpu.with_memory_space_constraint(a, pltpu.HBM) for a in (shot_fire_samples, table, record)))

    def following(yh, u, k, xh, v):
        shot = ((yh << 4 | u << 2 | k) + 1) % SHOT_DEVICES
        return shot >> 4, (shot >> 2) & 3, shot & 3, xh, v

    received = send(message, following)
    total = local(
        own_kernel,
        "own_spectra",
        shape((lanes - late_rows, receivers), f32),
        [smem] + vmem(2),
        [pltpu.VMEM((pairs - late, 2 * ROWS, SPAN), bf16)],
    )(shot_fire_samples, table, record)
    y = pl.pallas_call(
        finish_kernel,
        grid=(1,),
        out_shape=shape((QUARTERS, count, lanes), bf16),
        in_specs=[
            pl.BlockSpec(total.shape, lambda i: (0, 0)),
            pl.BlockSpec((receivers, WIN), lambda i: (0, 0)),
            pl.BlockSpec(table.shape, lambda i: (0, 0)),
            pl.BlockSpec(received.shape, lambda i: (0, 0)),
        ],
        out_specs=pl.BlockSpec((QUARTERS, count, lanes), lambda i: (0, 0, 0)),
        scratch_shapes=[pltpu.VMEM((lanes, receivers), f32), pltpu.VMEM((late, 2 * ROWS, SPAN), bf16)],
        compiler_params=pltpu.CompilerParams(vmem_limit_bytes=4 << 20),
        name="finish_spectra",
    )(total, record, table, received)

    y3, y2, y1 = [send(y, lambda yh, u, k, xh, v, m=m: (yh ^ m >> 1, u, k ^ (m & 1) << 1, xh, v)) for m in (3, 2, 1)]
    slices = shape((2, 2, count, lanes), bf16)
    y, mine, theirs = local(join_kernel, "join", (shape((2, 2) + y.shape, bf16), slices, slices), vmem(4))(
        y3, y2, y1, y
    )

    def to_partner(yh, u, k, xh, v):
        return yh, u, k ^ 1, xh, v

    quarter = local(core_kernel, "join_core", shape((2,) + mine.shape, bf16), vmem(2))(mine, send(theirs, to_partner))
    cross = send(quarter, lambda yh, u, k, xh, v: (yh, u, k, 1 - xh, v))
    q = local(choose_kernel, "choose", shape(quarter.shape, bf16), vmem(2))(quarter, cross)
    qs = [q] + [send(q, lambda yh, u, k, xh, v, m=m: (yh, u, k, xh, v ^ m)) for m in (1, 2, 3)]
    right = local(right_kernel, "right_side", shape((2 * QUARTERS, 2 * receivers, lanes), bf16), vmem(2))(
        y, send(y, to_partner)
    )

    total_shots = shots * lax.axis_size("shot")
    rows = ROWS * count
    scale = 1.0 / total_shots
    share = shape((rows, receivers), f32)
    width = 128
    wire = shape((rows * receivers // width, width), bf16)
    early = []
    for m in range(QUARTERS - 1):
        early += local(
            lambda *refs: gram_kernel(scale, *refs),
            "gram",
            (share, wire),
            vmem(2) + [pl.BlockSpec(memory_space=pl.ANY)],
        )(right, qs[m], early[-2] if early else right)
    p0, p1, p2, p3 = local(
        lambda *refs: last_kernel(scale, *refs),
        "last_gram",
        (share, wire, wire, wire),
        vmem(2 + len(early)),
        [pltpu.VMEM((QUARTERS,) + share.shape, f32), pltpu.VMEM((QUARTERS,) + wire.shape, bf16)],
    )(right, qs[3], *early)
    r1, r2, r3 = [send(p, lambda yh, u, k, xh, v, n=n: (yh, u ^ n, k, xh, v)) for n, p in ((1, p1), (2, p2), (3, p3))]
    sums = local(sum_kernel, "sum", share, vmem(4))(r2, r3, r1, p0)
    return sums.reshape(2, NF, count, receivers).transpose(0, 1, 3, 2)


def solution(mesh):
    return jax.shard_map(
        per_device,
        mesh=mesh,
        in_specs=(P("rcv", "shot"), P("shot")),
        out_specs=P(None, None, "rcv", "shot"),
        check_vma=False,
    )
```

```python
import math

import jax
import jax.numpy as jnp
import numpy as np
from jax import lax
from jax.experimental import pallas as pl
from jax.experimental.pallas import tpu as pltpu
from jax.sharding import PartitionSpec as P

import ml_dtypes

WIN = 2048
SPACING = 256
PAIR = 2 * SPACING
SPAN = WIN + PAIR
FREQ_BINS = (24, 40, 56, 80)
NF = len(FREQ_BINS)
ROWS = 2 * NF

SHOT_DEVICES = 32
RCV_DEVICES = 8
QUARTERS = 4
BLOCK = 128
LATE = WIN // SPACING


def dft_master():
    turns = np.arange(WIN)[None, :] * np.array(FREQ_BINS)[:, None] % WIN
    angle = 2.0 * math.pi / WIN * turns
    rows = np.concatenate([np.cos(angle), -np.sin(angle)], axis=0) / math.sqrt(WIN)
    rows = rows.astype(np.float32).astype(ml_dtypes.bfloat16).astype(np.float32)
    return rows


def send(block, to):
    route = []
    for shot in range(SHOT_DEVICES):
        for rcv in range(RCV_DEVICES):
            target = to(shot >> 4, (shot >> 2) & 3, shot & 3, rcv >> 2, rcv & 3)
            if target is not None:
                yh, u, k, xh, v = target
                route.append((shot * RCV_DEVICES + rcv, (yh << 4 | u << 2 | k) * RCV_DEVICES + (xh << 2 | v)))
    return lax.ppermute(block, ("shot", "rcv"), route)


shape = jax.ShapeDtypeStruct


def shot_index():
    return lax.axis_index("shot")


def vmem(count):
    return [pl.BlockSpec(memory_space=pltpu.VMEM)] * count


def shifted_blocks(table, by):
    rest, whole = by & (BLOCK - 1), by >= BLOCK
    zero = jnp.zeros((ROWS, BLOCK), table.dtype)
    turned = [pltpu.roll(table[:, BLOCK * i : BLOCK * (i + 1)], rest, 1) for i in range(WIN // BLOCK)]
    early = lax.broadcasted_iota(jnp.int32, zero.shape, 1) < rest
    part = [jnp.where(early, a, b) for a, b in zip([zero, *turned], [*turned, zero])]
    return [jnp.where(whole, a, b) for a, b in zip([zero, *part], [*part, zero])]


def pair_tables(table, first, second, low=0, high=SPAN):
    zero = jnp.zeros((ROWS, BLOCK), table.dtype)
    ahead = [zero] * (SPACING // BLOCK)
    rows = [shifted_blocks(table, first) + ahead, ahead + shifted_blocks(table, second)]
    rows = [jnp.concatenate(blocks[low // BLOCK : high // BLOCK], axis=1) for blocks in rows]
    return jnp.concatenate(rows, axis=0).astype(jnp.bfloat16)


def delay(fire, shot):
    return fire[shot] & (SPACING - 1)


def add_products(total, tables, first_pair, blocks):
    reach = SPAN // PAIR
    last_pair = first_pair + tables.shape[0] - 1
    for u, samples in blocks:
        low, high = max(first_pair, u - reach + 1), min(u, last_pair)
        left = jnp.concatenate(
            [tables[p - first_pair, :, PAIR * (u - p) : PAIR * (u - p + 1)] for p in range(low, high + 1)], axis=0
        )
        part = lax.dot_general(left, samples, (((1,), (1,)), ((), ())), preferred_element_type=jnp.float32)
        total[2 * ROWS * (low - first_pair) : 2 * ROWS * (high + 1 - first_pair), :] += part


def tail_kernel(fire_hbm, table_hbm, record, out, fire, table, tables, samples, message, sems):
    pairs = fire.shape[0] // 2
    late = LATE // 2
    start = record.shape[1] - samples.shape[1]
    copies = [
        pltpu.make_async_copy(fire_hbm, fire, sems.at[0]),
        pltpu.make_async_copy(table_hbm, table, sems.at[1]),
        pltpu.make_async_copy(record.at[:, start:], samples, sems.at[2]),
    ]
    for copy in copies:
        copy.start()
    message[...] = jnp.zeros_like(message)
    copies[0].wait()
    row = lax.broadcasted_iota(jnp.int32, (LATE, message.shape[1]), 0)
    delays = jnp.zeros(row.shape, jnp.int32)
    for i in range(LATE):
        delays = jnp.where(row == i, delay(fire, 2 * (pairs - late) + i), delays)
    message[ROWS * LATE :, :] = delays.astype(jnp.float32)
    copies[1].wait()
    master = table[...]
    for p in range(late):
        shot = 2 * (pairs - late + p)
        length = PAIR * (late - p)
        tables[p, :, :length] = pair_tables(master, delay(fire, shot), delay(fire, shot + 1), 0, length)
    copies[2].wait()
    blocks = [(pairs - late + v, samples[:, PAIR * v : PAIR * (v + 1)]) for v in range(late)]
    add_products(message, tables, pairs - late, blocks)
    out[...] = message[...].astype(out.dtype)


def own_kernel(fire, table, record, total, tables):
    pairs = record.shape[1] // PAIR
    master = table[...]
    for p in range(tables.shape[0]):
        tables[p] = pair_tables(master, delay(fire, 2 * p), delay(fire, 2 * p + 1))
    total[...] = jnp.zeros_like(total)
    add_products(total, tables, 0, [(u, record[:, PAIR * u : PAIR * (u + 1)]) for u in range(pairs)])


def finish_kernel(total, head, table, message, out, scratch, tables):
    own_rows = total.shape[0]
    lanes = scratch.shape[0]
    late = LATE // 2
    follows = (shot_index() > 0).astype(jnp.float32)
    master = table[...]
    message = message[...].astype(jnp.float32)
    for p in range(late):
        rows = [message[ROWS * LATE + 2 * p + i : ROWS * LATE + 2 * p + i + 1, :] for i in range(2)]
        first, second = [jnp.max(r).astype(jnp.int32) for r in rows]
        low = PAIR * (late - p)
        tables[p, :, low:] = pair_tables(master, first, second, low)
    scratch[own_rows:, :] = jnp.zeros((lanes - own_rows, total.shape[1]), jnp.float32)
    blocks = [(late + v, head[:, PAIR * v : PAIR * (v + 1)]) for v in range(late)]
    add_products(scratch.at[own_rows:, :], tables, 0, blocks)
    scratch[own_rows:, :] = message[: ROWS * LATE, :] + follows * scratch[own_rows:, :]
    scratch[:own_rows, :] = total[...]
    turn_over(scratch, out)


def turn_over(scratch, out):
    shots = scratch.shape[0] // ROWS
    ordered = jnp.concatenate([scratch[pl.ds(c, shots, stride=ROWS), :] for c in range(ROWS)], axis=0)
    turned = ordered.T
    count = out.shape[1]
    for k in range(QUARTERS):
        out[k] = turned[count * k : count * (k + 1), :].astype(out.dtype)


def join_kernel(y3, y2, y1, y0, out, mine, theirs):
    shot = shot_index()
    yh, k = shot >> 4, shot & 3
    z0 = k >> 1
    for m, block in enumerate((y0, y1, y2, y3)):
        place = z0 ^ (m & 1), yh ^ (m >> 1)
        out[place] = block[...]
        mine[place] = block[k]
        theirs[place] = block[k ^ 1]


def core_kernel(own, other, out):
    c = shot_index() & 1
    out[c] = own[...]
    out[1 - c] = other[...]


def choose_kernel(own, cross, out):
    straight = (shot_index() >> 4) == (lax.axis_index("rcv") >> 2)

    @pl.when(straight)
    def _():
        out[...] = own[...]

    @pl.when(jnp.logical_not(straight))
    def _():
        out[...] = cross[...]


def right_kernel(own, other, right):
    c = shot_index() & 1
    half = right.shape[2] // 2
    parts = right.shape[0] // 2
    for here, block in ((c, own), (1 - c, other)):
        for part in range(parts):
            z = block[part >> 1, part & 1].astype(jnp.float32).reshape(right.shape[1] // 2, 2 * half)
            w = jnp.concatenate([-z[:, half:], z[:, :half]], axis=1)
            right[parts * here + part] = jnp.concatenate([z, w], axis=0).astype(jnp.bfloat16)


def products(scale, right, q):
    count, lanes = q.shape[3:]
    half = lanes // 2
    span = right.shape[1] // 2
    lane = lax.broadcasted_iota(jnp.int32, (count, lanes), 1) % half // (half // NF)
    acc = jnp.zeros((NF * count, 2 * span), jnp.float32)
    for part in range(right.shape[0]):
        rows = q[part >> 2, (part >> 1) & 1, part & 1].astype(jnp.float32)
        left = jnp.concatenate([jnp.where(lane == f, rows, 0.0) for f in range(NF)], axis=0)
        acc = acc + lax.dot_general(
            left.astype(jnp.bfloat16), right[part], (((1,), (1,)), ((), ())), preferred_element_type=jnp.float32
        )
    return jnp.concatenate([acc[:, :span] * scale, acc[:, span:] * scale], axis=0)


def gram_kernel(scale, right, q, before, out, packed):
    out[...] = products(scale, right, q)
    pack(out, packed)


def last_kernel(scale, right, q, *refs):
    early, (p0, p1, p2, p3, total, wire) = refs[:-6], refs[-6:]
    turn = ((shot_index() >> 2) ^ lax.axis_index("rcv")) & 3
    for m in range(QUARTERS - 1):
        total[turn ^ m] = early[2 * m][...]
        wire[turn ^ m] = early[2 * m + 1][...]
    last = turn ^ (QUARTERS - 1)
    total[last] = products(scale, right, q)
    pack(total.at[last], wire.at[last])
    p0[...] = total[0]
    for n, out in ((1, p1), (2, p2), (3, p3)):
        out[...] = wire[n]


def pack(share, out):
    rows, width = out.shape
    lanes = share.shape[1]
    rest = width - lanes
    out[:, :lanes] = share[:rows].astype(out.dtype)
    pieces = [share[rows:, rest * g : rest * (g + 1)] for g in range(lanes // rest)]
    out[:, lanes:] = jnp.concatenate(pieces, axis=0).astype(out.dtype)


def sum_kernel(r2, r3, r1, p0, out):
    shares = r1[...].astype(jnp.float32) + r2[...].astype(jnp.float32) + r3[...].astype(jnp.float32)
    rows = shares.shape[0]
    lanes = out.shape[1]
    high = out.shape[0] - rows
    out[:rows] = p0[:rows] + shares[:, :lanes]
    pieces = [shares[high * g : high * (g + 1), lanes:] for g in range(rows // high)]
    out[rows:] = p0[rows:] + jnp.concatenate(pieces, axis=1)


def local(kernel, name, out_shape, in_specs, scratch=(), limit=4):
    single = not isinstance(out_shape, tuple)
    return pl.pallas_call(
        kernel,
        out_shape=out_shape,
        in_specs=in_specs,
        out_specs=vmem(1)[0] if single else tuple(vmem(len(out_shape))),
        scratch_shapes=list(scratch),
        compiler_params=pltpu.CompilerParams(vmem_limit_bytes=limit << 20),
        name=name,
    )


def per_device(record, shot_fire_samples):
    receivers, samples = record.shape
    shots = shot_fire_samples.shape[0]
    pairs, late = shots // 2, LATE // 2
    lanes = ROWS * shots
    late_rows = ROWS * LATE
    count = receivers // QUARTERS
    bf16, f32 = jnp.bfloat16, jnp.float32
    table = jnp.asarray(dft_master())
    smem, hbm = pl.BlockSpec(memory_space=pltpu.SMEM), pl.BlockSpec(memory_space=pltpu.HBM)

    message = local(
        tail_kernel,
        "tail_spectra",
        shape((late_rows + LATE, receivers), bf16),
        [hbm] * 3,
        [
            pltpu.SMEM((shots,), jnp.int32),
            pltpu.VMEM(table.shape, f32),
            pltpu.VMEM((late, 2 * ROWS, SPAN), bf16),
            pltpu.VMEM((receivers, WIN), bf16),
            pltpu.VMEM((late_rows + LATE, receivers), f32),
            pltpu.SemaphoreType.DMA((3,)),
        ],
    )(*(pltpu.with_memory_space_constraint(a, pltpu.HBM) for a in (shot_fire_samples, table, record)))

    def following(yh, u, k, xh, v):
        shot = ((yh << 4 | u << 2 | k) + 1) % SHOT_DEVICES
        return shot >> 4, (shot >> 2) & 3, shot & 3, xh, v

    received = send(message, following)
    total = local(
        own_kernel,
        "own_spectra",
        shape((lanes - late_rows, receivers), f32),
        [smem] + vmem(2),
        [pltpu.VMEM((pairs - late, 2 * ROWS, SPAN), bf16)],
    )(shot_fire_samples, table, record)
    y = pl.pallas_call(
        finish_kernel,
        grid=(1,),
        out_shape=shape((QUARTERS, count, lanes), bf16),
        in_specs=[
            pl.BlockSpec(total.shape, lambda i: (0, 0)),
            pl.BlockSpec((receivers, WIN), lambda i: (0, 0)),
            pl.BlockSpec(table.shape, lambda i: (0, 0)),
            pl.BlockSpec(received.shape, lambda i: (0, 0)),
        ],
        out_specs=pl.BlockSpec((QUARTERS, count, lanes), lambda i: (0, 0, 0)),
        scratch_shapes=[pltpu.VMEM((lanes, receivers), f32), pltpu.VMEM((late, 2 * ROWS, SPAN), bf16)],
        compiler_params=pltpu.CompilerParams(vmem_limit_bytes=4 << 20),
        name="finish_spectra",
    )(total, record, table, received)

    y3, y2, y1 = [send(y, lambda yh, u, k, xh, v, m=m: (yh ^ m >> 1, u, k ^ (m & 1) << 1, xh, v)) for m in (3, 2, 1)]
    slices = shape((2, 2, count, lanes), bf16)
    y, mine, theirs = local(join_kernel, "join", (shape((2, 2) + y.shape, bf16), slices, slices), vmem(4))(
        y3, y2, y1, y
    )

    def to_partner(yh, u, k, xh, v):
        return yh, u, k ^ 1, xh, v

    quarter = local(core_kernel, "join_core", shape((2,) + mine.shape, bf16), vmem(2))(mine, send(theirs, to_partner))
    cross = send(quarter, lambda yh, u, k, xh, v: (yh, u, k, 1 - xh, v))
    q = local(choose_kernel, "choose", shape(quarter.shape, bf16), vmem(2))(quarter, cross)
    qs = [q] + [send(q, lambda yh, u, k, xh, v, m=m: (yh, u, k, xh, v ^ m)) for m in (1, 2, 3)]
    right = local(right_kernel, "right_side", shape((2 * QUARTERS, 2 * receivers, lanes), bf16), vmem(2))(
        y, send(y, to_partner)
    )

    total_shots = shots * lax.axis_size("shot")
    rows = ROWS * count
    scale = 1.0 / total_shots
    share = shape((rows, receivers), f32)
    width = 128
    wire = shape((rows * receivers // width, width), bf16)
    early = []
    for m in range(QUARTERS - 1):
        early += local(
            lambda *refs: gram_kernel(scale, *refs),
            "gram",
            (share, wire),
            vmem(2) + [pl.BlockSpec(memory_space=pl.ANY)],
        )(right, qs[m], early[-2] if early else right)
    p0, p1, p2, p3 = local(
        lambda *refs: last_kernel(scale, *refs),
        "last_gram",
        (share, wire, wire, wire),
        vmem(2 + len(early)),
        [pltpu.VMEM((QUARTERS,) + share.shape, f32), pltpu.VMEM((QUARTERS,) + wire.shape, bf16)],
    )(right, qs[3], *early)
    r1, r2, r3 = [send(p, lambda yh, u, k, xh, v, n=n: (yh, u ^ n, k, xh, v)) for n, p in ((1, p1), (2, p2), (3, p3))]
    sums = local(sum_kernel, "sum", share, vmem(4))(r2, r3, r1, p0)
    return sums.reshape(2, NF, count, receivers).transpose(0, 1, 3, 2)


def solution(mesh):
    return jax.shard_map(
        per_device,
        mesh=mesh,
        in_specs=(P("rcv", "shot"), P("shot")),
        out_specs=P(None, None, "rcv", "shot"),
        check_vma=False,
    )
```

```python
import math

import jax
import jax.numpy as jnp
import numpy as np
from jax import lax
from jax.experimental import pallas as pl
from jax.experimental.pallas import tpu as pltpu
from jax.sharding import PartitionSpec as P

import ml_dtypes

WIN = 2048
SPACING = 256
PAIR = 2 * SPACING
SPAN = WIN + PAIR
FREQ_BINS = (24, 40, 56, 80)
NF = len(FREQ_BINS)
ROWS = 2 * NF

SHOT_DEVICES = 32
RCV_DEVICES = 8
QUARTERS = 4
BLOCK = 128
LATE = WIN // SPACING


def dft_master():
    turns = np.arange(WIN)[None, :] * np.array(FREQ_BINS)[:, None] % WIN
    angle = 2.0 * math.pi / WIN * turns
    rows = np.concatenate([np.cos(angle), -np.sin(angle)], axis=0) / math.sqrt(WIN)
    rows = rows.astype(np.float32).astype(ml_dtypes.bfloat16).astype(np.float32)
    return rows


def send(block, to):
    route = []
    for shot in range(SHOT_DEVICES):
        for rcv in range(RCV_DEVICES):
            target = to(shot >> 4, (shot >> 2) & 3, shot & 3, rcv >> 2, rcv & 3)
            if target is not None:
                yh, u, k, xh, v = target
                route.append((shot * RCV_DEVICES + rcv, (yh << 4 | u << 2 | k) * RCV_DEVICES + (xh << 2 | v)))
    return lax.ppermute(block, ("shot", "rcv"), route)


shape = jax.ShapeDtypeStruct


def shot_index():
    return lax.axis_index("shot")


def vmem(count):
    return [pl.BlockSpec(memory_space=pltpu.VMEM)] * count


def shifted_blocks(table, by):
    rest, whole = by & (BLOCK - 1), by >= BLOCK
    zero = jnp.zeros((ROWS, BLOCK), table.dtype)
    turned = [pltpu.roll(table[:, BLOCK * i : BLOCK * (i + 1)], rest, 1) for i in range(WIN // BLOCK)]
    early = lax.broadcasted_iota(jnp.int32, zero.shape, 1) < rest
    part = [jnp.where(early, a, b) for a, b in zip([zero, *turned], [*turned, zero])]
    return [jnp.where(whole, a, b) for a, b in zip([zero, *part], [*part, zero])]


def pair_tables(table, first, second, low=0, high=SPAN):
    zero = jnp.zeros((ROWS, BLOCK), table.dtype)
    ahead = [zero] * (SPACING // BLOCK)
    rows = [shifted_blocks(table, first) + ahead, ahead + shifted_blocks(table, second)]
    rows = [jnp.concatenate(blocks[low // BLOCK : high // BLOCK], axis=1) for blocks in rows]
    return jnp.concatenate(rows, axis=0).astype(jnp.bfloat16)


def delay(fire, shot):
    return fire[shot] & (SPACING - 1)


def add_products(total, tables, first_pair, blocks):
    reach = SPAN // PAIR
    last_pair = first_pair + tables.shape[0] - 1
    for u, samples in blocks:
        low, high = max(first_pair, u - reach + 1), min(u, last_pair)
        left = jnp.concatenate(
            [tables[p - first_pair, :, PAIR * (u - p) : PAIR * (u - p + 1)] for p in range(low, high + 1)], axis=0
        )
        part = lax.dot_general(left, samples, (((1,), (1,)), ((), ())), preferred_element_type=jnp.float32)
        total[2 * ROWS * (low - first_pair) : 2 * ROWS * (high + 1 - first_pair), :] += part


def tail_kernel(fire_hbm, table_hbm, record, out, fire, table, tables, samples, message, sems):
    pairs = fire.shape[0] // 2
    late = LATE // 2
    start = record.shape[1] - samples.shape[1]
    copies = [
        pltpu.make_async_copy(fire_hbm, fire, sems.at[0]),
        pltpu.make_async_copy(table_hbm, table, sems.at[1]),
        pltpu.make_async_copy(record.at[:, start:], samples, sems.at[2]),
    ]
    for copy in copies:
        copy.start()
    message[...] = jnp.zeros_like(message)
    copies[0].wait()
    row = lax.broadcasted_iota(jnp.int32, (LATE, message.shape[1]), 0)
    delays = jnp.zeros(row.shape, jnp.int32)
    for i in range(LATE):
        delays = jnp.where(row == i, delay(fire, 2 * (pairs - late) + i), delays)
    message[ROWS * LATE :, :] = delays.astype(jnp.float32)
    copies[1].wait()
    master = table[...]
    for p in range(late):
        shot = 2 * (pairs - late + p)
        length = PAIR * (late - p)
        tables[p, :, :length] = pair_tables(master, delay(fire, shot), delay(fire, shot + 1), 0, length)
    copies[2].wait()
    blocks = [(pairs - late + v, samples[:, PAIR * v : PAIR * (v + 1)]) for v in range(late)]
    add_products(message, tables, pairs - late, blocks)
    out[...] = message[...].astype(out.dtype)


def own_kernel(fire, table, record, total, tables):
    pairs = record.shape[1] // PAIR
    master = table[...]
    for p in range(tables.shape[0]):
        tables[p] = pair_tables(master, delay(fire, 2 * p), delay(fire, 2 * p + 1))
    total[...] = jnp.zeros_like(total)
    add_products(total, tables, 0, [(u, record[:, PAIR * u : PAIR * (u + 1)]) for u in range(pairs)])


def finish_kernel(total, head, table, message, out, scratch, tables):
    own_rows = total.shape[0]
    lanes = scratch.shape[0]
    late = LATE // 2
    follows = (shot_index() > 0).astype(jnp.float32)
    master = table[...]
    message = message[...].astype(jnp.float32)
    for p in range(late):
        rows = [message[ROWS * LATE + 2 * p + i : ROWS * LATE + 2 * p + i + 1, :] for i in range(2)]
        first, second = [jnp.max(r).astype(jnp.int32) for r in rows]
        low = PAIR * (late - p)
        tables[p, :, low:] = pair_tables(master, first, second, low)
    scratch[own_rows:, :] = jnp.zeros((lanes - own_rows, total.shape[1]), jnp.float32)
    blocks = [(late + v, head[:, PAIR * v : PAIR * (v + 1)]) for v in range(late)]
    add_products(scratch.at[own_rows:, :], tables, 0, blocks)
    scratch[own_rows:, :] = message[: ROWS * LATE, :] + follows * scratch[own_rows:, :]
    scratch[:own_rows, :] = total[...]
    turn_over(scratch, out)


def turn_over(scratch, out):
    shots = scratch.shape[0] // ROWS
    ordered = jnp.concatenate([scratch[pl.ds(c, shots, stride=ROWS), :] for c in range(ROWS)], axis=0)
    turned = ordered.T
    count = out.shape[1]
    for k in range(QUARTERS):
        out[k] = turned[count * k : count * (k + 1), :].astype(out.dtype)


def join_kernel(y3, y2, y1, y0, out, mine, theirs):
    shot = shot_index()
    yh, k = shot >> 4, shot & 3
    z0 = k >> 1
    for m, block in enumerate((y0, y1, y2, y3)):
        place = z0 ^ (m & 1), yh ^ (m >> 1)
        out[place] = block[...]
        mine[place] = block[k]
        theirs[place] = block[k ^ 1]


def core_kernel(own, other, out):
    c = shot_index() & 1
    out[c] = own[...]
    out[1 - c] = other[...]


def choose_kernel(own, cross, out):
    straight = (shot_index() >> 4) == (lax.axis_index("rcv") >> 2)

    @pl.when(straight)
    def _():
        out[...] = own[...]

    @pl.when(jnp.logical_not(straight))
    def _():
        out[...] = cross[...]


def right_kernel(own, other, right):
    c = shot_index() & 1
    half = right.shape[2] // 2
    parts = right.shape[0] // 2
    for here, block in ((c, own), (1 - c, other)):
        for part in range(parts):
            z = block[part >> 1, part & 1].astype(jnp.float32).reshape(right.shape[1] // 2, 2 * half)
            w = jnp.concatenate([-z[:, half:], z[:, :half]], axis=1)
            right[parts * here + part] = jnp.concatenate([z, w], axis=0).astype(jnp.bfloat16)


def products(scale, right, q):
    count, lanes = q.shape[3:]
    half = lanes // 2
    span = right.shape[1] // 2
    lane = lax.broadcasted_iota(jnp.int32, (count, lanes), 1) % half // (half // NF)
    acc = jnp.zeros((NF * count, 2 * span), jnp.float32)
    for part in range(right.shape[0]):
        rows = q[part >> 2, (part >> 1) & 1, part & 1].astype(jnp.float32)
        left = jnp.concatenate([jnp.where(lane == f, rows, 0.0) for f in range(NF)], axis=0)
        acc = acc + lax.dot_general(
            left.astype(jnp.bfloat16), right[part], (((1,), (1,)), ((), ())), preferred_element_type=jnp.float32
        )
    return jnp.concatenate([acc[:, :span] * scale, acc[:, span:] * scale], axis=0)


def gram_kernel(scale, right, q, before, out, packed):
    out[...] = products(scale, right, q)
    pack(out, packed)


def last_kernel(scale, right, q, *refs):
    early, (p0, p1, p2, p3, total, wire) = refs[:-6], refs[-6:]
    turn = ((shot_index() >> 2) ^ lax.axis_index("rcv")) & 3
    for m in range(QUARTERS - 1):
        total[turn ^ m] = early[2 * m][...]
        wire[turn ^ m] = early[2 * m + 1][...]
    last = turn ^ (QUARTERS - 1)
    total[last] = products(scale, right, q)
    pack(total.at[last], wire.at[last])
    p0[...] = total[0]
    for n, out in ((1, p1), (2, p2), (3, p3)):
        out[...] = wire[n]


def pack(share, out):
    rows, width = out.shape
    lanes = share.shape[1]
    rest = width - lanes
    out[:, :lanes] = share[:rows].astype(out.dtype)
    pieces = [share[rows:, rest * g : rest * (g + 1)] for g in range(lanes // rest)]
    out[:, lanes:] = jnp.concatenate(pieces, axis=0).astype(out.dtype)


def sum_kernel(r2, r1, r3, p0, out):
    shares = r1[...].astype(jnp.float32) + r2[...].astype(jnp.float32) + r3[...].astype(jnp.float32)
    rows = shares.shape[0]
    lanes = out.shape[1]
    high = out.shape[0] - rows
    out[:rows] = p0[:rows] + shares[:, :lanes]
    pieces = [shares[high * g : high * (g + 1), lanes:] for g in range(rows // high)]
    out[rows:] = p0[rows:] + jnp.concatenate(pieces, axis=1)


def local(kernel, name, out_shape, in_specs, scratch=(), limit=4):
    single = not isinstance(out_shape, tuple)
    return pl.pallas_call(
        kernel,
        out_shape=out_shape,
        in_specs=in_specs,
        out_specs=vmem(1)[0] if single else tuple(vmem(len(out_shape))),
        scratch_shapes=list(scratch),
        compiler_params=pltpu.CompilerParams(vmem_limit_bytes=limit << 20),
        name=name,
    )


def per_device(record, shot_fire_samples):
    receivers, samples = record.shape
    shots = shot_fire_samples.shape[0]
    pairs, late = shots // 2, LATE // 2
    lanes = ROWS * shots
    late_rows = ROWS * LATE
    count = receivers // QUARTERS
    bf16, f32 = jnp.bfloat16, jnp.float32
    table = jnp.asarray(dft_master())
    smem, hbm = pl.BlockSpec(memory_space=pltpu.SMEM), pl.BlockSpec(memory_space=pltpu.HBM)

    message = local(
        tail_kernel,
        "tail_spectra",
        shape((late_rows + LATE, receivers), bf16),
        [hbm] * 3,
        [
            pltpu.SMEM((shots,), jnp.int32),
            pltpu.VMEM(table.shape, f32),
            pltpu.VMEM((late, 2 * ROWS, SPAN), bf16),
            pltpu.VMEM((receivers, WIN), bf16),
            pltpu.VMEM((late_rows + LATE, receivers), f32),
            pltpu.SemaphoreType.DMA((3,)),
        ],
    )(*(pltpu.with_memory_space_constraint(a, pltpu.HBM) for a in (shot_fire_samples, table, record)))

    def following(yh, u, k, xh, v):
        shot = ((yh << 4 | u << 2 | k) + 1) % SHOT_DEVICES
        return shot >> 4, (shot >> 2) & 3, shot & 3, xh, v

    received = send(message, following)
    total = local(
        own_kernel,
        "own_spectra",
        shape((lanes - late_rows, receivers), f32),
        [smem] + vmem(2),
        [pltpu.VMEM((pairs - late, 2 * ROWS, SPAN), bf16)],
    )(shot_fire_samples, table, record)
    y = pl.pallas_call(
        finish_kernel,
        grid=(1,),
        out_shape=shape((QUARTERS, count, lanes), bf16),
        in_specs=[
            pl.BlockSpec(total.shape, lambda i: (0, 0)),
            pl.BlockSpec((receivers, WIN), lambda i: (0, 0)),
            pl.BlockSpec(table.shape, lambda i: (0, 0)),
            pl.BlockSpec(received.shape, lambda i: (0, 0)),
        ],
        out_specs=pl.BlockSpec((QUARTERS, count, lanes), lambda i: (0, 0, 0)),
        scratch_shapes=[pltpu.VMEM((lanes, receivers), f32), pltpu.VMEM((late, 2 * ROWS, SPAN), bf16)],
        compiler_params=pltpu.CompilerParams(vmem_limit_bytes=4 << 20),
        name="finish_spectra",
    )(total, record, table, received)

    y3, y2, y1 = [send(y, lambda yh, u, k, xh, v, m=m: (yh ^ m >> 1, u, k ^ (m & 1) << 1, xh, v)) for m in (3, 2, 1)]
    slices = shape((2, 2, count, lanes), bf16)
    y, mine, theirs = local(join_kernel, "join", (shape((2, 2) + y.shape, bf16), slices, slices), vmem(4))(
        y3, y2, y1, y
    )

    def to_partner(yh, u, k, xh, v):
        return yh, u, k ^ 1, xh, v

    quarter = local(core_kernel, "join_core", shape((2,) + mine.shape, bf16), vmem(2))(mine, send(theirs, to_partner))
    cross = send(quarter, lambda yh, u, k, xh, v: (yh, u, k, 1 - xh, v))
    q = local(choose_kernel, "choose", shape(quarter.shape, bf16), vmem(2))(quarter, cross)
    qs = [q] + [send(q, lambda yh, u, k, xh, v, m=m: (yh, u, k, xh, v ^ m)) for m in (1, 2, 3)]
    right = local(right_kernel, "right_side", shape((2 * QUARTERS, 2 * receivers, lanes), bf16), vmem(2))(
        y, send(y, to_partner)
    )

    total_shots = shots * lax.axis_size("shot")
    rows = ROWS * count
    scale = 1.0 / total_shots
    share = shape((rows, receivers), f32)
    width = 128
    wire = shape((rows * receivers // width, width), bf16)
    early = []
    for m in range(QUARTERS - 1):
        early += local(
            lambda *refs: gram_kernel(scale, *refs),
            "gram",
            (share, wire),
            vmem(2) + [pl.BlockSpec(memory_space=pl.ANY)],
        )(right, qs[m], early[-2] if early else right)
    p0, p1, p2, p3 = local(
        lambda *refs: last_kernel(scale, *refs),
        "last_gram",
        (share, wire, wire, wire),
        vmem(2 + len(early)),
        [pltpu.VMEM((QUARTERS,) + share.shape, f32), pltpu.VMEM((QUARTERS,) + wire.shape, bf16)],
    )(right, qs[3], *early)
    r1, r2, r3 = [send(p, lambda yh, u, k, xh, v, n=n: (yh, u ^ n, k, xh, v)) for n, p in ((1, p1), (2, p2), (3, p3))]
    sums = local(sum_kernel, "sum", share, vmem(4))(r2, r1, r3, p0)
    return sums.reshape(2, NF, count, receivers).transpose(0, 1, 3, 2)


def solution(mesh):
    return jax.shard_map(
        per_device,
        mesh=mesh,
        in_specs=(P("rcv", "shot"), P("shot")),
        out_specs=P(None, None, "rcv", "shot"),
        check_vma=False,
    )
```

```python
import math

import jax
import jax.numpy as jnp
import numpy as np
from jax import lax
from jax.experimental import pallas as pl
from jax.experimental.pallas import tpu as pltpu
from jax.sharding import PartitionSpec as P

import ml_dtypes

WIN = 2048
SPACING = 256
PAIR = 2 * SPACING
SPAN = WIN + PAIR
FREQ_BINS = (24, 40, 56, 80)
NF = len(FREQ_BINS)
ROWS = 2 * NF

SHOT_DEVICES = 32
RCV_DEVICES = 8
QUARTERS = 4
BLOCK = 128
LATE = WIN // SPACING


def dft_master():
    turns = np.arange(WIN)[None, :] * np.array(FREQ_BINS)[:, None] % WIN
    angle = 2.0 * math.pi / WIN * turns
    rows = np.concatenate([np.cos(angle), -np.sin(angle)], axis=0) / math.sqrt(WIN)
    rows = rows.astype(np.float32).astype(ml_dtypes.bfloat16).astype(np.float32)
    return rows


def send(block, to):
    route = []
    for shot in range(SHOT_DEVICES):
        for rcv in range(RCV_DEVICES):
            target = to(shot >> 4, (shot >> 2) & 3, shot & 3, rcv >> 2, rcv & 3)
            if target is not None:
                yh, u, k, xh, v = target
                route.append((shot * RCV_DEVICES + rcv, (yh << 4 | u << 2 | k) * RCV_DEVICES + (xh << 2 | v)))
    return lax.ppermute(block, ("shot", "rcv"), route)


shape = jax.ShapeDtypeStruct


def shot_index():
    return lax.axis_index("shot")


def vmem(count):
    return [pl.BlockSpec(memory_space=pltpu.VMEM)] * count


def shifted_blocks(table, by):
    rest, whole = by & (BLOCK - 1), by >= BLOCK
    zero = jnp.zeros((ROWS, BLOCK), table.dtype)
    turned = [pltpu.roll(table[:, BLOCK * i : BLOCK * (i + 1)], rest, 1) for i in range(WIN // BLOCK)]
    early = lax.broadcasted_iota(jnp.int32, zero.shape, 1) < rest
    part = [jnp.where(early, a, b) for a, b in zip([zero, *turned], [*turned, zero])]
    return [jnp.where(whole, a, b) for a, b in zip([zero, *part], [*part, zero])]


def pair_tables(table, first, second, low=0, high=SPAN):
    zero = jnp.zeros((ROWS, BLOCK), table.dtype)
    ahead = [zero] * (SPACING // BLOCK)
    rows = [shifted_blocks(table, first) + ahead, ahead + shifted_blocks(table, second)]
    rows = [jnp.concatenate(blocks[low // BLOCK : high // BLOCK], axis=1) for blocks in rows]
    return jnp.concatenate(rows, axis=0).astype(jnp.bfloat16)


def delay(fire, shot):
    return fire[shot] & (SPACING - 1)


def add_products(total, tables, first_pair, blocks):
    reach = SPAN // PAIR
    last_pair = first_pair + tables.shape[0] - 1
    for u, samples in blocks:
        low, high = max(first_pair, u - reach + 1), min(u, last_pair)
        left = jnp.concatenate(
            [tables[p - first_pair, :, PAIR * (u - p) : PAIR * (u - p + 1)] for p in range(low, high + 1)], axis=0
        )
        part = lax.dot_general(left, samples, (((1,), (1,)), ((), ())), preferred_element_type=jnp.float32)
        total[2 * ROWS * (low - first_pair) : 2 * ROWS * (high + 1 - first_pair), :] += part


def tail_kernel(fire_hbm, table_hbm, record, out, fire, table, tables, samples, message, sems):
    pairs = fire.shape[0] // 2
    late = LATE // 2
    start = record.shape[1] - samples.shape[1]
    copies = [
        pltpu.make_async_copy(fire_hbm, fire, sems.at[0]),
        pltpu.make_async_copy(table_hbm, table, sems.at[1]),
        pltpu.make_async_copy(record.at[:, start:], samples, sems.at[2]),
    ]
    for copy in copies:
        copy.start()
    message[...] = jnp.zeros_like(message)
    copies[0].wait()
    row = lax.broadcasted_iota(jnp.int32, (LATE, message.shape[1]), 0)
    delays = jnp.zeros(row.shape, jnp.int32)
    for i in range(LATE):
        delays = jnp.where(row == i, delay(fire, 2 * (pairs - late) + i), delays)
    message[ROWS * LATE :, :] = delays.astype(jnp.float32)
    copies[1].wait()
    master = table[...]
    for p in range(late):
        shot = 2 * (pairs - late + p)
        length = PAIR * (late - p)
        tables[p, :, :length] = pair_tables(master, delay(fire, shot), delay(fire, shot + 1), 0, length)
    copies[2].wait()
    blocks = [(pairs - late + v, samples[:, PAIR * v : PAIR * (v + 1)]) for v in range(late)]
    add_products(message, tables, pairs - late, blocks)
    out[...] = message[...].astype(out.dtype)


def own_kernel(fire, table, record, total, tables):
    pairs = record.shape[1] // PAIR
    master = table[...]
    for p in range(tables.shape[0]):
        tables[p] = pair_tables(master, delay(fire, 2 * p), delay(fire, 2 * p + 1))
    total[...] = jnp.zeros_like(total)
    add_products(total, tables, 0, [(u, record[:, PAIR * u : PAIR * (u + 1)]) for u in range(pairs)])


def finish_kernel(total, head, table, message, out, scratch, tables):
    own_rows = total.shape[0]
    lanes = scratch.shape[0]
    late = LATE // 2
    follows = (shot_index() > 0).astype(jnp.float32)
    master = table[...]
    message = message[...].astype(jnp.float32)
    for p in range(late):
        rows = [message[ROWS * LATE + 2 * p + i : ROWS * LATE + 2 * p + i + 1, :] for i in range(2)]
        first, second = [jnp.max(r).astype(jnp.int32) for r in rows]
        low = PAIR * (late - p)
        tables[p, :, low:] = pair_tables(master, first, second, low)
    scratch[own_rows:, :] = jnp.zeros((lanes - own_rows, total.shape[1]), jnp.float32)
    blocks = [(late + v, head[:, PAIR * v : PAIR * (v + 1)]) for v in range(late)]
    add_products(scratch.at[own_rows:, :], tables, 0, blocks)
    scratch[own_rows:, :] = message[: ROWS * LATE, :] + follows * scratch[own_rows:, :]
    scratch[:own_rows, :] = total[...]
    turn_over(scratch, out)


def turn_over(scratch, out):
    shots = scratch.shape[0] // ROWS
    ordered = jnp.concatenate([scratch[pl.ds(c, shots, stride=ROWS), :] for c in range(ROWS)], axis=0)
    turned = ordered.T
    count = out.shape[1]
    for k in range(QUARTERS):
        out[k] = turned[count * k : count * (k + 1), :].astype(out.dtype)


def join_kernel(y3, y2, y1, y0, out, mine, theirs):
    shot = shot_index()
    yh, k = shot >> 4, shot & 3
    z0 = k >> 1
    for m, block in enumerate((y0, y1, y2, y3)):
        place = z0 ^ (m & 1), yh ^ (m >> 1)
        out[place] = block[...]
        mine[place] = block[k]
        theirs[place] = block[k ^ 1]


def core_kernel(own, other, out):
    c = shot_index() & 1
    out[c] = own[...]
    out[1 - c] = other[...]


def choose_kernel(own, cross, out):
    straight = (shot_index() >> 4) == (lax.axis_index("rcv") >> 2)

    @pl.when(straight)
    def _():
        out[...] = own[...]

    @pl.when(jnp.logical_not(straight))
    def _():
        out[...] = cross[...]


def right_kernel(own, other, right):
    c = shot_index() & 1
    half = right.shape[2] // 2
    parts = right.shape[0] // 2
    for here, block in ((c, own), (1 - c, other)):
        for part in range(parts):
            z = block[part >> 1, part & 1].astype(jnp.float32).reshape(right.shape[1] // 2, 2 * half)
            w = jnp.concatenate([-z[:, half:], z[:, :half]], axis=1)
            right[parts * here + part] = jnp.concatenate([z, w], axis=0).astype(jnp.bfloat16)


def products(scale, right, q):
    count, lanes = q.shape[3:]
    half = lanes // 2
    span = right.shape[1] // 2
    lane = lax.broadcasted_iota(jnp.int32, (count, lanes), 1) % half // (half // NF)
    acc = jnp.zeros((NF * count, 2 * span), jnp.float32)
    for part in range(right.shape[0]):
        rows = q[part >> 2, (part >> 1) & 1, part & 1].astype(jnp.float32)
        left = jnp.concatenate([jnp.where(lane == f, rows, 0.0) for f in range(NF)], axis=0)
        acc = acc + lax.dot_general(
            left.astype(jnp.bfloat16), right[part], (((1,), (1,)), ((), ())), preferred_element_type=jnp.float32
        )
    return jnp.concatenate([acc[:, :span] * scale, acc[:, span:] * scale], axis=0)


def gram_kernel(scale, right, q, before, out, packed):
    out[...] = products(scale, right, q)
    pack(out, packed)


def last_kernel(scale, right, q, *refs):
    early, (p0, p1, p2, p3, total, wire) = refs[:-6], refs[-6:]
    turn = ((shot_index() >> 2) ^ lax.axis_index("rcv")) & 3
    for m in range(QUARTERS - 1):
        total[turn ^ m] = early[2 * m][...]
        wire[turn ^ m] = early[2 * m + 1][...]
    last = turn ^ (QUARTERS - 1)
    total[last] = products(scale, right, q)
    pack(total.at[last], wire.at[last])
    p0[...] = total[0]
    for n, out in ((1, p1), (2, p2), (3, p3)):
        out[...] = wire[n]


def pack(share, out):
    rows, width = out.shape
    lanes = share.shape[1]
    rest = width - lanes
    out[:, :lanes] = share[:rows].astype(out.dtype)
    pieces = [share[rows:, rest * g : rest * (g + 1)] for g in range(lanes // rest)]
    out[:, lanes:] = jnp.concatenate(pieces, axis=0).astype(out.dtype)


def sum_kernel(r3, r2, r1, p0, out):
    shares = r1[...].astype(jnp.float32) + r2[...].astype(jnp.float32) + r3[...].astype(jnp.float32)
    rows = shares.shape[0]
    lanes = out.shape[1]
    high = out.shape[0] - rows
    out[:rows] = p0[:rows] + shares[:, :lanes]
    pieces = [shares[high * g : high * (g + 1), lanes:] for g in range(rows // high)]
    out[rows:] = p0[rows:] + jnp.concatenate(pieces, axis=1)


def local(kernel, name, out_shape, in_specs, scratch=(), limit=4):
    single = not isinstance(out_shape, tuple)
    return pl.pallas_call(
        kernel,
        out_shape=out_shape,
        in_specs=in_specs,
        out_specs=vmem(1)[0] if single else tuple(vmem(len(out_shape))),
        scratch_shapes=list(scratch),
        compiler_params=pltpu.CompilerParams(vmem_limit_bytes=limit << 20),
        name=name,
    )


def per_device(record, shot_fire_samples):
    receivers, samples = record.shape
    shots = shot_fire_samples.shape[0]
    pairs, late = shots // 2, LATE // 2
    lanes = ROWS * shots
    late_rows = ROWS * LATE
    count = receivers // QUARTERS
    bf16, f32 = jnp.bfloat16, jnp.float32
    table = jnp.asarray(dft_master())
    smem, hbm = pl.BlockSpec(memory_space=pltpu.SMEM), pl.BlockSpec(memory_space=pltpu.HBM)

    message = local(
        tail_kernel,
        "tail_spectra",
        shape((late_rows + LATE, receivers), bf16),
        [hbm] * 3,
        [
            pltpu.SMEM((shots,), jnp.int32),
            pltpu.VMEM(table.shape, f32),
            pltpu.VMEM((late, 2 * ROWS, SPAN), bf16),
            pltpu.VMEM((receivers, WIN), bf16),
            pltpu.VMEM((late_rows + LATE, receivers), f32),
            pltpu.SemaphoreType.DMA((3,)),
        ],
    )(*(pltpu.with_memory_space_constraint(a, pltpu.HBM) for a in (shot_fire_samples, table, record)))

    def following(yh, u, k, xh, v):
        shot = ((yh << 4 | u << 2 | k) + 1) % SHOT_DEVICES
        return shot >> 4, (shot >> 2) & 3, shot & 3, xh, v

    received = send(message, following)
    total = local(
        own_kernel,
        "own_spectra",
        shape((lanes - late_rows, receivers), f32),
        [smem] + vmem(2),
        [pltpu.VMEM((pairs - late, 2 * ROWS, SPAN), bf16)],
    )(shot_fire_samples, table, record)
    y = pl.pallas_call(
        finish_kernel,
        grid=(1,),
        out_shape=shape((QUARTERS, count, lanes), bf16),
        in_specs=[
            pl.BlockSpec(total.shape, lambda i: (0, 0)),
            pl.BlockSpec((receivers, WIN), lambda i: (0, 0)),
            pl.BlockSpec(table.shape, lambda i: (0, 0)),
            pl.BlockSpec(received.shape, lambda i: (0, 0)),
        ],
        out_specs=pl.BlockSpec((QUARTERS, count, lanes), lambda i: (0, 0, 0)),
        scratch_shapes=[pltpu.VMEM((lanes, receivers), f32), pltpu.VMEM((late, 2 * ROWS, SPAN), bf16)],
        compiler_params=pltpu.CompilerParams(vmem_limit_bytes=4 << 20),
        name="finish_spectra",
    )(total, record, table, received)

    y3, y2, y1 = [send(y, lambda yh, u, k, xh, v, m=m: (yh ^ m >> 1, u, k ^ (m & 1) << 1, xh, v)) for m in (3, 2, 1)]
    slices = shape((2, 2, count, lanes), bf16)
    y, mine, theirs = local(join_kernel, "join", (shape((2, 2) + y.shape, bf16), slices, slices), vmem(4))(
        y3, y2, y1, y
    )

    def to_partner(yh, u, k, xh, v):
        return yh, u, k ^ 1, xh, v

    quarter = local(core_kernel, "join_core", shape((2,) + mine.shape, bf16), vmem(2))(mine, send(theirs, to_partner))
    cross = send(quarter, lambda yh, u, k, xh, v: (yh, u, k, 1 - xh, v))
    q = local(choose_kernel, "choose", shape(quarter.shape, bf16), vmem(2))(quarter, cross)
    qs = [q] + [send(q, lambda yh, u, k, xh, v, m=m: (yh, u, k, xh, v ^ m)) for m in (1, 2, 3)]
    right = local(right_kernel, "right_side", shape((2 * QUARTERS, 2 * receivers, lanes), bf16), vmem(2))(
        y, send(y, to_partner)
    )

    total_shots = shots * lax.axis_size("shot")
    rows = ROWS * count
    scale = 1.0 / total_shots
    share = shape((rows, receivers), f32)
    width = 128
    wire = shape((rows * receivers // width, width), bf16)
    early = []
    for m in range(QUARTERS - 1):
        early += local(
            lambda *refs: gram_kernel(scale, *refs),
            "gram",
            (share, wire),
            vmem(2) + [pl.BlockSpec(memory_space=pl.ANY)],
        )(right, qs[m], early[-2] if early else right)
    p0, p1, p2, p3 = local(
        lambda *refs: last_kernel(scale, *refs),
        "last_gram",
        (share, wire, wire, wire),
        vmem(2 + len(early)),
        [pltpu.VMEM((QUARTERS,) + share.shape, f32), pltpu.VMEM((QUARTERS,) + wire.shape, bf16)],
    )(right, qs[3], *early)
    r1, r2, r3 = [send(p, lambda yh, u, k, xh, v, n=n: (yh, u ^ n, k, xh, v)) for n, p in ((1, p1), (2, p2), (3, p3))]
    sums = local(sum_kernel, "sum", share, vmem(4))(r3, r2, r1, p0)
    return sums.reshape(2, NF, count, receivers).transpose(0, 1, 3, 2)


def solution(mesh):
    return jax.shard_map(
        per_device,
        mesh=mesh,
        in_specs=(P("rcv", "shot"), P("shot")),
        out_specs=P(None, None, "rcv", "shot"),
        check_vma=False,
    )
```
